32 devices in a mesh: shard: 2 (over y), ctx: 4 (over z), tp: 4 (over x, core).
Axes of the slice: x: 2, y: 2, z: 4, core: 2. Of those that a mesh axis runs over, the one named last changes fastest.
Arguments:
- inputs: bfloat16 [2, 4096, 768], P('shard', 'ctx'), may hold values from -6 to 6
- lengths: int32 [2], P('shard'), may hold values from 1024 to 4096, as said below
- global_blocks: int32 [2, 2], P('shard'), may hold values from 0 to 15, as said below
- random_blocks: int32 [2, 64, 3], P('shard', 'ctx'), may hold values from 0 to 63
- master_blocks: float32 [768, 96, 96], P(('shard', 'ctx', 'tp'))
- outer_vectors: float32 [6, 768], replicated
- inner_biases: float32 [4, 1152], P('tp'), may hold values from -4 to 4
- left_stats: float32 [768, 96, 96], P(('shard', 'ctx', 'tp')), as said below
- right_stats: float32 [768, 96, 96], P(('shard', 'ctx', 'tp')), as said below
- left_roots: float32 [768, 96, 96], P(('shard', 'ctx', 'tp')), as said below
- right_roots: float32 [768, 96, 96], P(('shard', 'ctx', 'tp')), as said below
- cotangent: bfloat16 [2, 4096, 768], P('shard', 'ctx'), may hold values from -6 to 6
Outputs:
- output: bfloat16 [2, 4096, 768], P('shard', 'ctx')
- input_grad: bfloat16 [2, 4096, 768], P('shard', 'ctx')
- block_grads: float32 [768, 96, 96], P(('shard', 'ctx', 'tp'))
- outer_grads: float32 [6, 768], P(None, ('shard', 'ctx'))
- inner_grads: float32 [4, 1152], P('tp', ('shard', 'ctx'))
- maxima: float32 [12], P('tp')
- left_new: float32 [768, 96, 96], P(('shard', 'ctx', 'tp'))
- right_new: float32 [768, 96, 96], P(('shard', 'ctx', 'tp'))
- new_blocks: float32 [768, 96, 96], P(('shard', 'ctx', 'tp'))
- new_outer: float32 [6, 768], P(None, ('shard', 'ctx'))
- new_inner: float32 [4, 1152], P('tp', ('shard', 'ctx'))
The draws below stay inside these ranges and needn't reach their ends.
Inputs may be any that keep to these rules, and one draw needn't show every extreme that they name: `lengths`: sequence 0 holds 4096 valid tokens. `global_blocks`: the two ids of a sequence differ. `left_stats`: each block is symmetric. `right_stats`: each block is symmetric. `left_roots`: each block is symmetric. `right_roots`: each block is symmetric.
All inputs are finite; a program needn't handle non-finite values.
Results may differ from the reference program's by a relative error of at most 0.018.
Values may be sent and summed in bfloat16 or wider, within the bound.
No kernel may reach another device: no remote copies, remote signals or barrier semaphores. Data moves between devices by JAX's collectives and lax.ppermute only.
A program may use at most 192 MiB of HBM per device.

```python
import math
import jax
import jax.numpy as jnp
from jax import lax

D = 768
HEADS = 12
HEAD = 64
FF = 3072
BLOCK = 64
SEQ = 4096
PB = 96
SLOTS = 2
NBQ = 64
HT = 192
FT = 768
OWNERS = 8
PBLK = 192
BPD = 24
NB_ALL = 768
INNER_W = 1152
N_TP = 4


def draw_lengths(key, part):
    drawn = jax.random.randint(key, (SLOTS,), SEQ // 4, SEQ + 1, dtype=jnp.int32)
    return drawn.at[0].set(SEQ)


def draw_global_blocks(key, part):
    slot_keys = jax.random.split(jax.random.fold_in(key, 3), SLOTS)

    def pick_pair(slot_key):
        return jax.random.permutation(slot_key, SEQ // (4 * BLOCK))[:2].astype(jnp.int32)
    return jax.vmap(pick_pair)(slot_keys)


def draw_master_blocks(key, part):
    tensor_count = NB_ALL // PBLK
    global_index = jnp.arange(NB_ALL, dtype=jnp.int32)
    tensor_index = global_index // BPD % tensor_count
    local_index = global_index // (BPD * tensor_count) * BPD + global_index % BPD
    head_cols = HEADS * HEAD // tensor_count
    unit_count = FF // tensor_count
    qkv_cols = 3 * head_cols // PB
    first_end = D // PB * qkv_cols
    second_end = first_end + head_cols // PB * (D // PB)
    third_end = second_end + D // PB * (unit_count // PB)
    base_scale = jnp.where(local_index < first_end, D ** (-0.5), jnp.where(local_index < second_end, 5.0 * (HEADS * HEAD) ** (-0.5), jnp.where(local_index < third_end, D ** (-0.5), FF ** (-0.5))))
    ranking = jax.random.permutation(jax.random.fold_in(key, 1), HEADS).astype(jnp.float32)
    head_scale = 3.0 ** ((ranking + 0.5) / HEADS)
    column = (local_index % qkv_cols)[:, None] * PB + jnp.arange(PB, dtype=jnp.int32)[None, :]
    head_of = jnp.clip(tensor_index[:, None] * (head_cols // HEAD) + column // HEAD, 0, HEADS - 1)
    query_col = (local_index[:, None] < first_end) & (column < head_cols)
    col_scale = jnp.where(query_col, head_scale[head_of], 1.0)
    noise_key = jax.random.fold_in(key, 2)
    noise = jax.random.normal(noise_key, (NB_ALL, PB, PB), jnp.float32)
    return noise * base_scale[:, None, None] * col_scale[:, None, :]


def draw_outer_vectors(key, part):
    noise_key = jax.random.fold_in(key, 4)
    noise = jax.random.normal(noise_key, (6, D), jnp.float32)
    row_ids = jnp.arange(6, dtype=jnp.int32)
    is_gain = (row_ids == 2) | (row_ids == 4)
    return jnp.where(is_gain[:, None], 1.0 + 0.15 * noise, 0.3 * noise)


def definite_blocks(key, scale):
    off_diag = jax.random.normal(key, (NB_ALL, PB, PB), jnp.float32)
    symmetric = (off_diag + jnp.swapaxes(off_diag, 1, 2)) * (0.03 / math.sqrt(2.0))
    diagonal_vals = jnp.exp(jax.random.uniform(jax.random.fold_in(key, 7), (NB_ALL, PB), jnp.float32, math.log(0.5), math.log(2.0)))
    identity = jnp.eye(PB, dtype=jnp.float32)
    return scale * (symmetric * (1.0 - identity) + identity * diagonal_vals[:, :, None])


def draw_left_stats(key, part):
    return definite_blocks(jax.random.fold_in(key, 11), PB * SLOTS * SEQ / 16.0)


def draw_right_stats(key, part):
    return definite_blocks(jax.random.fold_in(key, 12), PB * SLOTS * SEQ / 16.0)


def draw_left_roots(key, part):
    return definite_blocks(jax.random.fold_in(key, 13), (PB * SLOTS * SEQ / 16.0) ** (-0.25))


def draw_right_roots(key, part):
    return definite_blocks(jax.random.fold_in(key, 14), (PB * SLOTS * SEQ / 16.0) ** (-0.25))


def set_ends(array, own_key, low, top_value):
    extent = array.shape
    place = [jax.random.randint(jax.random.fold_in(own_key, axis), (), 0, extent[axis]) for axis in range(len(extent))]
    array = array.at[tuple(place)].set(low)
    longest = extent.index(max(extent))
    place[longest] = (place[longest] + 1) % extent[longest]
    return array.at[tuple(place)].set(top_value)


def shard_levels(stream_key, extent, cuts, least, largest):
    level, own = 1.0, jax.random.fold_in(stream_key, 6)
    for position, blocks in cuts:
        heights = jnp.exp(jax.random.uniform(jax.random.fold_in(own, position), (blocks,), jnp.float32, least / len(cuts), largest / len(cuts)))
        level = level * jnp.repeat(heights, extent[position] // blocks).reshape([-1 if axis == position else 1 for axis in range(len(extent))])
    return level


def scatter_about(stream_key, dims, spread, bound, shards=(), kind=jnp.bfloat16):
    values = spread * jax.random.normal(stream_key, dims, jnp.float32)
    if shards:
        values = values * shard_levels(stream_key, dims, shards, -0.22, 0.18)
    return jnp.clip(values, -bound, bound).astype(kind)


def setup_inputs(seed: int = 0) -> dict:
    key_list = jax.random.split(jax.random.key(seed), 13)
    return {
        "inputs": scatter_about(key_list[0], (SLOTS, SEQ, D), 1.0, 6.0, ((0, 2), (1, 4))),
        "lengths": draw_lengths(jax.random.fold_in(key_list[12], 71), 0),
        "global_blocks": draw_global_blocks(jax.random.fold_in(key_list[12], 71), 0),
        "random_blocks": set_ends(jax.random.randint(key_list[3], (SLOTS, NBQ, 3), 0, NBQ), jax.random.fold_in(key_list[3], 1), 0, NBQ - 1).astype(jnp.int32),
        "master_blocks": draw_master_blocks(jax.random.fold_in(key_list[12], 71), 0),
        "outer_vectors": draw_outer_vectors(jax.random.fold_in(key_list[12], 71), 0),
        "inner_biases": scatter_about(key_list[6], (N_TP, INNER_W), 0.3, 4.0, ((0, 4),), jnp.float32),
        "left_stats": draw_left_stats(jax.random.fold_in(key_list[12], 71), 0),
        "right_stats": draw_right_stats(jax.random.fold_in(key_list[12], 71), 0),
        "left_roots": draw_left_roots(jax.random.fold_in(key_list[12], 71), 0),
        "right_roots": draw_right_roots(jax.random.fold_in(key_list[12], 71), 0),
        "cotangent": scatter_about(key_list[11], (SLOTS, SEQ, D), 1.0, 6.0, ((0, 2), (1, 4))),
    }


eps_norm = 1e-06
tau_clip = 9.0
rate_matrix = 0.3
rate_vector = 0.001
neg_large = -1e+30
high = lax.Precision.HIGHEST

@jax.custom_vjp
def low(v):
    return lax.optimization_barrier(v.astype(jnp.bfloat16)).astype(jnp.float32)

@jax.custom_vjp
def low_back(v):
    return v

def low_keep(v):
    return (low(v), None)

def low_pass(kept, grad):
    return (grad,)

def back_keep(v):
    return (v, None)

def back_low(kept, grad):
    return (low(grad),)
low.defvjp(low_keep, low_pass)
low_back.defvjp(back_keep, back_low)

def matmul_high(left, right):
    return jnp.dot(left, right, precision=high, preferred_element_type=jnp.float32)

def layer_norm(values, gain, shift):
    mean_val = lax.optimization_barrier(jnp.mean(values, axis=-1, keepdims=True))
    centred = values - mean_val
    var_val = lax.optimization_barrier(jnp.mean(centred * centred, axis=-1, keepdims=True))
    return centred * lax.rsqrt(var_val + eps_norm) * gain + shift

def tensor_major(blocks):
    return blocks.reshape(OWNERS, N_TP, BPD, PB, PB).transpose(1, 0, 2, 3, 4).reshape(N_TP, PBLK, PB, PB)

def owner_major(blocks):
    trail = blocks.shape[2:]
    order = (1, 0, 2) + tuple(range(3, 3 + len(trail)))
    return blocks.reshape((N_TP, OWNERS, BPD) + trail).transpose(order).reshape((NB_ALL,) + trail)

def grid_many(blocks, row_count, col_count):
    lead = blocks.shape[0]
    shaped = blocks.reshape(lead, row_count // PB, col_count // PB, PB, PB)
    return shaped.transpose(0, 1, 3, 2, 4).reshape(lead, row_count, col_count)

def ungrid_many(matrix):
    lead, row_count, col_count = matrix.shape
    shaped = matrix.reshape(lead, row_count // PB, PB, col_count // PB, PB)
    return shaped.transpose(0, 1, 3, 2, 4).reshape(lead, -1, PB, PB)

def block_layout(slot_length, global_ids, random_ids, first_block, rows_blocks, block_count):
    rows = first_block + jnp.arange(rows_blocks, dtype=jnp.int32)
    window = jnp.stack([rows - 1, rows, rows + 1], axis=1)
    globals_row = jnp.broadcast_to(global_ids[None, :], (rows_blocks, 2))
    listed = jnp.concatenate([window, globals_row, random_ids], axis=1).astype(jnp.int32)
    inside = (listed >= 0) & (listed < block_count)
    clipped = jnp.clip(listed, 0, block_count - 1)
    key_pos = listed[:, :, None] * BLOCK + jnp.arange(BLOCK, dtype=jnp.int32)[None, None, :]
    key_mask = (inside[:, :, None] & (key_pos < slot_length)).reshape(rows_blocks, -1)
    query_pos = (first_block * BLOCK + jnp.arange(rows_blocks * BLOCK, dtype=jnp.int32)).reshape(rows_blocks, BLOCK)
    return (clipped, key_mask, query_pos < slot_length)

def pick_blocks(full_rows, clipped, head_count):
    block_count = full_rows.shape[0] // BLOCK
    picked = full_rows.reshape(block_count, BLOCK, -1)[clipped]
    return picked.reshape(clipped.shape[0], clipped.shape[1] * BLOCK, head_count, HEAD)

def slot_forward(params, inputs_f, slot_length, global_ids, random_ids):
    w_query, w_key, w_value, w_out, w_up, w_down, q_bias, v_bias, up_bias, outer = params
    block_count = SEQ // BLOCK
    queries = low_back(low(matmul_high(inputs_f, low(w_query)) + q_bias))
    key_rows = low_back(low(matmul_high(inputs_f, low(w_key))))
    value_rows = low_back(low(matmul_high(inputs_f, low(w_value)) + v_bias))
    clipped, key_mask, query_mask = block_layout(slot_length, global_ids, random_ids, 0, block_count, block_count)
    query_blocks = queries.reshape(block_count, BLOCK, HEADS, HEAD)
    key_blocks = pick_blocks(key_rows, clipped, HEADS)
    value_blocks = pick_blocks(value_rows, clipped, HEADS)
    raw_scores = jnp.einsum('lqhd,lkhd->lhqk', query_blocks, key_blocks, precision=high) * HEAD ** (-0.5)
    peak_logit = lax.optimization_barrier(jnp.max(jnp.where(key_mask[:, None, None, :] & query_mask[:, None, :, None], raw_scores, neg_large), axis=(0, 2, 3)))
    scores = low_back(raw_scores)
    masked = jnp.where(key_mask[:, None, None, :], scores, neg_large)
    row_top = lax.optimization_barrier(jnp.max(masked, axis=-1, keepdims=True))
    shifted = jnp.exp(masked - row_top)
    probs = shifted / lax.optimization_barrier(jnp.sum(shifted, axis=-1, keepdims=True))
    attended = jnp.einsum('lhqk,lkhd->lqhd', low(probs), value_blocks, precision=high).reshape(SEQ, HEADS * HEAD)
    attended = low_back(low(attended))
    branch = low_back(matmul_high(attended, low(w_out)) + outer[0])
    x_first = layer_norm(inputs_f + branch, outer[2], outer[3])
    gate_pre = low_back(matmul_high(low(x_first), low(w_up)) + up_bias)
    activated = jax.nn.gelu(gate_pre, approximate=True)
    ff_out = low_back(matmul_high(low(activated), low(w_down)) + outer[1])
    result = layer_norm(x_first + ff_out, outer[4], outer[5])
    return (result, peak_logit)

def forward(params, inputs_f, lengths, global_blocks, random_blocks):
    step_fn = jax.checkpoint(slot_forward)

    def scan_step(carry, item):
        slot_in, slot_length, global_ids, random_ids = item
        result, peak_logit = step_fn(params, slot_in, slot_length, global_ids, random_ids)
        return (carry, (result, peak_logit))
    _, (results, peaks) = lax.scan(scan_step, jnp.zeros((), jnp.float32), (inputs_f, lengths, global_blocks, random_blocks))
    return (results, lax.optimization_barrier(jnp.max(peaks, axis=0)))

def reference(inputs, lengths, global_blocks, random_blocks, master_blocks, outer_vectors, inner_biases, left_stats, right_stats, left_roots, right_roots, cotangent):
    first_end = D // PB * (3 * HT // PB)
    second_end = first_end + HT // PB * (D // PB)
    third_end = second_end + D // PB * (FT // PB)
    tensor_blocks = tensor_major(master_blocks)
    qkv_all = grid_many(tensor_blocks[:, :first_end], D, 3 * HT)
    out_all = grid_many(tensor_blocks[:, first_end:second_end], HT, D)
    up_all = grid_many(tensor_blocks[:, second_end:third_end], D, FT)
    down_all = grid_many(tensor_blocks[:, third_end:], FT, D)
    w_query = qkv_all[:, :, :HT].transpose(1, 0, 2).reshape(D, HEADS * HEAD)
    w_key = qkv_all[:, :, HT:2 * HT].transpose(1, 0, 2).reshape(D, HEADS * HEAD)
    w_value = qkv_all[:, :, 2 * HT:].transpose(1, 0, 2).reshape(D, HEADS * HEAD)
    w_out = out_all.reshape(HEADS * HEAD, D)
    w_up = up_all.transpose(1, 0, 2).reshape(D, FF)
    w_down = down_all.reshape(FF, D)
    q_bias = inner_biases[:, :HT].reshape(-1)
    v_bias = inner_biases[:, HT:2 * HT].reshape(-1)
    up_bias = inner_biases[:, 2 * HT:].reshape(-1)
    params = (w_query, w_key, w_value, w_out, w_up, w_down, q_bias, v_bias, up_bias, outer_vectors)
    inputs_f = inputs.astype(jnp.float32)

    def run_layer(param_set, layer_in):
        return forward(param_set, layer_in, lengths, global_blocks, random_blocks)
    results, back_fn, maxima = jax.vjp(run_layer, params, inputs_f, has_aux=True)
    row_valid = (jnp.arange(SEQ, dtype=jnp.int32)[None, :] < lengths[:, None]).astype(jnp.float32)
    cot_masked = cotangent.astype(jnp.float32) * row_valid[:, :, None]
    grad_params, grad_inputs = back_fn(cot_masked)
    g_query, g_key, g_value, g_out, g_up, g_down, g_qbias, g_vbias, g_upbias, g_outer = grad_params
    g_qkv_all = jnp.concatenate([gm.reshape(D, N_TP, HT).transpose(1, 0, 2) for gm in (g_query, g_key, g_value)], axis=2)
    tensor_grads = jnp.concatenate([ungrid_many(g_qkv_all), ungrid_many(g_out.reshape(N_TP, HT, D)), ungrid_many(g_up.reshape(D, N_TP, FT).transpose(1, 0, 2)), ungrid_many(g_down.reshape(N_TP, FT, D))], axis=1)
    block_grads = owner_major(tensor_grads)
    g_inner = jnp.concatenate([g_qbias.reshape(N_TP, HT), g_vbias.reshape(N_TP, HT), g_upbias.reshape(N_TP, FT)], axis=1)
    left_new = 0.5 * left_stats + 0.5 * jnp.einsum('bij,bkj->bik', block_grads, block_grads, precision=high)
    right_new = 0.5 * right_stats + 0.5 * jnp.einsum('bji,bjk->bik', block_grads, block_grads, precision=high)
    left_applied = jnp.einsum('bij,bjk->bik', left_roots, block_grads, precision=high)
    step_val = jnp.einsum('bij,bjk->bik', left_applied, right_roots, precision=high)
    clip_sqrt = jnp.sqrt(tau_clip / jnp.maximum(maxima, tau_clip))
    head_cols = jnp.repeat(clip_sqrt, HEAD).reshape(N_TP, HT)
    table = jnp.concatenate([head_cols, head_cols, jnp.ones((N_TP, HT), jnp.float32)], axis=1)
    qkv_factor = jnp.broadcast_to(table.reshape(N_TP, 1, 3 * HT // PB, PB), (N_TP, D // PB, 3 * HT // PB, PB)).reshape(N_TP, first_end, PB)
    factor = jnp.concatenate([qkv_factor, jnp.ones((N_TP, PBLK - first_end, PB), jnp.float32)], axis=1)
    factor = owner_major(factor)
    new_blocks = (master_blocks - rate_matrix * step_val) * factor[:, None, :]
    new_outer = outer_vectors - rate_vector * g_outer
    inner_factor = jnp.concatenate([head_cols, jnp.ones((N_TP, HT + FT), jnp.float32)], axis=1)
    new_inner = (inner_biases - rate_vector * g_inner) * inner_factor
    return (results.astype(jnp.bfloat16), grad_inputs.astype(jnp.bfloat16), block_grads, g_outer, g_inner, maxima, left_new, right_new, new_blocks, new_outer, new_inner)
```

```python
import functools

import jax
import jax.numpy as jnp
from jax import lax
from jax.experimental import pallas as pl
from jax.experimental.pallas import tpu as pltpu
from jax.sharding import PartitionSpec as P

D = 768
HEADS = 12
HEAD = 64
FF = 3072
BLOCK = 64
SEQ = 4096
PB = 96
LIST = 8
WIDE = 8

eps_norm = 1e-06
tau_clip = 9.0
rate_matrix = 0.3
rate_vector = 0.001
neg_large = -1e30
bf16 = jnp.bfloat16
f32 = jnp.float32
vmem_limit = 56 << 20
OWN = ("shard", "ctx")


def params_of(**more):
    return pltpu.CompilerParams(vmem_limit_bytes=vmem_limit, **more)


def dot32(left, right, dims=((1,), (0,))):
    return lax.dot_general(left, right, (dims, ((), ())), preferred_element_type=f32)


def layer_norm(values, gain, shift):
    mean_val = jnp.mean(values, axis=-1, keepdims=True)
    centred = values - mean_val
    var_val = jnp.mean(centred * centred, axis=-1, keepdims=True)
    return centred * lax.rsqrt(var_val + eps_norm) * gain + shift


def gelu_tanh(values):
    return jax.nn.gelu(values, approximate=True)


def swap(rows, mask):
    count = lax.axis_size("tp")
    return lax.ppermute(rows, "tp", [(i, i ^ mask) for i in range(count)])


def shift_ctx(rows, step):
    count = lax.axis_size("ctx")
    return lax.ppermute(rows, "ctx", [(i, (i + step) % count) for i in range(count)])


def gather_quarters(own):
    side = swap(own, 1)
    across = swap(own, 2)
    return own, side, across, swap(across, 1)


def scatter_sum(part):
    sent = swap(jnp.concatenate([part[1], part[3]], axis=0), 1)
    rows = part.shape[1]
    far = (part[2].astype(f32) + sent[rows:].astype(f32)).astype(bf16)
    got = swap(far, 2)
    return part[0].astype(f32) + sent[:rows].astype(f32) + got.astype(f32)


def pack_kernel(blocks_ref, out_ref):
    for j in range(WIDE):
        out_ref[:, PB * j : PB * (j + 1)] = blocks_ref[j].astype(bf16)


def pack_rows(blocks):
    rows = blocks.shape[0] // WIDE
    return pl.pallas_call(
        pack_kernel,
        grid=(rows,),
        in_specs=[pl.BlockSpec((WIDE, PB, PB), lambda i: (i, 0, 0))],
        out_specs=pl.BlockSpec((PB, PB * WIDE), lambda i: (i, 0)),
        out_shape=jax.ShapeDtypeStruct((rows * PB, PB * WIDE), bf16),
        compiler_params=params_of(),
        name="pack_rows",
    )(blocks)


def qkv_unpack_kernel(src_ref, q_ref, kv_ref, *, cols):
    rows = D // PB
    q_ref[...] = jnp.zeros(q_ref.shape, bf16)
    for i in range(rows):
        for c in range(3):
            unit = 3 * i + c
            piece = src_ref[
                PB * (unit // 4) : PB * (unit // 4 + 1), cols * (unit % 4) : cols * (unit % 4 + 1)
            ]
            if c == 0:
                q_ref[PB * i : PB * (i + 1), :cols] = piece
            else:
                kv_ref[PB * i : PB * (i + 1), cols * (c - 1) : cols * c] = piece


def qkv_unpack(packed, cols, wide):
    return pl.pallas_call(
        functools.partial(qkv_unpack_kernel, cols=cols),
        out_shape=(
            jax.ShapeDtypeStruct((D, wide), bf16),
            jax.ShapeDtypeStruct((D, 2 * cols), bf16),
        ),
        compiler_params=params_of(),
        name="qkv_unpack",
    )(packed)


def qkv_pack_kernel(q_ref, kv_ref, out_ref, *, cols):
    for i in range(D // PB):
        for c in range(3):
            unit = 3 * i + c
            rows = slice(PB * i, PB * (i + 1))
            piece = q_ref[rows, :cols] if c == 0 else kv_ref[rows, cols * (c - 1) : cols * c]
            out_ref[
                PB * (unit // 4) : PB * (unit // 4 + 1), cols * (unit % 4) : cols * (unit % 4 + 1)
            ] = piece.astype(bf16)


def qkv_pack(grad_q, grad_kv, cols):
    return pl.pallas_call(
        functools.partial(qkv_pack_kernel, cols=cols),
        out_shape=jax.ShapeDtypeStruct((3 * cols, D), bf16),
        compiler_params=params_of(),
        name="qkv_pack",
    )(grad_q, grad_kv)


def head_masks(wide, heads, first):
    lane = lax.broadcasted_iota(jnp.int32, (BLOCK, wide), 1) // HEAD
    return [lane == h + first for h in range(heads)]


def spread(block, masks):
    zero = jnp.zeros_like(block)
    return jnp.concatenate([jnp.where(mask, block, zero) for mask in masks], axis=0)


def fold(stacked, masks):
    total = None
    for h, mask in enumerate(masks):
        part = jnp.where(mask, stacked[BLOCK * h : BLOCK * (h + 1)], 0.0)
        total = part if total is None else total + part
    return total


def listed_rows(addr_ref, kv_ref, i):
    return jnp.concatenate(
        [
            kv_ref[pl.ds(pl.multiple_of(addr_ref[i * LIST + e] * BLOCK, BLOCK), BLOCK), :]
            for e in range(LIST)
        ],
        axis=0,
    )


def fwd_kernel(addr_ref, valid_ref, query_ref, q_ref, kv_ref, att_ref, p_ref, top_ref, *, heads):
    i = pl.program_id(0)
    wide = q_ref.shape[1]
    start = kv_ref.shape[1] - wide

    @pl.when(i == 0)
    def _():
        top_ref[...] = jnp.full(top_ref.shape, neg_large, f32)

    scale = jnp.asarray(HEAD ** (-0.5), bf16)
    q_all = spread(q_ref[...] * scale, head_masks(wide, heads, 0))
    listed = listed_rows(addr_ref, kv_ref, i)
    scores = dot32(q_all, listed[:, :wide], ((1,), (1,)))
    lane = lax.broadcasted_iota(jnp.int32, (1, LIST * BLOCK), 1)
    limit = jnp.zeros((1, LIST * BLOCK), jnp.int32)
    for e in range(LIST):
        limit = jnp.where(lane // BLOCK == e, valid_ref[i * LIST + e], limit)
    scores = jnp.where(lane % BLOCK < limit, scores, neg_large)
    row_top = jnp.max(scores, axis=1, keepdims=True)
    shifted = jnp.exp(scores - row_top)
    probs = shifted * (1.0 / jnp.sum(shifted, axis=1, keepdims=True))
    probs_low = probs.astype(bf16)
    p_ref[0] = probs_low
    out = dot32(probs_low, listed[:, start:])
    att_ref[...] = fold(out, head_masks(wide, heads, (heads * HEAD - start) // HEAD)).astype(bf16)
    row = lax.broadcasted_iota(jnp.int32, row_top.shape, 0) % BLOCK
    seen = jnp.where(row < query_ref[i], row_top, neg_large)
    for h in range(heads):
        best = jnp.max(seen[BLOCK * h : BLOCK * (h + 1)], axis=0, keepdims=True)
        top_ref[h : h + 1, :] = jnp.maximum(top_ref[h : h + 1, :], best)


def attention_forward(queries, kv_all, addr, valid, query_valid, heads):
    tokens, wide = queries.shape
    blocks = tokens // BLOCK
    rows = heads * BLOCK
    cols = LIST * BLOCK
    return pl.pallas_call(
        functools.partial(fwd_kernel, heads=heads),
        grid_spec=pltpu.PrefetchScalarGridSpec(
            num_scalar_prefetch=3,
            grid=(blocks,),
            in_specs=[
                pl.BlockSpec((BLOCK, wide), lambda i, *_: (i, 0)),
                pl.BlockSpec(kv_all.shape, lambda i, *_: (0, 0), pipeline_mode=pl.Buffered(1)),
            ],
            out_specs=[
                pl.BlockSpec((BLOCK, wide), lambda i, *_: (i, 0)),
                pl.BlockSpec((1, rows, cols), lambda i, *_: (i, 0, 0)),
                pl.BlockSpec((8, 128), lambda i, *_: (0, 0)),
            ],
        ),
        out_shape=(
            jax.ShapeDtypeStruct((tokens, wide), bf16),
            jax.ShapeDtypeStruct((blocks, rows, cols), bf16),
            jax.ShapeDtypeStruct((8, 128), f32),
        ),
        compiler_params=params_of(dimension_semantics=("arbitrary",)),
        cost_estimate=pl.CostEstimate(
            flops=4 * blocks * rows * cols * wide,
            bytes_accessed=2 * (kv_all.size + 2 * queries.size + blocks * rows * cols),
            transcendentals=blocks * rows * cols,
        ),
        name="attention_forward",
    )(addr, valid, query_valid, queries, kv_all)


def bwd_kernel(addr_ref, q_ref, do_ref, p_ref, kv_ref, dq_ref, dkv_ref, sums_ref, acc_ref, *, heads):
    i = pl.program_id(0)
    wide = q_ref.shape[1]
    start = kv_ref.shape[1] - wide
    first = (heads * HEAD - start) // HEAD

    @pl.when(i == 0)
    def _():
        acc_ref[...] = jnp.zeros(acc_ref.shape, f32)
        sums_ref[...] = jnp.zeros(sums_ref.shape, f32)

    scale = jnp.asarray(HEAD ** (-0.5), bf16)
    q_masks = head_masks(wide, heads, 0)
    q_all = spread(q_ref[...] * scale, q_masks)
    do_all = spread(do_ref[...], head_masks(wide, heads, first))
    listed = listed_rows(addr_ref, kv_ref, i)
    probs_low = p_ref[0]
    probs = probs_low.astype(f32)
    d_probs = dot32(do_all, listed[:, start:], ((1,), (1,)))
    delta = jnp.sum(probs * d_probs, axis=1, keepdims=True)
    d_scores = (probs * (d_probs - delta)).astype(bf16)
    d_query = (fold(dot32(d_scores, listed[:, :wide]), q_masks) * HEAD ** (-0.5)).astype(bf16)
    dq_ref[...] = d_query
    sums_ref[0:1, :wide] += jnp.sum(d_query.astype(f32), axis=0, keepdims=True)
    d_key = dot32(d_scores, q_all, ((0,), (0,)))
    d_value = dot32(probs_low, do_all, ((0,), (0,)))
    sums_ref[1:2, :wide] += jnp.sum(d_value, axis=0, keepdims=True)
    for e in range(LIST):
        rows = pl.ds(pl.multiple_of(addr_ref[i * LIST + e] * BLOCK, BLOCK), BLOCK)
        part = slice(BLOCK * e, BLOCK * (e + 1))
        acc_ref[rows, :start] += d_key[part, :start]
        acc_ref[rows, start:wide] += d_key[part, start:] + d_value[part, : wide - start]
        acc_ref[rows, wide:] += d_value[part, wide - start :]

    @pl.when(i == pl.num_programs(0) - 1)
    def _():
        dkv_ref[...] = acc_ref[...].astype(bf16)


def attention_backward(queries, d_out, probs, kv_all, addr, heads):
    tokens, wide = queries.shape
    blocks = tokens // BLOCK
    rows = heads * BLOCK
    cols = LIST * BLOCK
    return pl.pallas_call(
        functools.partial(bwd_kernel, heads=heads),
        grid_spec=pltpu.PrefetchScalarGridSpec(
            num_scalar_prefetch=1,
            grid=(blocks,),
            in_specs=[
                pl.BlockSpec((BLOCK, wide), lambda i, *_: (i, 0)),
                pl.BlockSpec((BLOCK, wide), lambda i, *_: (i, 0)),
                pl.BlockSpec((1, rows, cols), lambda i, *_: (i, 0, 0)),
                pl.BlockSpec(kv_all.shape, lambda i, *_: (0, 0), pipeline_mode=pl.Buffered(1)),
            ],
            out_specs=[
                pl.BlockSpec((BLOCK, wide), lambda i, *_: (i, 0)),
                pl.BlockSpec(kv_all.shape, lambda i, *_: (0, 0), pipeline_mode=pl.Buffered(1)),
                pl.BlockSpec((8, wide), lambda i, *_: (0, 0)),
            ],
            scratch_shapes=[pltpu.VMEM(kv_all.shape, f32)],
        ),
        out_shape=(
            jax.ShapeDtypeStruct((tokens, wide), bf16),
            jax.ShapeDtypeStruct(kv_all.shape, bf16),
            jax.ShapeDtypeStruct((8, wide), f32),
        ),
        compiler_params=params_of(dimension_semantics=("arbitrary",)),
        cost_estimate=pl.CostEstimate(
            flops=8 * blocks * rows * cols * wide,
            bytes_accessed=2 * (2 * kv_all.size + 3 * queries.size + blocks * rows * cols),
            transcendentals=0,
        ),
        name="attention_backward",
    )(addr, queries, d_out, probs, kv_all)


def two_parts(values):
    high = values.astype(bf16)
    return high, (values - high.astype(f32)).astype(bf16)


def shampoo_kernel(
    g_ref, mb_ref, ls_ref, rs_ref, lr_ref, rr_ref, fac_ref, bg_ref, ln_ref, rn_ref, nb_ref, *, width
):
    for j in range(width):
        grad = g_ref[:, PB * j : PB * (j + 1)]
        bg_ref[j] = grad.astype(f32)
        ln_ref[j] = 0.5 * ls_ref[j] + 0.5 * dot32(grad, grad, ((1,), (1,)))
        rn_ref[j] = 0.5 * rs_ref[j] + 0.5 * dot32(grad, grad, ((0,), (0,)))
        left_hi, left_lo = two_parts(lr_ref[j])
        applied_hi, applied_lo = two_parts(dot32(left_hi, grad) + dot32(left_lo, grad))
        right_hi, right_lo = two_parts(rr_ref[j])
        step_val = (
            dot32(applied_hi, right_hi) + dot32(applied_hi, right_lo) + dot32(applied_lo, right_hi)
        )
        nb_ref[j] = (mb_ref[j] - rate_matrix * step_val) * fac_ref[j]


def shampoo(grads, width, master, left_s, right_s, left_r, right_r, factor):
    count = master.shape[0]
    block = pl.BlockSpec((width, PB, PB), lambda i: (i, 0, 0))
    shape = jax.ShapeDtypeStruct((count, PB, PB), f32)
    return pl.pallas_call(
        functools.partial(shampoo_kernel, width=width),
        grid=(count // width,),
        in_specs=[pl.BlockSpec((PB, PB * width), lambda i: (i, 0))]
        + [block] * 5
        + [pl.BlockSpec((width, 1, PB), lambda i: (i, 0, 0))],
        out_specs=[block] * 4,
        out_shape=[shape] * 4,
        compiler_params=params_of(),
        name="shampoo",
    )(grads, master, left_s, right_s, left_r, right_r, factor)


def per_device(
    inputs,
    lengths,
    global_blocks,
    random_blocks,
    master_blocks,
    outer_vectors,
    inner_biases,
    left_stats,
    right_stats,
    left_roots,
    right_roots,
    cotangent,
):
    tensor_count = lax.axis_size("tp")
    owner_count = lax.axis_size(OWN)
    ctx_count = lax.axis_size("ctx")
    heads_here = HEADS // tensor_count
    cols = heads_here * HEAD
    units = FF // tensor_count
    wide = 256
    pad = wide - cols
    tokens = inputs.shape[1]
    quarter = tokens // 4
    rows_blocks = tokens // BLOCK
    quarter_blocks = rows_blocks // 4
    block_count = SEQ // BLOCK
    blocks_here = master_blocks.shape[0]
    packed = blocks_here % WIDE == 0
    me = lax.axis_index("tp")
    z = lax.axis_index("ctx")
    owner = lax.axis_index(OWN)
    bo, b2, g1, beta1, g2, beta2 = [outer_vectors[i] for i in range(6)]

    if packed:
        weights = lax.all_gather(pack_rows(master_blocks), OWN, axis=0, tiled=True)
    else:
        weights = pack_rows(lax.all_gather(master_blocks.astype(bf16), OWN, axis=0, tiled=True))
    edge1, edge2, edge3 = 3 * cols, 4 * cols, 4 * cols + D
    w_q, w_kv = qkv_unpack(weights[:edge1], cols, wide)
    w_out = jnp.concatenate([jnp.zeros((pad, D), bf16), weights[edge1:edge2]], axis=0)
    w_up = weights[edge2:edge3]
    w_down = weights[edge3:]

    flat_in = inputs.reshape(tokens, D)
    own_in = lax.dynamic_slice_in_dim(flat_in, me * quarter, quarter, 0)
    chunks = [
        jnp.concatenate(
            [
                lax.dynamic_slice_in_dim(flat_in, (me ^ r) * quarter, quarter, 0)
                for r in range(4)
            ],
            axis=0,
        )
    ]
    for step in range(1, ctx_count):
        chunks.append(jnp.concatenate(gather_quarters(shift_ctx(own_in, step)), axis=0))

    rel = jnp.arange(rows_blocks, dtype=jnp.int32)
    place = ((rel // quarter_blocks) ^ me) * quarter_blocks + rel % quarter_blocks
    rows = z * rows_blocks + place
    length = lengths[0]
    listed = jnp.concatenate(
        [
            jnp.stack([rows - 1, rows, rows + 1], axis=1),
            jnp.broadcast_to(global_blocks[0][None, :], (rows_blocks, 2)),
            random_blocks[0][place],
        ],
        axis=1,
    ).astype(jnp.int32)
    inside = (listed >= 0) & (listed < block_count)
    held = jnp.clip(listed, 0, block_count - 1)
    valid = jnp.where(inside, jnp.clip(length - listed * BLOCK, 0, BLOCK), 0).reshape(-1)
    local = held % rows_blocks
    addr = (
        ((z - held // rows_blocks) % ctx_count) * rows_blocks
        + ((local // quarter_blocks) ^ me) * quarter_blocks
        + local % quarter_blocks
    ).reshape(-1)
    query_valid = jnp.clip(length - rows * BLOCK, 0, BLOCK)

    inner_row = inner_biases[0]
    q_bias = jnp.concatenate([inner_row[:cols], jnp.zeros((pad,), f32)])
    kv_bias = jnp.concatenate([jnp.zeros((cols,), f32), inner_row[cols : 2 * cols]])
    up_bias = inner_row[2 * cols :]
    queries = (dot32(chunks[0], w_q) + q_bias).astype(bf16)
    kv_all = jnp.concatenate([(dot32(c, w_kv) + kv_bias).astype(bf16) for c in chunks], axis=0)
    in_all = jnp.concatenate(chunks, axis=0)
    att, probs, tops = attention_forward(queries, kv_all, addr, valid, query_valid, heads_here)
    tops_all = lax.all_gather(tops, OWN, axis=0, tiled=False)

    own_f32 = own_in.astype(f32)
    branch = scatter_sum(dot32(att, w_out).astype(bf16).reshape(4, quarter, D)) + bo
    hidden = own_f32 + branch
    x_first, back_first = jax.vjp(layer_norm, hidden, g1, beta1)
    x_low = jnp.concatenate(gather_quarters(x_first.astype(bf16)), axis=0)
    gate = dot32(x_low, w_up) + up_bias
    act_low = gelu_tanh(gate).astype(bf16)
    ff = scatter_sum(dot32(act_low, w_down).astype(bf16).reshape(4, quarter, D)) + b2
    result, back_second = jax.vjp(layer_norm, x_first + ff, g2, beta2)
    out_quarters = gather_quarters(result.astype(bf16))

    own_cot = lax.dynamic_slice_in_dim(cotangent.reshape(tokens, D), me * quarter, quarter, 0)
    positions = z * tokens + me * quarter + jnp.arange(quarter, dtype=jnp.int32)
    d_result = own_cot.astype(f32) * (positions < length).astype(f32)[:, None]
    d_mixed, d_gain2, d_shift2 = back_second(d_result)
    d_ff_own = d_mixed.astype(bf16)
    d_bias2 = jnp.sum(d_ff_own.astype(f32), axis=0)
    d_ff = jnp.concatenate(gather_quarters(d_ff_own), axis=0)
    d_act = dot32(d_ff, w_down, ((1,), (1,)))
    _, back_gelu = jax.vjp(gelu_tanh, gate)
    d_gate = back_gelu(d_act)[0].astype(bf16)
    d_upbias = jnp.sum(d_gate.astype(f32), axis=0)
    d_first = d_mixed + scatter_sum(
        dot32(d_gate, w_up, ((1,), (1,))).astype(bf16).reshape(4, quarter, D)
    )
    d_hidden, d_gain1, d_shift1 = back_first(d_first)
    d_branch_own = d_hidden.astype(bf16)
    d_bias_out = jnp.sum(d_branch_own.astype(f32), axis=0)
    d_branch = jnp.concatenate(gather_quarters(d_branch_own), axis=0)
    d_att = dot32(d_branch, w_out, ((1,), (1,))).astype(bf16)
    d_query, d_kv, sums = attention_backward(queries, d_att, probs, kv_all, addr, heads_here)

    total = d_hidden
    for step in list(range(1, ctx_count)) + [0]:
        part = dot32(d_kv[step * tokens : (step + 1) * tokens], w_kv, ((1,), (1,)))
        if step == 0:
            part = part + dot32(d_query, w_q, ((1,), (1,)))
        mine = scatter_sum(part.astype(bf16).reshape(4, quarter, D))
        if step:
            mine = shift_ctx(mine.astype(bf16), ctx_count - step).astype(f32)
        total = total + mine
    grad_quarters = gather_quarters(total.astype(bf16))

    g_down = dot32(act_low, d_ff, ((0,), (0,))).astype(bf16)
    g_up = dot32(x_low, d_gate, ((0,), (0,))).astype(bf16)
    g_out = dot32(att, d_branch, ((0,), (0,)))[pad:].astype(bf16)
    g_q = dot32(chunks[0], d_query, ((0,), (0,)))
    g_kv = dot32(in_all, d_kv, ((0,), (0,)))
    g_qkv = qkv_pack(g_q, g_kv, cols)
    grads = jnp.concatenate([g_qkv, g_out, g_up, g_down], axis=0)
    outer_part = jnp.stack([d_bias_out, d_bias2, d_gain1, d_shift1, d_gain2, d_shift2], axis=0)
    inner_part = jnp.concatenate([sums[0, :cols], sums[1, pad:], d_upbias])
    outer_cols = D // owner_count
    inner_cols = inner_part.shape[0] // owner_count
    if packed:
        extra = 16
        vector = jnp.concatenate(
            [
                outer_part.reshape(6, owner_count, outer_cols)
                .transpose(1, 0, 2)
                .reshape(owner_count, -1),
                inner_part.reshape(owner_count, inner_cols),
            ],
            axis=1,
        )
        vector = jnp.pad(
            vector.astype(bf16)[:, None, :],
            ((0, 0), (0, extra - 1), (0, D - vector.shape[1])),
        )
        own_rows = grads.shape[0] // owner_count
        joined = jnp.concatenate([grads.reshape(owner_count, own_rows, D), vector], axis=1)
        summed = lax.psum_scatter(joined, OWN, scatter_dimension=0, tiled=True)[0]
        own_grads = summed[:own_rows]
        row = summed[own_rows].astype(f32)
        outer_own = row[: 6 * outer_cols].reshape(6, outer_cols)
        inner_own = row[6 * outer_cols : 6 * outer_cols + inner_cols][None, :]
        width = WIDE
    else:
        blocks = (
            grads.reshape(-1, PB, WIDE, PB).transpose(0, 2, 1, 3).reshape(-1, PB, PB)
        )
        own_grads = lax.psum_scatter(blocks, OWN, scatter_dimension=0, tiled=True)
        own_grads = own_grads.reshape(blocks_here * PB, PB)
        outer_own = lax.psum_scatter(outer_part, OWN, scatter_dimension=1, tiled=True)
        inner_own = lax.psum_scatter(inner_part[None, :], OWN, scatter_dimension=1, tiled=True)
        width = 1
    outer_own = outer_own + swap(outer_own, 1)
    outer_own = outer_own + swap(outer_own, 2)

    maxima = jnp.max(tops_all, axis=0)[:heads_here, 0]
    clip_sqrt = jnp.sqrt(tau_clip / jnp.maximum(maxima, tau_clip))
    head_factor = jnp.repeat(clip_sqrt, HEAD)
    table = jnp.concatenate([head_factor, head_factor, jnp.ones((cols,), f32)]).reshape(-1, PB)
    own_index = owner * blocks_here + jnp.arange(blocks_here, dtype=jnp.int32)
    per_row = 3 * cols // PB
    own_factor = jnp.where(
        (own_index < D // PB * per_row)[:, None], table[own_index % per_row], 1.0
    )
    block_sum, left_new, right_new, new_blocks = shampoo(
        own_grads,
        width,
        master_blocks,
        left_stats,
        right_stats,
        left_roots,
        right_roots,
        own_factor[:, None, :],
    )
    own_outer = lax.dynamic_slice_in_dim(outer_vectors, owner * outer_cols, outer_cols, 1)
    new_outer = own_outer - rate_vector * outer_own
    inner_factor = jnp.concatenate([head_factor, jnp.ones((cols + units,), f32)])
    own_inner_factor = lax.dynamic_slice_in_dim(inner_factor, owner * inner_cols, inner_cols, 0)
    own_inner = lax.dynamic_slice_in_dim(inner_biases, owner * inner_cols, inner_cols, 1)
    new_inner = (own_inner - rate_vector * inner_own) * own_inner_factor[None, :]

    def placed(quarters):
        whole = jnp.zeros((tokens, D), bf16)
        for r, piece in enumerate(quarters):
            whole = lax.dynamic_update_slice_in_dim(whole, piece, (me ^ r) * quarter, 0)
        return whole.reshape(inputs.shape)

    return (
        placed(out_quarters),
        placed(grad_quarters),
        block_sum,
        outer_own,
        inner_own,
        maxima,
        left_new,
        right_new,
        new_blocks,
        new_outer,
        new_inner,
    )


def solution(mesh):
    return jax.shard_map(
        per_device,
        mesh=mesh,
        in_specs=(
            P("shard", "ctx", None),
            P("shard"),
            P("shard", None),
            P("shard", "ctx", None),
            P(("shard", "ctx", "tp"), None, None),
            P(),
            P("tp", None),
            P(("shard", "ctx", "tp"), None, None),
            P(("shard", "ctx", "tp"), None, None),
            P(("shard", "ctx", "tp"), None, None),
            P(("shard", "ctx", "tp"), None, None),
            P("shard", "ctx", None),
        ),
        out_specs=(
            P("shard", "ctx", None),
            P("shard", "ctx", None),
            P(("shard", "ctx", "tp"), None, None),
            P(None, ("shard", "ctx")),
            P("tp", ("shard", "ctx")),
            P("tp"),
            P(("shard", "ctx", "tp"), None, None),
            P(("shard", "ctx", "tp"), None, None),
            P(("shard", "ctx", "tp"), None, None),
            P(None, ("shard", "ctx")),
            P("tp", ("shard", "ctx")),
        ),
        check_vma=False,
    )
```

```python
import functools

import jax
import jax.numpy as jnp
from jax import lax
from jax.experimental import pallas as pl
from jax.experimental.pallas import tpu as pltpu
from jax.sharding import PartitionSpec as P

D = 768
HEADS = 12
HEAD = 64
FF = 3072
BLOCK = 64
SEQ = 4096
PB = 96
LIST = 8
WIDE = 8

eps_norm = 1e-06
tau_clip = 9.0
rate_matrix = 0.3
rate_vector = 0.001
neg_large = -1e30
bf16 = jnp.bfloat16
f32 = jnp.float32
vmem_limit = 56 << 20
OWN = ("shard", "ctx")


def params_of(**more):
    return pltpu.CompilerParams(vmem_limit_bytes=vmem_limit, **more)


def small_params(**more):
    return pltpu.CompilerParams(vmem_limit_bytes=32 << 20, **more)


def dot32(left, right, dims=((1,), (0,))):
    return lax.dot_general(left, right, (dims, ((), ())), preferred_element_type=f32)


def layer_norm(values, gain, shift):
    mean_val = jnp.mean(values, axis=-1, keepdims=True)
    centred = values - mean_val
    var_val = jnp.mean(centred * centred, axis=-1, keepdims=True)
    return centred * lax.rsqrt(var_val + eps_norm) * gain + shift


def gelu_tanh(values):
    return jax.nn.gelu(values, approximate=True)


def swap(rows, mask):
    count = lax.axis_size("tp")
    return lax.ppermute(rows, "tp", [(i, i ^ mask) for i in range(count)])


def shift_ctx(rows, step):
    count = lax.axis_size("ctx")
    return lax.ppermute(rows, "ctx", [(i, (i + step) % count) for i in range(count)])


def shift_shard(rows, step):
    count = lax.axis_size("shard")
    return lax.ppermute(rows, "shard", [(i, (i + step) % count) for i in range(count)])


def owner_move(rows, pairs):
    return lax.ppermute(rows, OWN, pairs)


def after(value, *others):
    return lax.optimization_barrier((value,) + others)[0]


def near_first(count):
    return sorted(range(1, count), key=lambda step: min(step, count - step))


def gather_quarters(own):
    side = swap(own, 1)
    across = swap(own, 2)
    return own, side, across, swap(across, 1)


def scatter_sum(part):
    sent = swap(jnp.concatenate([part[1], part[3]], axis=0), 1)
    rows = part.shape[1]
    far = (part[2].astype(f32) + sent[rows:].astype(f32)).astype(bf16)
    got = swap(far, 2)
    return part[0].astype(f32) + sent[:rows].astype(f32) + got.astype(f32)


def pack_kernel(blocks_ref, out_ref):
    for j in range(WIDE):
        out_ref[:, PB * j : PB * (j + 1)] = blocks_ref[j].astype(bf16)


def pack_rows(blocks):
    rows = blocks.shape[0] // WIDE
    return pl.pallas_call(
        pack_kernel,
        grid=(rows,),
        in_specs=[pl.BlockSpec((WIDE, PB, PB), lambda i: (i, 0, 0))],
        out_specs=pl.BlockSpec((PB, PB * WIDE), lambda i: (i, 0)),
        out_shape=jax.ShapeDtypeStruct((rows * PB, PB * WIDE), bf16),
        compiler_params=params_of(),
        name="pack_rows",
    )(blocks)


def unpack_kernel(place_ref, near_ref, far_ref, q_ref, kv_ref, out_ref, all_ref, *, cols):
    half = near_ref.shape[0]
    all_ref[:half] = near_ref[...]
    all_ref[half:] = far_ref[...]
    q_ref[...] = jnp.zeros(q_ref.shape, bf16)
    for i in range(D // PB):
        for c in range(3):
            unit = 3 * i + c
            piece = all_ref[place_ref[unit // 4], :, cols * (unit % 4) : cols * (unit % 4 + 1)]
            if c == 0:
                q_ref[PB * i : PB * (i + 1), :cols] = piece
            else:
                kv_ref[PB * i : PB * (i + 1), cols * (c - 1) : cols * c] = piece
    pad = out_ref.shape[0] - cols
    out_ref[:pad, :] = jnp.zeros((pad, D), bf16)
    for i in range(cols // PB):
        out_ref[pad + PB * i : pad + PB * (i + 1), :] = all_ref[place_ref[3 * cols // PB + i]]


def unpack_first(place, near, far, cols, wide):
    full = pl.BlockSpec(memory_space=pltpu.VMEM)
    return pl.pallas_call(
        functools.partial(unpack_kernel, cols=cols),
        in_specs=[pl.BlockSpec(memory_space=pltpu.SMEM), full, full],
        out_specs=[full, full, full],
        out_shape=(
            jax.ShapeDtypeStruct((D, wide), bf16),
            jax.ShapeDtypeStruct((D, 2 * cols), bf16),
            jax.ShapeDtypeStruct((wide, D), bf16),
        ),
        scratch_shapes=[pltpu.VMEM((near.shape[0] + far.shape[0], PB, D), bf16)],
        compiler_params=params_of(),
        name="unpack_first",
    )(place, near, far)


def qkv_pack_kernel(q_ref, kv_ref, out_ref, *, cols):
    for i in range(D // PB):
        for c in range(3):
            unit = 3 * i + c
            rows = slice(PB * i, PB * (i + 1))
            piece = q_ref[rows, :cols] if c == 0 else kv_ref[rows, cols * (c - 1) : cols * c]
            out_ref[
                PB * (unit // 4) : PB * (unit // 4 + 1), cols * (unit % 4) : cols * (unit % 4 + 1)
            ] = piece.astype(bf16)


def qkv_pack(grad_q, grad_kv, cols):
    return pl.pallas_call(
        functools.partial(qkv_pack_kernel, cols=cols),
        out_shape=jax.ShapeDtypeStruct((3 * cols, D), bf16),
        compiler_params=params_of(),
        name="qkv_pack",
    )(grad_q, grad_kv)


def head_masks(wide, heads, first):
    lane = lax.broadcasted_iota(jnp.int32, (BLOCK, wide), 1) // HEAD
    return [lane == h + first for h in range(heads)]


def spread(block, masks):
    zero = jnp.zeros_like(block)
    return jnp.concatenate([jnp.where(mask, block, zero) for mask in masks], axis=0)


def fold(stacked, masks):
    total = None
    for h, mask in enumerate(masks):
        part = jnp.where(mask, stacked[BLOCK * h : BLOCK * (h + 1)], 0.0)
        total = part if total is None else total + part
    return total


def listed_rows(addr_ref, kv_ref, i):
    return jnp.concatenate(
        [
            kv_ref[pl.ds(pl.multiple_of(addr_ref[i * LIST + e] * BLOCK, BLOCK), BLOCK), :]
            for e in range(LIST)
        ],
        axis=0,
    )


def load_chunks(chunk_refs, all_ref, sem):
    rows = chunk_refs[0].shape[0]
    copies = [
        pltpu.make_async_copy(ref, all_ref.at[pl.ds(c * rows, rows)], sem.at[c])
        for c, ref in enumerate(chunk_refs)
    ]
    for copy in copies:
        copy.start()
    for copy in copies:
        copy.wait()


def fwd_kernel(addr_ref, valid_ref, query_ref, q_ref, *refs, heads, group, chunks):
    chunk_refs = refs[:chunks]
    att_ref, p_ref, top_ref, kv_ref, sem = refs[chunks:]
    i = pl.program_id(0)
    wide = q_ref.shape[1]
    start = kv_ref.shape[1] - wide

    @pl.when(i == 0)
    def _():
        top_ref[...] = jnp.full(top_ref.shape, neg_large, f32)
        load_chunks(chunk_refs, kv_ref, sem)

    scale = jnp.asarray(HEAD ** (-0.5), bf16)
    q_masks = head_masks(wide, heads, 0)
    v_masks = head_masks(wide, heads, (heads * HEAD - start) // HEAD)
    lane = lax.broadcasted_iota(jnp.int32, (1, LIST * BLOCK), 1)
    for u in range(group):
        block = i * group + u
        mine = slice(u * BLOCK, (u + 1) * BLOCK)
        q_all = spread(q_ref[mine] * scale, q_masks)
        listed = listed_rows(addr_ref, kv_ref, block)
        scores = dot32(q_all, listed[:, :wide], ((1,), (1,)))
        limit = jnp.zeros((1, LIST * BLOCK), jnp.int32)
        for e in range(LIST):
            limit = jnp.where(lane // BLOCK == e, valid_ref[block * LIST + e], limit)
        scores = jnp.where(lane % BLOCK < limit, scores, neg_large)
        row_top = jnp.max(scores, axis=1, keepdims=True)
        shifted = jnp.exp(scores - row_top)
        probs = shifted * (1.0 / jnp.sum(shifted, axis=1, keepdims=True))
        probs_low = probs.astype(bf16)
        p_ref[u] = probs_low
        out = dot32(probs_low, listed[:, start:])
        att_ref[mine] = fold(out, v_masks).astype(bf16)
        row = lax.broadcasted_iota(jnp.int32, row_top.shape, 0) % BLOCK
        seen = jnp.where(row < query_ref[block], row_top, neg_large)
        for h in range(heads):
            best = jnp.max(seen[BLOCK * h : BLOCK * (h + 1)], axis=0, keepdims=True)
            top_ref[h : h + 1, :] = jnp.maximum(top_ref[h : h + 1, :], best)


def attention_forward(queries, kv_chunks, addr, valid, query_valid, heads, group=2):
    tokens, wide = queries.shape
    blocks = tokens // BLOCK
    rows = heads * BLOCK
    cols = LIST * BLOCK
    chunks = len(kv_chunks)
    kv_shape = (chunks * tokens, kv_chunks[0].shape[1])
    return pl.pallas_call(
        functools.partial(fwd_kernel, heads=heads, group=group, chunks=chunks),
        grid_spec=pltpu.PrefetchScalarGridSpec(
            num_scalar_prefetch=3,
            grid=(blocks // group,),
            in_specs=[pl.BlockSpec((group * BLOCK, wide), lambda i, *_: (i, 0))]
            + [pl.BlockSpec(memory_space=pl.ANY)] * chunks,
            out_specs=[
                pl.BlockSpec((group * BLOCK, wide), lambda i, *_: (i, 0)),
                pl.BlockSpec((group, rows, cols), lambda i, *_: (i, 0, 0)),
                pl.BlockSpec((8, 128), lambda i, *_: (0, 0)),
            ],
            scratch_shapes=[pltpu.VMEM(kv_shape, bf16), pltpu.SemaphoreType.DMA((chunks,))],
        ),
        out_shape=(
            jax.ShapeDtypeStruct((tokens, wide), bf16),
            jax.ShapeDtypeStruct((blocks, rows, cols), bf16),
            jax.ShapeDtypeStruct((8, 128), f32),
        ),
        compiler_params=small_params(dimension_semantics=("arbitrary",)),
        cost_estimate=pl.CostEstimate(
            flops=4 * blocks * rows * cols * wide,
            bytes_accessed=2 * (kv_shape[0] * kv_shape[1] + 2 * queries.size + blocks * rows * cols),
            transcendentals=blocks * rows * cols,
        ),
        name="attention_forward",
    )(addr, valid, query_valid, queries, *kv_chunks)


def bwd_kernel(addr_ref, q_ref, do_ref, p_ref, *refs, heads, group, chunks):
    chunk_refs = refs[:chunks]
    dq_ref, dkv_ref, sums_ref, kv_ref, acc_ref, sem = refs[chunks:]
    i = pl.program_id(0)
    wide = q_ref.shape[1]
    start = kv_ref.shape[1] - wide

    @pl.when(i == 0)
    def _():
        acc_ref[...] = jnp.zeros(acc_ref.shape, f32)
        sums_ref[...] = jnp.zeros(sums_ref.shape, f32)
        load_chunks(chunk_refs, kv_ref, sem)

    scale = jnp.asarray(HEAD ** (-0.5), bf16)
    q_masks = head_masks(wide, heads, 0)
    v_masks = head_masks(wide, heads, (heads * HEAD - start) // HEAD)
    for u in range(group):
        block = i * group + u
        mine = slice(u * BLOCK, (u + 1) * BLOCK)
        q_all = spread(q_ref[mine] * scale, q_masks)
        do_all = spread(do_ref[mine], v_masks)
        listed = listed_rows(addr_ref, kv_ref, block)
        probs_low = p_ref[u]
        probs = probs_low.astype(f32)
        d_probs = dot32(do_all, listed[:, start:], ((1,), (1,)))
        delta = jnp.sum(probs * d_probs, axis=1, keepdims=True)
        d_scores = (probs * (d_probs - delta)).astype(bf16)
        d_query = (fold(dot32(d_scores, listed[:, :wide]), q_masks) * HEAD ** (-0.5)).astype(bf16)
        dq_ref[mine] = d_query
        sums_ref[0:1, :wide] += jnp.sum(d_query.astype(f32), axis=0, keepdims=True)
        d_key = dot32(d_scores, q_all, ((0,), (0,)))
        d_value = dot32(probs_low, do_all, ((0,), (0,)))
        sums_ref[1:2, :wide] += jnp.sum(d_value, axis=0, keepdims=True)
        for e in range(LIST):
            rows = pl.ds(pl.multiple_of(addr_ref[block * LIST + e] * BLOCK, BLOCK), BLOCK)
            part = slice(BLOCK * e, BLOCK * (e + 1))
            acc_ref[rows, :start] += d_key[part, :start]
            acc_ref[rows, start:wide] += d_key[part, start:] + d_value[part, : wide - start]
            acc_ref[rows, wide:] += d_value[part, wide - start :]

    @pl.when(i == pl.num_programs(0) - 1)
    def _():
        dkv_ref[...] = acc_ref[...].astype(bf16)


def attention_backward(queries, d_out, probs, kv_chunks, addr, heads, group=2):
    tokens, wide = queries.shape
    blocks = tokens // BLOCK
    rows = heads * BLOCK
    cols = LIST * BLOCK
    chunks = len(kv_chunks)
    kv_shape = (chunks * tokens, kv_chunks[0].shape[1])
    return pl.pallas_call(
        functools.partial(bwd_kernel, heads=heads, group=group, chunks=chunks),
        grid_spec=pltpu.PrefetchScalarGridSpec(
            num_scalar_prefetch=1,
            grid=(blocks // group,),
            in_specs=[
                pl.BlockSpec((group * BLOCK, wide), lambda i, *_: (i, 0)),
                pl.BlockSpec((group * BLOCK, wide), lambda i, *_: (i, 0)),
                pl.BlockSpec((group, rows, cols), lambda i, *_: (i, 0, 0)),
            ]
            + [pl.BlockSpec(memory_space=pl.ANY)] * chunks,
            out_specs=[
                pl.BlockSpec((group * BLOCK, wide), lambda i, *_: (i, 0)),
                pl.BlockSpec(kv_shape, lambda i, *_: (0, 0), pipeline_mode=pl.Buffered(1)),
                pl.BlockSpec((8, wide), lambda i, *_: (0, 0)),
            ],
            scratch_shapes=[
                pltpu.VMEM(kv_shape, bf16),
                pltpu.VMEM(kv_shape, f32),
                pltpu.SemaphoreType.DMA((chunks,)),
            ],
        ),
        out_shape=(
            jax.ShapeDtypeStruct((tokens, wide), bf16),
            jax.ShapeDtypeStruct(kv_shape, bf16),
            jax.ShapeDtypeStruct((8, wide), f32),
        ),
        compiler_params=small_params(dimension_semantics=("arbitrary",)),
        cost_estimate=pl.CostEstimate(
            flops=8 * blocks * rows * cols * wide,
            bytes_accessed=2 * (2 * kv_shape[0] * kv_shape[1] + 3 * queries.size + blocks * rows * cols),
            transcendentals=0,
        ),
        name="attention_backward",
    )(addr, queries, d_out, probs, *kv_chunks)


def two_parts(values):
    high = values.astype(bf16)
    return high, (values - high.astype(f32)).astype(bf16)


def shampoo_kernel(
    g_ref, mb_ref, ls_ref, rs_ref, lr_ref, rr_ref, fac_ref, bg_ref, ln_ref, rn_ref, nb_ref, *, width
):
    for j in range(width):
        grad = g_ref[:, PB * j : PB * (j + 1)]
        bg_ref[j] = grad.astype(f32)
        ln_ref[j] = 0.5 * ls_ref[j] + 0.5 * dot32(grad, grad, ((1,), (1,)))
        rn_ref[j] = 0.5 * rs_ref[j] + 0.5 * dot32(grad, grad, ((0,), (0,)))
        left_hi, left_lo = two_parts(lr_ref[j])
        applied_hi, applied_lo = two_parts(dot32(left_hi, grad) + dot32(left_lo, grad))
        right_hi, right_lo = two_parts(rr_ref[j])
        step_val = (
            dot32(applied_hi, right_hi) + dot32(applied_hi, right_lo) + dot32(applied_lo, right_hi)
        )
        nb_ref[j] = (mb_ref[j] - rate_matrix * step_val) * fac_ref[j]


def shampoo(grads, width, master, left_s, right_s, left_r, right_r, factor):
    count = master.shape[0]
    block = pl.BlockSpec((width, PB, PB), lambda i: (i, 0, 0))
    shape = jax.ShapeDtypeStruct((count, PB, PB), f32)
    return pl.pallas_call(
        functools.partial(shampoo_kernel, width=width),
        grid=(count // width,),
        in_specs=[pl.BlockSpec((PB, PB * width), lambda i: (i, 0))]
        + [block] * 5
        + [pl.BlockSpec((width, 1, PB), lambda i: (i, 0, 0))],
        out_specs=[block] * 4,
        out_shape=[shape] * 4,
        compiler_params=params_of(),
        name="shampoo",
    )(grads, master, left_s, right_s, left_r, right_r, factor)


def per_device(
    inputs,
    lengths,
    global_blocks,
    random_blocks,
    master_blocks,
    outer_vectors,
    inner_biases,
    left_stats,
    right_stats,
    left_roots,
    right_roots,
    cotangent,
):
    tensor_count = lax.axis_size("tp")
    owner_count = lax.axis_size(OWN)
    ctx_count = lax.axis_size("ctx")
    heads_here = HEADS // tensor_count
    cols = heads_here * HEAD
    units = FF // tensor_count
    wide = 256
    pad = wide - cols
    tokens = inputs.shape[1]
    quarter = tokens // 4
    rows_blocks = tokens // BLOCK
    quarter_blocks = rows_blocks // 4
    block_count = SEQ // BLOCK
    blocks_here = master_blocks.shape[0]
    packed = owner_count == WIDE and blocks_here == 3 * WIDE
    shard_count = lax.axis_size("shard")
    me = lax.axis_index("tp")
    z = lax.axis_index("ctx")
    y = lax.axis_index("shard")
    owner = lax.axis_index(OWN)
    bo, b2, g1, beta1, g2, beta2 = [outer_vectors[i] for i in range(6)]

    first = jnp.arange(WIDE, dtype=jnp.int32)
    flat_in = inputs.reshape(tokens, D)
    own_in = lax.dynamic_slice_in_dim(flat_in, me * quarter, quarter, 0)
    if packed:
        own_packed = pack_rows(master_blocks)
        held_row = None
        for j in range(3):
            moved = owner_move(
                own_packed[PB * j : PB * (j + 1)],
                [(d, 3 * d + j) for d in range(WIDE) if 3 * d + j < WIDE],
            )
            held_row = moved if held_row is None else held_row + moved
        near = jnp.stack(
            [held_row] + [shift_ctx(held_row, step) for step in range(1, ctx_count)], axis=0
        )
        far = jnp.concatenate([shift_shard(near, u) for u in range(1, shard_count)], axis=0)
        weights = lax.all_gather(after(own_packed, far), OWN, axis=0, tiled=True)
        row_place = ((y - first // ctx_count) % shard_count) * ctx_count + (
            z - first % ctx_count
        ) % ctx_count
    else:
        weights = pack_rows(lax.all_gather(master_blocks.astype(bf16), OWN, axis=0, tiled=True))
        halves = weights[: WIDE * PB].reshape(2, WIDE // 2, PB, D)
        near, far = halves[0], halves[1]
        row_place = first
    w_q, w_kv, w_out = unpack_first(row_place, near, far, cols, wide)
    edge = 4 * cols
    w_up = weights[edge : edge + D]
    w_down = weights[edge + D :]

    chunks = [None] * ctx_count
    chunks[0] = jnp.concatenate(
        [lax.dynamic_slice_in_dim(flat_in, (me ^ r) * quarter, quarter, 0) for r in range(4)],
        axis=0,
    )
    moved = []
    for n, step in enumerate(near_first(ctx_count)):
        source = own_in if n < 2 else after(own_in, moved[n - 2])
        moved.append(shift_ctx(source, step))
        chunks[step] = jnp.concatenate(gather_quarters(moved[n]), axis=0)

    rel = jnp.arange(rows_blocks, dtype=jnp.int32)
    place = ((rel // quarter_blocks) ^ me) * quarter_blocks + rel % quarter_blocks
    rows = z * rows_blocks + place
    length = lengths[0]
    listed = jnp.concatenate(
        [
            jnp.stack([rows - 1, rows, rows + 1], axis=1),
            jnp.broadcast_to(global_blocks[0][None, :], (rows_blocks, 2)),
            random_blocks[0][place],
        ],
        axis=1,
    ).astype(jnp.int32)
    inside = (listed >= 0) & (listed < block_count)
    held = jnp.clip(listed, 0, block_count - 1)
    valid = jnp.where(inside, jnp.clip(length - listed * BLOCK, 0, BLOCK), 0).reshape(-1)
    local = held % rows_blocks
    addr = (
        ((z - held // rows_blocks) % ctx_count) * rows_blocks
        + ((local // quarter_blocks) ^ me) * quarter_blocks
        + local % quarter_blocks
    ).reshape(-1)
    query_valid = jnp.clip(length - rows * BLOCK, 0, BLOCK)

    inner_row = inner_biases[0]
    q_bias = jnp.concatenate([inner_row[:cols], jnp.zeros((pad,), f32)])
    kv_bias = jnp.concatenate([jnp.zeros((cols,), f32), inner_row[cols : 2 * cols]])
    up_bias = inner_row[2 * cols :]
    queries = (dot32(chunks[0], w_q) + q_bias).astype(bf16)
    kv_chunks = [(dot32(c, w_kv) + kv_bias).astype(bf16) for c in chunks]
    in_all = jnp.concatenate(chunks, axis=0)
    att, probs, tops = attention_forward(queries, kv_chunks, addr, valid, query_valid, heads_here)
    tops = tops[:heads_here, 0]

    own_f32 = own_in.astype(f32)
    branch = scatter_sum(dot32(att, w_out).astype(bf16).reshape(4, quarter, D)) + bo
    hidden = own_f32 + branch
    x_first, back_first = jax.vjp(layer_norm, hidden, g1, beta1)
    x_low = jnp.concatenate(gather_quarters(x_first.astype(bf16)), axis=0)
    gate = dot32(x_low, w_up) + up_bias
    act_low = gelu_tanh(gate).astype(bf16)
    ff = scatter_sum(dot32(act_low, w_down).astype(bf16).reshape(4, quarter, D)) + b2
    result, back_second = jax.vjp(layer_norm, x_first + ff, g2, beta2)
    out_own = result.astype(bf16)

    own_cot = lax.dynamic_slice_in_dim(cotangent.reshape(tokens, D), me * quarter, quarter, 0)
    positions = z * tokens + me * quarter + jnp.arange(quarter, dtype=jnp.int32)
    d_result = own_cot.astype(f32) * (positions < length).astype(f32)[:, None]
    d_mixed, d_gain2, d_shift2 = back_second(d_result)
    d_ff_own = d_mixed.astype(bf16)
    d_bias2 = jnp.sum(d_ff_own.astype(f32), axis=0)
    d_ff = jnp.concatenate(gather_quarters(d_ff_own), axis=0)
    d_act = dot32(d_ff, w_down, ((1,), (1,)))
    _, back_gelu = jax.vjp(gelu_tanh, gate)
    d_gate = back_gelu(d_act)[0].astype(bf16)
    d_upbias = jnp.sum(d_gate.astype(f32), axis=0)
    d_first = d_mixed + scatter_sum(
        dot32(d_gate, w_up, ((1,), (1,))).astype(bf16).reshape(4, quarter, D)
    )
    d_hidden, d_gain1, d_shift1 = back_first(d_first)
    d_branch_own = d_hidden.astype(bf16)
    d_bias_out = jnp.sum(d_branch_own.astype(f32), axis=0)
    d_branch = jnp.concatenate(gather_quarters(d_branch_own), axis=0)
    d_att = dot32(d_branch, w_out, ((1,), (1,))).astype(bf16)
    out_quarters = gather_quarters(after(out_own, d_branch))
    d_query, d_kv, sums = attention_backward(
        queries, d_att, probs, kv_chunks, addr, heads_here
    )

    g_down = dot32(act_low, d_ff, ((0,), (0,))).astype(bf16)
    g_up = dot32(x_low, d_gate, ((0,), (0,))).astype(bf16)
    if packed:
        early = jnp.concatenate([jnp.zeros((edge, D), bf16), g_up, g_down], axis=0)
        early_own = lax.psum_scatter(early, OWN, scatter_dimension=0, tiled=True)
    g_out = dot32(att, d_branch, ((0,), (0,)))[pad:].astype(bf16)

    total = d_hidden
    parts = []
    for step in near_first(ctx_count)[::-1] + [0]:
        part = dot32(d_kv[step * tokens : (step + 1) * tokens], w_kv, ((1,), (1,)))
        if step == 0:
            part = part + dot32(d_query, w_q, ((1,), (1,)))
        part = part.astype(bf16)
        parts.append(part)
        mine = scatter_sum(part.reshape(4, quarter, D))
        if step:
            mine = shift_ctx(mine.astype(bf16), ctx_count - step).astype(f32)
        total = total + mine
    grad_quarters = gather_quarters(total.astype(bf16))

    d_kv_late = after(d_kv, *parts[:2])
    g_q = dot32(chunks[0], d_query, ((0,), (0,)))
    g_kv = dot32(in_all, d_kv_late, ((0,), (0,)))
    g_qkv = qkv_pack(g_q, g_kv, cols)
    outer_part = jnp.stack([d_bias_out, d_bias2, d_gain1, d_shift1, d_gain2, d_shift2], axis=0)
    inner_part = jnp.concatenate([sums[0, :cols], sums[1, pad:], d_upbias])
    outer_cols = D // owner_count
    inner_cols = inner_part.shape[0] // owner_count
    if packed:
        extra = 16
        vector = jnp.concatenate(
            [
                outer_part.reshape(6, owner_count, outer_cols)
                .transpose(1, 0, 2)
                .reshape(owner_count, -1),
                inner_part.reshape(owner_count, inner_cols),
            ],
            axis=1,
        ).astype(bf16)
        used = vector.shape[1]
        left = tops
        pieces = []
        for _ in range(3):
            piece = lax.reduce_precision(left, 8, 7)
            pieces.append(piece)
            left = left - piece
        slots = jnp.where(
            (jnp.arange(owner_count) == owner)[:, None], jnp.concatenate(pieces)[None, :], 0.0
        ).astype(bf16)
        slots = jnp.broadcast_to(slots.reshape(1, -1), (owner_count, slots.size))
        vector = jnp.stack(
            [
                jnp.pad(vector, ((0, 0), (0, D - used))),
                jnp.pad(slots, ((0, 0), (0, D - slots.shape[1]))),
            ],
            axis=1,
        )
        vector = jnp.pad(vector, ((0, 0), (0, extra - 2), (0, 0)))
        rows_of = jnp.concatenate([g_qkv, g_out], axis=0).reshape(owner_count, PB, D)
        late = jnp.concatenate([rows_of, vector], axis=1).reshape(
            shard_count, ctx_count, PB + extra, D
        )
        half = lax.dynamic_index_in_dim(late, y, 0, keepdims=False).astype(f32)
        for u in range(1, shard_count):
            sent = lax.dynamic_index_in_dim(late, (y + u) % shard_count, 0, keepdims=False)
            half = half + shift_shard(sent, u).astype(f32)
        half = half.astype(bf16)
        late_own = lax.dynamic_index_in_dim(half, z, 0, keepdims=False).astype(f32)
        for step in near_first(ctx_count):
            sent = lax.dynamic_index_in_dim(half, (z + step) % ctx_count, 0, keepdims=False)
            late_own = late_own + shift_ctx(sent, step).astype(f32)
        late_low = late_own[:PB].astype(bf16)
        own_grads = early_own + jnp.concatenate(
            [
                owner_move(
                    late_low, [(3 * d + j, d) for d in range(WIDE) if 3 * d + j < WIDE]
                )
                for j in range(3)
            ],
            axis=0,
        )
        row = late_own[PB]
        outer_own = row[: 6 * outer_cols].reshape(6, outer_cols)
        inner_own = row[6 * outer_cols : used][None, :]
        seen = late_own[PB + 1, : slots.shape[1]].reshape(owner_count, 3, heads_here)
        maxima = jnp.max(seen[:, 0] + seen[:, 1] + seen[:, 2], axis=0)
        width = WIDE
    else:
        grads = jnp.concatenate([g_qkv, g_out, g_up, g_down], axis=0)
        blocks = grads.reshape(-1, PB, WIDE, PB).transpose(0, 2, 1, 3).reshape(-1, PB, PB)
        own_grads = lax.psum_scatter(blocks, OWN, scatter_dimension=0, tiled=True)
        own_grads = own_grads.reshape(blocks_here * PB, PB)
        outer_own = lax.psum_scatter(outer_part, OWN, scatter_dimension=1, tiled=True)
        inner_own = lax.psum_scatter(inner_part[None, :], OWN, scatter_dimension=1, tiled=True)
        maxima = lax.pmax(tops, OWN)
        width = 1
    outer_own = outer_own + swap(outer_own, 1)
    outer_own = outer_own + swap(outer_own, 2)

    clip_sqrt = jnp.sqrt(tau_clip / jnp.maximum(maxima, tau_clip))
    head_factor = jnp.repeat(clip_sqrt, HEAD)
    table = jnp.concatenate([head_factor, head_factor, jnp.ones((cols,), f32)]).reshape(-1, PB)
    own_index = owner * blocks_here + jnp.arange(blocks_here, dtype=jnp.int32)
    per_row = 3 * cols // PB
    own_factor = jnp.where(
        (own_index < D // PB * per_row)[:, None], table[own_index % per_row], 1.0
    )
    block_sum, left_new, right_new, new_blocks = shampoo(
        own_grads,
        width,
        master_blocks,
        left_stats,
        right_stats,
        left_roots,
        right_roots,
        own_factor[:, None, :],
    )
    own_outer = lax.dynamic_slice_in_dim(outer_vectors, owner * outer_cols, outer_cols, 1)
    new_outer = own_outer - rate_vector * outer_own
    inner_factor = jnp.concatenate([head_factor, jnp.ones((cols + units,), f32)])
    own_inner_factor = lax.dynamic_slice_in_dim(inner_factor, owner * inner_cols, inner_cols, 0)
    own_inner = lax.dynamic_slice_in_dim(inner_biases, owner * inner_cols, inner_cols, 1)
    new_inner = (own_inner - rate_vector * inner_own) * own_inner_factor[None, :]

    def placed(quarters):
        whole = jnp.zeros((tokens, D), bf16)
        for r, piece in enumerate(quarters):
            whole = lax.dynamic_update_slice_in_dim(whole, piece, (me ^ r) * quarter, 0)
        return whole.reshape(inputs.shape)

    return (
        placed(out_quarters),
        placed(grad_quarters),
        block_sum,
        outer_own,
        inner_own,
        maxima,
        left_new,
        right_new,
        new_blocks,
        new_outer,
        new_inner,
    )


def solution(mesh):
    return jax.shard_map(
        per_device,
        mesh=mesh,
        in_specs=(
            P("shard", "ctx", None),
            P("shard"),
            P("shard", None),
            P("shard", "ctx", None),
            P(("shard", "ctx", "tp"), None, None),
            P(),
            P("tp", None),
            P(("shard", "ctx", "tp"), None, None),
            P(("shard", "ctx", "tp"), None, None),
            P(("shard", "ctx", "tp"), None, None),
            P(("shard", "ctx", "tp"), None, None),
            P("shard", "ctx", None),
        ),
        out_specs=(
            P("shard", "ctx", None),
            P("shard", "ctx", None),
            P(("shard", "ctx", "tp"), None, None),
            P(None, ("shard", "ctx")),
            P("tp", ("shard", "ctx")),
            P("tp"),
            P(("shard", "ctx", "tp"), None, None),
            P(("shard", "ctx", "tp"), None, None),
            P(("shard", "ctx", "tp"), None, None),
            P(None, ("shard", "ctx")),
            P("tp", ("shard", "ctx")),
        ),
        check_vma=False,
    )
```

```python
import functools

import jax
import jax.numpy as jnp
from jax import lax
from jax.experimental import pallas as pl
from jax.experimental.pallas import tpu as pltpu
from jax.sharding import PartitionSpec as P


D = 768
HEADS = 12
HEAD = 64
BLOCK = 64
SEQ = 4096
PB = 96
LIST = 8
WIDE = 8

eps_norm = 1e-06
tau_clip = 9.0
rate_matrix = 0.3
rate_vector = 0.001
neg_large = -1e30
GELU = 0.7978845608028654
ANY = pl.ANY
bf16 = jnp.bfloat16
f32 = jnp.float32
OWN = ("shard", "ctx")


def params_of(mib, **more):
    return pltpu.CompilerParams(vmem_limit_bytes=mib << 20, **more)


def in_place():
    return pl.BlockSpec(memory_space=ANY)


def whole_block(shape, single=False):
    zeros = (0,) * len(shape)
    mode = dict(pipeline_mode=pl.Buffered(1)) if single else {}
    return pl.BlockSpec(shape, lambda *_: zeros, **mode)


def cost(flops, moved, exps=0):
    return pl.CostEstimate(flops=flops, bytes_accessed=moved, transcendentals=exps)


def dot32(left, right, dims=((1,), (0,))):
    return lax.dot_general(left, right, (dims, ((), ())), preferred_element_type=f32)


def normalized(values):
    centred = values - jnp.mean(values, axis=-1, keepdims=True)
    factor = lax.rsqrt(jnp.mean(centred * centred, axis=-1, keepdims=True) + eps_norm)
    return centred * factor, factor


def norm_back(grad, gain, unit, factor):
    scaled = grad * gain
    mean_grad = jnp.mean(scaled, axis=-1, keepdims=True)
    mean_unit = jnp.mean(scaled * unit, axis=-1, keepdims=True)
    return factor * (scaled - mean_grad - unit * mean_unit)


def column_sum(values):
    return jnp.sum(values, axis=0, keepdims=True)


def gelu_parts(gate):
    inner = GELU * (gate + 0.044715 * gate * gate * gate)
    return inner, jnp.tanh(inner)


def copy_in(source, target, sem):
    copy = pltpu.make_async_copy(source, target, sem)
    copy.start()
    return copy


def swap(rows, mask):
    count = lax.axis_size("tp")
    return lax.ppermute(rows, "tp", [(i, i ^ mask) for i in range(count)])


def shift_ctx(rows, step):
    count = lax.axis_size("ctx")
    return lax.ppermute(rows, "ctx", [(i, (i + step) % count) for i in range(count)])


def shift_shard(rows, step):
    count = lax.axis_size("shard")
    return lax.ppermute(rows, "shard", [(i, (i + step) % count) for i in range(count)])


def owner_move(rows, pairs):
    return lax.ppermute(rows, OWN, pairs)


def after(value, *others):
    return lax.optimization_barrier((value,) + others)[0]


def near_first(count):
    return sorted(range(1, count), key=lambda step: min(step, count - step))


def pack_kernel(blocks_ref, out_ref):
    for j in range(WIDE):
        out_ref[:, PB * j : PB * (j + 1)] = blocks_ref[j].astype(bf16)


def pack_rows(blocks):
    rows = blocks.shape[0] // WIDE
    return pl.pallas_call(
        pack_kernel,
        grid=(rows,),
        in_specs=[pl.BlockSpec((WIDE, PB, PB), lambda i: (i, 0, 0))],
        out_specs=pl.BlockSpec((PB, PB * WIDE), lambda i: (i, 0)),
        out_shape=jax.ShapeDtypeStruct((rows * PB, PB * WIDE), bf16),
        compiler_params=params_of(3),
        name="pack_rows",
    )(blocks)


def unpack_kernel(turn_ref, near_ref, far_ref, q_ref, kv_ref, out_ref, all_ref, *, cols):
    half = near_ref.shape[0]
    all_ref[:half] = near_ref[...]
    all_ref[half:] = far_ref[...]
    q_ref[...] = jnp.zeros(q_ref.shape, bf16)
    for i in range(D // PB):
        for c in range(3):
            unit = 3 * i + c
            piece = all_ref[turn_ref[unit // 4], :, cols * (unit % 4) : cols * (unit % 4 + 1)]
            if c == 0:
                q_ref[PB * i : PB * (i + 1), :cols] = piece
            else:
                kv_ref[PB * i : PB * (i + 1), cols * (c - 1) : cols * c] = piece
    pad = out_ref.shape[0] - cols
    out_ref[:pad, :] = jnp.zeros((pad, D), bf16)
    for i in range(cols // PB):
        out_ref[pad + PB * i : pad + PB * (i + 1), :] = all_ref[turn_ref[3 * cols // PB + i]]


def unpack_first(turns, near, far, cols, wide):
    full = pl.BlockSpec(memory_space=pltpu.VMEM)
    return pl.pallas_call(
        functools.partial(unpack_kernel, cols=cols),
        in_specs=[pl.BlockSpec(memory_space=pltpu.SMEM), full, full],
        out_specs=[full, full, full],
        out_shape=(
            jax.ShapeDtypeStruct((D, wide), bf16),
            jax.ShapeDtypeStruct((D, 2 * cols), bf16),
            jax.ShapeDtypeStruct((wide, D), bf16),
        ),
        scratch_shapes=[pltpu.VMEM((near.shape[0] + far.shape[0], PB, D), bf16)],
        compiler_params=params_of(8),
        name="unpack_first",
    )(turns, near, far)


def tables_kernel(
    ids_ref, len_ref, glob_ref, rand_ref, addr_ref, valid_ref, query_ref, turn_ref, *, rows_blocks, ctx_count, shard_count
):
    me, y, z, owner = ids_ref[0], ids_ref[1], ids_ref[2], ids_ref[3]
    per = rows_blocks // 4
    length = len_ref[0]
    block_count = SEQ // BLOCK

    def body(i, carry):
        place = (lax.div(i, per) ^ me) * per + lax.rem(i, per)
        row = z * rows_blocks + place
        listed = [row - 1, row, row + 1, glob_ref[0, 0], glob_ref[0, 1]]
        listed += [rand_ref[place, n] for n in range(3)]
        for e, block in enumerate(listed):
            held = jnp.clip(block, 0, block_count - 1)
            valid = jnp.clip(length - block * BLOCK, 0, BLOCK)
            valid_ref[i * LIST + e] = jnp.where(held == block, valid, 0)
            chunk = lax.div(held, rows_blocks)
            local = held - chunk * rows_blocks
            step = lax.rem(z - chunk + ctx_count, ctx_count)
            part = lax.div(local, per)
            addr_ref[i * LIST + e] = (
                step * rows_blocks + (part ^ me) * per + (local - part * per)
            )
        query_ref[i] = jnp.clip(length - row * BLOCK, 0, BLOCK)
        return carry

    lax.fori_loop(0, rows_blocks, body, 0)
    for k in range(WIDE):
        ky, kz = k // ctx_count, k % ctx_count
        turn_ref[k] = lax.rem(y - ky + shard_count, shard_count) * ctx_count + lax.rem(
            z - kz + ctx_count, ctx_count
        )
        turn_ref[WIDE + k] = lax.rem(ky - y + shard_count, shard_count) * ctx_count + lax.rem(
            kz - z + ctx_count, ctx_count
        )
        turn_ref[2 * WIDE + k] = lax.rem(y - ky + shard_count, shard_count) * ctx_count + lax.rem(
            z - kz + ctx_count, ctx_count
        )
    turn_ref[3 * WIDE] = owner
    turn_ref[3 * WIDE + 1] = me
    tokens = rows_blocks * BLOCK
    quarter = tokens // 4
    turn_ref[3 * WIDE + 2] = jnp.clip(length - z * tokens - me * quarter, 0, quarter)


def index_tables(ids, lengths, global_blocks, random_blocks, rows_blocks, ctx_count, shard_count):
    smem = pl.BlockSpec(memory_space=pltpu.SMEM)
    shapes = [(rows_blocks * LIST,), (rows_blocks * LIST,), (rows_blocks,), (3 * WIDE + 8,)]
    return pl.pallas_call(
        functools.partial(
            tables_kernel, rows_blocks=rows_blocks, ctx_count=ctx_count, shard_count=shard_count
        ),
        in_specs=[smem] * 4,
        out_specs=[smem] * 4,
        out_shape=[jax.ShapeDtypeStruct(shape, jnp.int32) for shape in shapes],
        compiler_params=params_of(2),
        name="index_tables",
    )(ids, lengths, global_blocks, random_blocks)


def pick_kernel(ids_ref, x_ref, out_ref):
    out_ref[...] = x_ref[...]


def pick_quarter(ids, values):
    rows = values.shape[0] // 4
    return pl.pallas_call(
        pick_kernel,
        grid_spec=pltpu.PrefetchScalarGridSpec(
            num_scalar_prefetch=1,
            grid=(1,),
            in_specs=[pl.BlockSpec((rows, D), lambda i, ids: (ids[0], 0))],
            out_specs=pl.BlockSpec((rows, D), lambda i, ids: (0, 0)),
        ),
        out_shape=jax.ShapeDtypeStruct((rows, D), bf16),
        compiler_params=params_of(3),
        name="pick_quarter",
    )(ids, values)


def place_kernel(ids_ref, *refs):
    pieces, (out_ref, sem) = refs[:4], refs[4:]
    rows = pieces[0].shape[0]
    loads = []
    for r, piece in enumerate(pieces):
        start = pl.multiple_of((ids_ref[0] ^ r) * rows, rows)
        loads.append(copy_in(piece, out_ref.at[pl.ds(start, rows)], sem.at[r]))
    for load in loads:
        load.wait()


def place_quarters(ids, pieces):
    rows = pieces[0].shape[0]
    return pl.pallas_call(
        place_kernel,
        grid_spec=pltpu.PrefetchScalarGridSpec(
            num_scalar_prefetch=1,
            grid=(1,),
            in_specs=[in_place()] * 4,
            out_specs=whole_block((4 * rows, D), single=True),
            scratch_shapes=[pltpu.SemaphoreType.DMA((4,))],
        ),
        out_shape=jax.ShapeDtypeStruct((4 * rows, D), bf16),
        compiler_params=params_of(4),
    )(ids, *pieces)


def sort_kernel(turn_ref, a_ref, b_ref, c_ref, first_ref, rest_ref):
    for group in range(3):
        slot = lax.rem(WIDE * group + turn_ref[3 * WIDE], 3)
        value = jnp.where(slot == 0, a_ref[...], jnp.where(slot == 1, b_ref[...], c_ref[...]))
        if group == 0:
            first_ref[...] = value
        else:
            rest_ref[PB * (group - 1) : PB * group] = value


def sort_held(turns, held):
    return pl.pallas_call(
        sort_kernel,
        grid_spec=pltpu.PrefetchScalarGridSpec(
            num_scalar_prefetch=1,
            grid=(1,),
            in_specs=[whole_block((PB, D))] * 3,
            out_specs=[whole_block((PB, D)), whole_block((2 * PB, D))],
        ),
        out_shape=[
            jax.ShapeDtypeStruct((PB, D), bf16),
            jax.ShapeDtypeStruct((2 * PB, D), bf16),
        ],
        compiler_params=params_of(4),
        name="sort_held",
    )(turns, *held)


def deal_kernel(turn_ref, first_ref, up_ref, down_ref, a_ref, b_ref, c_ref):
    groups = (first_ref[:PB].astype(bf16), up_ref[...].astype(bf16), down_ref[...].astype(bf16))
    for slot, out_ref in enumerate((a_ref, b_ref, c_ref)):
        target = lax.rem(3 * (turn_ref[3 * WIDE] + WIDE - slot), WIDE)
        group = lax.div(3 * target + slot, WIDE)
        out_ref[...] = jnp.where(group == 0, groups[0], jnp.where(group == 1, groups[1], groups[2]))


def deal_rows(turns, first, up, down):
    one = whole_block((PB, D))
    return pl.pallas_call(
        deal_kernel,
        grid_spec=pltpu.PrefetchScalarGridSpec(
            num_scalar_prefetch=1,
            grid=(1,),
            in_specs=[whole_block(first.shape), one, one],
            out_specs=[one] * 3,
        ),
        out_shape=[jax.ShapeDtypeStruct((PB, D), bf16)] * 3,
        compiler_params=params_of(6),
        name="deal_rows",
    )(turns, first, up, down)


def project_kernel(ids_ref, *refs, step, heads_q, chained):
    count = 1 if heads_q else 4
    pieces = refs[:count]
    rest = list(refs[count:])
    wkv_ref, bkv_ref = rest[:2]
    rest = rest[2:]
    if heads_q:
        wq_ref, bq_ref = rest[:2]
        rest = rest[2:]
    if chained:
        rest = rest[2:]
    in_all, kv_all = rest[:2]
    rest = rest[2:]
    if heads_q:
        q_ref = rest[0]
        rest = rest[1:]
    x_ref, kv_ref, sem, out_sem = rest
    tokens = x_ref.shape[0]
    rows = tokens // 4
    loads = []
    for r in range(4):
        if heads_q:
            source = pieces[0].at[pl.ds(pl.multiple_of((ids_ref[0] ^ r) * rows, rows), rows)]
        else:
            source = pieces[r]
        loads.append(copy_in(source, x_ref.at[pl.ds(r * rows, rows)], sem.at[r]))
    for load in loads:
        load.wait()
    saves = [copy_in(x_ref, in_all.at[pl.ds(step * tokens, tokens)], out_sem.at[0])]

    def body(r, carry):
        mine = pl.ds(pl.multiple_of(r * rows, rows), rows)
        kv_ref[mine, :] = (dot32(x_ref[mine, :], wkv_ref[...]) + bkv_ref[...]).astype(bf16)
        if heads_q:
            q_ref[mine, :] = (dot32(x_ref[mine, :], wq_ref[...]) + bq_ref[...]).astype(bf16)
        return carry

    lax.fori_loop(0, 4, body, 0)
    saves.append(copy_in(kv_ref, kv_all.at[pl.ds(step * tokens, tokens)], out_sem.at[1]))
    for save in saves:
        save.wait()


def project_chunk(ids, pieces, step, count, w_kv, b_kv, w_q, b_q, carried):
    width = pieces[0].shape[1]
    tokens = pieces[0].shape[0] * len(pieces)
    kv_cols = w_kv.shape[1]
    with_q = w_q is not None
    chained = carried is not None
    args = list(pieces) + [w_kv, b_kv]
    specs = [in_place()] * len(pieces) + [whole_block(w_kv.shape), whole_block(b_kv.shape)]
    if with_q:
        args += [w_q, b_q]
        specs += [whole_block(w_q.shape), whole_block(b_q.shape)]
    aliases = {}
    if chained:
        aliases = {len(args) + 1: 0, len(args) + 2: 1}
        args += list(carried)
        specs += [in_place()] * 2
    shapes = [
        jax.ShapeDtypeStruct((count * tokens, width), bf16),
        jax.ShapeDtypeStruct((count * tokens, kv_cols), bf16),
    ]
    outs = [in_place()] * 2
    if with_q:
        shapes.append(jax.ShapeDtypeStruct((tokens, w_q.shape[1]), bf16))
        outs.append(whole_block((tokens, w_q.shape[1])))
    return pl.pallas_call(
        functools.partial(project_kernel, step=step, heads_q=with_q, chained=chained),
        grid_spec=pltpu.PrefetchScalarGridSpec(
            num_scalar_prefetch=1,
            grid=(1,),
            in_specs=specs,
            out_specs=outs,
            scratch_shapes=[
                pltpu.VMEM((tokens, width), bf16),
                pltpu.VMEM((tokens, kv_cols), bf16),
                pltpu.SemaphoreType.DMA((4,)),
                pltpu.SemaphoreType.DMA((2,)),
            ],
        ),
        out_shape=shapes,
        input_output_aliases=aliases,
        compiler_params=params_of(8),
        cost_estimate=cost(2 * tokens * width * kv_cols, 4 * tokens * (width + kv_cols)),
    )(ids, *args)


def split_store(r, value, keep_ref, send_ref):
    @pl.when(r % 2 == 0)
    def _():
        keep_ref[...] = value

    @pl.when(r % 2 == 1)
    def _():
        send_ref[...] = value


def out_kernel(att_ref, w_ref, keep_ref, send_ref):
    split_store(
        pl.program_id(0), dot32(att_ref[...], w_ref[...]).astype(bf16), keep_ref, send_ref
    )


def out_project(att, w_out):
    tokens, wide = att.shape
    rows = tokens // 4
    half = pl.BlockSpec((rows, D), lambda r: (r // 2, 0))
    shape = jax.ShapeDtypeStruct((tokens // 2, D), bf16)
    return pl.pallas_call(
        out_kernel,
        grid=(4,),
        in_specs=[pl.BlockSpec((rows, wide), lambda r: (r, 0)), whole_block(w_out.shape)],
        out_specs=[half, half],
        out_shape=[shape, shape],
        compiler_params=params_of(4),
        cost_estimate=cost(2 * tokens * wide * D, 2 * tokens * (wide + D)),
        name="out_project",
    )(att, w_out)


def summed(keep_ref, sent_ref, got_ref):
    return keep_ref[...].astype(f32) + sent_ref[...].astype(f32) + got_ref[...].astype(f32)


def first_norm_kernel(ids_ref, x_ref, keep_ref, sent_ref, got_ref, vec_ref, hid_ref, x1_ref, low_ref):
    hidden = x_ref[...].astype(f32) + (summed(keep_ref, sent_ref, got_ref) + vec_ref[0:1, :])
    hid_ref[...] = hidden
    unit, _ = normalized(hidden)
    x1 = unit * vec_ref[2:3, :] + vec_ref[3:4, :]
    x1_ref[...] = x1
    low_ref[...] = x1.astype(bf16)


def norm_tiles(rows):
    return 4 if rows % 64 == 0 else 1


def first_norm(ids, values, keep, sent, got, vectors):
    rows = got.shape[0]
    tiles = norm_tiles(rows)
    block = pl.BlockSpec((rows // tiles, D), lambda i, ids: (i, 0))
    mine = pl.BlockSpec((rows // tiles, D), lambda i, ids: (ids[0] * tiles + i, 0))
    return pl.pallas_call(
        first_norm_kernel,
        grid_spec=pltpu.PrefetchScalarGridSpec(
            num_scalar_prefetch=1,
            grid=(tiles,),
            in_specs=[mine] + [block] * 3 + [whole_block(vectors.shape)],
            out_specs=[block] * 3,
        ),
        out_shape=[
            jax.ShapeDtypeStruct((rows, D), f32),
            jax.ShapeDtypeStruct((rows, D), f32),
            jax.ShapeDtypeStruct((rows, D), bf16),
        ],
        compiler_params=params_of(5),
        cost_estimate=cost(20 * rows * D, 20 * rows * D),
        name="first_norm",
    )(ids, values, keep, sent, got, vectors)


def second_norm_kernel(
    turn_ref, x1_ref, keep_ref, sent_ref, got_ref, cot_ref, vec_ref, out_ref, dmix_ref, low_ref, sums_ref
):
    i = pl.program_id(0)

    @pl.when(i == 0)
    def _():
        sums_ref[...] = jnp.zeros(sums_ref.shape, f32)

    mixed = x1_ref[...] + (summed(keep_ref, sent_ref, got_ref) + vec_ref[1:2, :])
    unit, factor = normalized(mixed)
    out_ref[...] = (unit * vec_ref[4:5, :] + vec_ref[5:6, :]).astype(bf16)
    row = lax.broadcasted_iota(jnp.int32, mixed.shape, 0) + i * mixed.shape[0]
    grad = jnp.where(row < turn_ref[3 * WIDE + 2], cot_ref[...].astype(f32), 0.0)
    d_mixed = norm_back(grad, vec_ref[4:5, :], unit, factor)
    dmix_ref[...] = d_mixed
    low = d_mixed.astype(bf16)
    low_ref[...] = low
    sums_ref[0:1, :] += column_sum(grad * unit)
    sums_ref[1:2, :] += column_sum(grad)
    sums_ref[2:3, :] += column_sum(low.astype(f32))


def second_norm(turns, x1, keep, sent, got, cot, vectors):
    rows = x1.shape[0]
    tiles = norm_tiles(rows)
    block = pl.BlockSpec((rows // tiles, D), lambda i, *_: (i, 0))
    mine = pl.BlockSpec((rows // tiles, D), lambda i, turns: (turns[3 * WIDE + 1] * tiles + i, 0))
    return pl.pallas_call(
        second_norm_kernel,
        grid_spec=pltpu.PrefetchScalarGridSpec(
            num_scalar_prefetch=1,
            grid=(tiles,),
            in_specs=[block] * 4 + [mine, whole_block(vectors.shape)],
            out_specs=[block] * 3 + [whole_block((8, D))],
        ),
        out_shape=[
            jax.ShapeDtypeStruct((rows, D), bf16),
            jax.ShapeDtypeStruct((rows, D), f32),
            jax.ShapeDtypeStruct((rows, D), bf16),
            jax.ShapeDtypeStruct((8, D), f32),
        ],
        compiler_params=params_of(6),
        cost_estimate=cost(40 * rows * D, 20 * rows * D),
        name="second_norm",
    )(turns, x1, keep, sent, got, cot, vectors)


def first_back_kernel(
    hid_ref, dmix_ref, keep_ref, sent_ref, got_ref, vec_ref, dhid_ref, low_ref, sums_ref
):
    @pl.when(pl.program_id(0) == 0)
    def _():
        sums_ref[...] = jnp.zeros(sums_ref.shape, f32)

    grad = dmix_ref[...] + summed(keep_ref, sent_ref, got_ref)
    unit, factor = normalized(hid_ref[...])
    d_hidden = norm_back(grad, vec_ref[2:3, :], unit, factor)
    dhid_ref[...] = d_hidden
    low = d_hidden.astype(bf16)
    low_ref[...] = low
    sums_ref[0:1, :] += column_sum(grad * unit)
    sums_ref[1:2, :] += column_sum(grad)
    sums_ref[2:3, :] += column_sum(low.astype(f32))


def first_back(hidden, d_mixed, keep, sent, got, vectors):
    rows = hidden.shape[0]
    tiles = norm_tiles(rows)
    block = pl.BlockSpec((rows // tiles, D), lambda i: (i, 0))
    return pl.pallas_call(
        first_back_kernel,
        grid=(tiles,),
        in_specs=[block] * 5 + [whole_block(vectors.shape)],
        out_specs=[block] * 2 + [whole_block((8, D))],
        out_shape=[
            jax.ShapeDtypeStruct((rows, D), f32),
            jax.ShapeDtypeStruct((rows, D), bf16),
            jax.ShapeDtypeStruct((8, D), f32),
        ],
        compiler_params=params_of(6),
        cost_estimate=cost(40 * rows * D, 20 * rows * D),
        name="first_back",
    )(hidden, d_mixed, keep, sent, got, vectors)


def assemble_kernel(turn_ref, near_ref, far_ref, up_ref, down_ref, sem):
    near = near_ref.shape[0]
    copies = []
    for p in range(WIDE):
        source = near_ref.at[p] if p < near else far_ref.at[p - near]
        start = pl.multiple_of(turn_ref[2 * WIDE + p] * PB, PB)
        for n, target in enumerate((up_ref, down_ref)):
            copies.append(
                copy_in(source.at[pl.ds(PB * n, PB)], target.at[pl.ds(start, PB)], sem)
            )
    for copy in copies:
        copy.wait()


def assemble(turns, near, far):
    return pl.pallas_call(
        assemble_kernel,
        grid_spec=pltpu.PrefetchScalarGridSpec(
            num_scalar_prefetch=1,
            grid=(1,),
            in_specs=[in_place()] * 2,
            out_specs=[whole_block((D, D), single=True)] * 2,
            scratch_shapes=[pltpu.SemaphoreType.DMA],
        ),
        out_shape=[jax.ShapeDtypeStruct((D, D), bf16)] * 2,
        compiler_params=params_of(5),
        cost_estimate=cost(0, 8 * D * D),
        name="assemble",
    )(turns, near, far)


def feed_kernel(
    xa_ref, xb_ref, wu_ref, wd_ref, b_ref, x_ref, gate_ref, act_ref, keep_ref, send_ref, sem
):
    i = pl.program_id(0)
    rows = xa_ref.shape[0]

    first = pltpu.make_async_copy(xa_ref, x_ref.at[pl.ds(0, rows)], sem.at[0])
    second = pltpu.make_async_copy(xb_ref, x_ref.at[pl.ds(rows, rows)], sem.at[1])

    @pl.when(i == 0)
    def _():
        first.start()
        second.start()
        first.wait()

    @pl.when(i == 1)
    def _():
        second.wait()

    mine = pl.ds(pl.multiple_of(i * rows, rows), rows)
    gate = dot32(x_ref[mine, :], wu_ref[...]) + b_ref[...]
    gate_ref[...] = gate
    _, tanh = gelu_parts(gate)
    act = (0.5 * gate * (1.0 + tanh)).astype(bf16)
    act_ref[...] = act

    split_store(i, dot32(act, wd_ref[...]).astype(bf16), keep_ref, send_ref)


def feed_forward(piece_a, piece_b, w_up, w_down, up_bias):
    rows = piece_a.shape[0]
    step = pl.BlockSpec((rows, D), lambda i, *_: (i, 0))
    one = whole_block((rows, D))
    return pl.pallas_call(
        feed_kernel,
        grid_spec=pltpu.PrefetchScalarGridSpec(num_scalar_prefetch=0, grid=(2,),
        in_specs=[in_place()] * 2 + [whole_block((D, D))] * 2 + [whole_block(up_bias.shape)],
        out_specs=[whole_block((2 * rows, D)), step, step, one, one],
        scratch_shapes=[pltpu.SemaphoreType.DMA((2,))],
        ),
        out_shape=[
            jax.ShapeDtypeStruct((2 * rows, D), bf16),
            jax.ShapeDtypeStruct((2 * rows, D), f32),
            jax.ShapeDtypeStruct((2 * rows, D), bf16),
            jax.ShapeDtypeStruct((rows, D), bf16),
            jax.ShapeDtypeStruct((rows, D), bf16),
        ],
        compiler_params=params_of(13),
        cost_estimate=cost(8 * rows * D * D, 24 * rows * D),
        name="feed_forward",
    )(piece_a, piece_b, w_up, w_down, up_bias)


def feed_back_kernel(
    da_ref, db_ref, wu_ref, wd_ref, gate_ref, d_ref, dgate_ref, keep_ref, send_ref, sums_ref, sem
):
    i = pl.program_id(0)
    rows = da_ref.shape[0]

    first = pltpu.make_async_copy(da_ref, d_ref.at[pl.ds(0, rows)], sem.at[0])
    second = pltpu.make_async_copy(db_ref, d_ref.at[pl.ds(rows, rows)], sem.at[1])

    @pl.when(i == 0)
    def _():
        first.start()
        second.start()
        sums_ref[...] = jnp.zeros(sums_ref.shape, f32)
        first.wait()

    @pl.when(i == 1)
    def _():
        second.wait()

    mine = pl.ds(pl.multiple_of(i * rows, rows), rows)
    d_act = dot32(d_ref[mine, :], wd_ref[...], ((1,), (1,)))
    gate = gate_ref[...]
    _, tanh = gelu_parts(gate)
    slope = GELU * (1.0 + 3.0 * 0.044715 * gate * gate)
    d_gate = (d_act * (0.5 * (1.0 + tanh) + 0.5 * gate * (1.0 - tanh * tanh) * slope)).astype(bf16)
    dgate_ref[...] = d_gate
    sums_ref[0:1, :] += column_sum(d_gate.astype(f32))

    split_store(i, dot32(d_gate, wu_ref[...], ((1,), (1,))).astype(bf16), keep_ref, send_ref)


def feed_back(piece_a, piece_b, w_up, w_down, gate):
    rows = piece_a.shape[0]
    step = pl.BlockSpec((rows, D), lambda i, *_: (i, 0))
    one = whole_block((rows, D))
    return pl.pallas_call(
        feed_back_kernel,
        grid_spec=pltpu.PrefetchScalarGridSpec(num_scalar_prefetch=0, grid=(2,),
        in_specs=[in_place()] * 2 + [whole_block((D, D))] * 2 + [step],
        out_specs=[whole_block((2 * rows, D)), step, one, one, whole_block((8, D))],
        scratch_shapes=[pltpu.SemaphoreType.DMA((2,))],
        ),
        out_shape=[
            jax.ShapeDtypeStruct((2 * rows, D), bf16),
            jax.ShapeDtypeStruct((2 * rows, D), bf16),
            jax.ShapeDtypeStruct((rows, D), bf16),
            jax.ShapeDtypeStruct((rows, D), bf16),
            jax.ShapeDtypeStruct((8, D), f32),
        ],
        compiler_params=params_of(13),
        cost_estimate=cost(8 * rows * D * D, 24 * rows * D),
        name="feed_back",
    )(piece_a, piece_b, w_up, w_down, gate)


def group_kernel(turn_ref, left_n, left_f, right_n, right_f, keep_ref, send_ref, all_ref):
    i = pl.program_id(0)
    value = dot32(left_n[...], right_n[...], ((0,), (0,)))
    value = (value + dot32(left_f[...], right_f[...], ((0,), (0,)))).astype(bf16)
    per = value.shape[0] // PB
    for k in range(per):
        all_ref[turn_ref[WIDE + i * per + k]] = value[PB * k : PB * (k + 1)]

    @pl.when(i == pl.num_programs(0) - 1)
    def _():
        near = keep_ref.shape[0]
        keep_ref[...] = all_ref[:near]
        send_ref[...] = all_ref[near:]


def group_grads(turns, left, right, near):
    rows = left[0].shape[0]
    wide = D // 2
    tile = pl.BlockSpec((rows, wide), lambda i, *_: (0, i))
    full = whole_block((rows, D))
    shapes = [(near, PB, D), (WIDE - near, PB, D)]
    return pl.pallas_call(
        group_kernel,
        grid_spec=pltpu.PrefetchScalarGridSpec(
            num_scalar_prefetch=1,
            grid=(2,),
            in_specs=[tile] * 2 + [full] * 2,
            out_specs=[whole_block(shape) for shape in shapes],
            scratch_shapes=[pltpu.VMEM((WIDE, PB, D), bf16)],
        ),
        out_shape=[jax.ShapeDtypeStruct(shape, bf16) for shape in shapes],
        compiler_params=params_of(12),
        cost_estimate=cost(4 * rows * D * D, 12 * rows * D),
    )(turns, *left, *right)


def dx_kernel(dkv_ref, w_ref, *refs, with_q):
    keep_ref, send_ref = refs[-2:]
    i = pl.program_id(0)
    part = dot32(dkv_ref[...], w_ref[...], ((1,), (1,)))
    if with_q:

        @pl.when(i >= pl.num_programs(0) - 4)
        def _():
            more = part + dot32(refs[0][...], refs[1][...], ((1,), (1,)))
            split_store(i, more.astype(bf16), keep_ref, send_ref)

        @pl.when(i < pl.num_programs(0) - 4)
        def _():
            split_store(i, part.astype(bf16), keep_ref, send_ref)

    else:
        split_store(i, part.astype(bf16), keep_ref, send_ref)


def dx_part(d_kv, w_kv, steps, tokens, d_query, w_q):
    rows = tokens // 4
    count = len(steps)
    with_q = steps[-1] == 0
    half = pl.BlockSpec((rows, D), lambda i: (i // 2, 0))
    shape = jax.ShapeDtypeStruct((count * tokens // 2, D), bf16)
    cols = w_kv.shape[1]

    def chunk_row(i):
        step = steps[-1]
        for n in range(count - 1):
            step = jnp.where(i // 4 == n, steps[n], step)
        return 4 * step + i % 4, 0

    args = [d_kv, w_kv]
    specs = [pl.BlockSpec((rows, cols), chunk_row), whole_block(w_kv.shape)]
    if with_q:
        args += [d_query, w_q]
        specs += [
            pl.BlockSpec((rows, w_q.shape[1]), lambda i: (i % 4, 0)),
            whole_block(w_q.shape),
        ]
    return pl.pallas_call(
        functools.partial(dx_kernel, with_q=with_q),
        grid=(4 * count,),
        in_specs=specs,
        out_specs=[half, half],
        out_shape=[shape, shape],
        compiler_params=params_of(7),
        cost_estimate=cost(2 * count * tokens * cols * D, 2 * count * tokens * (cols + D)),
    )(*args)


def late_kernel(
    turn_ref, x_ref, dkv_ref, dq_ref, att_ref, db_ref, s1_ref, s2_ref, sa_ref, bn_ref, bf_ref, top_ref,
    keep_ref, send_ref, acc_kv, acc_q, acc_o, turn_kv, turn_q, inner_ref, vec_ref, all_ref,
    *, cols, steps_q, heads, owners
):
    i = pl.program_id(0)

    @pl.when(i == 0)
    def _():
        acc_kv[...] = jnp.zeros(acc_kv.shape, f32)
        acc_q[...] = jnp.zeros(acc_q.shape, f32)
        acc_o[...] = jnp.zeros(acc_o.shape, f32)

    x = x_ref[...]
    acc_kv[...] += dot32(dkv_ref[...], x, ((0,), (0,)))

    @pl.when(i < steps_q)
    def _():
        acc_q[...] += dot32(dq_ref[...], x, ((0,), (0,)))
        acc_o[...] += dot32(att_ref[...], db_ref[...], ((0,), (0,)))

    @pl.when(i == pl.num_programs(0) - 1)
    def _():
        turn_kv[...] = acc_kv[...].T.astype(bf16)
        turn_q[...] = acc_q[...].T.astype(bf16)
        pad = acc_o.shape[0] - cols
        for k in range(D // PB):
            for c in range(3):
                unit = 3 * k + c
                rows = slice(PB * k, PB * (k + 1))
                piece = turn_q[rows, :cols] if c == 0 else turn_kv[rows, cols * (c - 1) : cols * c]
                all_ref[
                    turn_ref[WIDE + unit // 4], :PB, cols * (unit % 4) : cols * (unit % 4 + 1)
                ] = piece
        for k in range(cols // PB):
            all_ref[turn_ref[WIDE + 3 * cols // PB + k], :PB, :] = acc_o[
                pad + PB * k : pad + PB * (k + 1), :
            ].astype(bf16)
        inner_ref[0:1, :cols] = sa_ref[0:1, :cols]
        inner_ref[0:1, cols : 2 * cols] = sa_ref[1:2, pad : pad + cols]
        inner_ref[0:1, 2 * cols :] = bn_ref[0:1, :] + bf_ref[0:1, :]
        outer_cols = D // owners
        inner_cols = inner_ref.shape[1] // owners
        lane = lax.broadcasted_iota(jnp.int32, (1, D), 1)
        slots = jnp.zeros((1, D), f32)
        base = turn_ref[3 * WIDE] * 3 * heads
        for h in range(heads):
            left = top_ref[h : h + 1, :1]
            for part in range(3):
                piece = left.astype(bf16).astype(f32)
                slots = jnp.where(lane == base + part * heads + h, piece, slots)
                left = left - piece
        vec_ref[...] = jnp.zeros(vec_ref.shape, f32)
        vec_ref[7:8, :] = slots
        outer_rows = [(s1_ref, 2), (s2_ref, 2), (s1_ref, 0), (s1_ref, 1), (s2_ref, 0), (s2_ref, 1)]
        for k in range(owners):
            for n, (ref, row) in enumerate(outer_rows):
                vec_ref[n : n + 1, :outer_cols] = ref[
                    row : row + 1, outer_cols * k : outer_cols * (k + 1)
                ]
            vec_ref[6:7, :inner_cols] = inner_ref[0:1, inner_cols * k : inner_cols * (k + 1)]
            all_ref[turn_ref[WIDE + k], PB:, :] = vec_ref[...].astype(bf16)
        near = keep_ref.shape[0]
        keep_ref[...] = all_ref[:near]
        send_ref[...] = all_ref[near:]


def late_grads(turns, in_all, d_kv, d_query, att, d_branch, s1, s2, sa, bn, bf, tops, cols, heads, near):
    tokens, wide = d_query.shape
    tile = min(512, tokens)
    steps_q = tokens // tile
    owners = WIDE
    under = 16

    def rows_of(width, last):
        return pl.BlockSpec((tile, width), lambda i, *_: (jnp.minimum(i, last), 0))

    steps = in_all.shape[0] // tile
    small = [s1, s2, sa, bn, bf, tops]
    return pl.pallas_call(
        functools.partial(late_kernel, cols=cols, steps_q=steps_q, heads=heads, owners=owners),
        grid_spec=pltpu.PrefetchScalarGridSpec(
            num_scalar_prefetch=1,
            grid=(steps,),
            in_specs=[
                rows_of(D, steps - 1),
                rows_of(2 * cols, steps - 1),
                rows_of(wide, steps_q - 1),
                rows_of(wide, steps_q - 1),
                rows_of(D, steps_q - 1),
            ]
            + [whole_block(v.shape) for v in small],
            out_specs=[
                whole_block((near, PB + under, D)),
                whole_block((owners - near, PB + under, D)),
            ],
            scratch_shapes=[
                pltpu.VMEM((2 * cols, D), f32),
                pltpu.VMEM((wide, D), f32),
                pltpu.VMEM((wide, D), f32),
                pltpu.VMEM((D, 2 * cols), bf16),
                pltpu.VMEM((D, wide), bf16),
                pltpu.VMEM((1, 2 * cols + D), f32),
                pltpu.VMEM((under, D), f32),
                pltpu.VMEM((owners, PB + under, D), bf16),
            ],
        ),
        out_shape=[
            jax.ShapeDtypeStruct((near, PB + under, D), bf16),
            jax.ShapeDtypeStruct((owners - near, PB + under, D), bf16),
        ],
        compiler_params=params_of(20),
        cost_estimate=cost(2 * in_all.shape[0] * D * 2 * cols, 2 * in_all.shape[0] * (D + 2 * cols)),
        name="late_grads",
    )(turns, in_all, d_kv, d_query, att, d_branch, *small)


def head_masks(wide, heads, first):
    lane = lax.broadcasted_iota(jnp.int32, (BLOCK, wide), 1) // HEAD
    return [lane == h + first for h in range(heads)]


def spread(block, masks):
    zero = jnp.zeros_like(block)
    return jnp.concatenate([jnp.where(mask, block, zero) for mask in masks], axis=0)


def fold(stacked, masks):
    total = None
    for h, mask in enumerate(masks):
        part = jnp.where(mask, stacked[BLOCK * h : BLOCK * (h + 1)], 0.0)
        total = part if total is None else total + part
    return total


def listed_rows(addr_ref, kv_ref, i):
    return jnp.concatenate(
        [
            kv_ref[pl.ds(pl.multiple_of(addr_ref[i * LIST + e] * BLOCK, BLOCK), BLOCK), :]
            for e in range(LIST)
        ],
        axis=0,
    )


def fwd_kernel(
    addr_ref, valid_ref, query_ref, q_ref, kv_src, att_ref, p_ref, top_ref, kv_ref, sem, *, heads, group
):
    i = pl.program_id(0)
    wide = q_ref.shape[1]
    start = kv_ref.shape[1] - wide

    @pl.when(i == 0)
    def _():
        load = copy_in(kv_src, kv_ref, sem)
        top_ref[...] = jnp.full(top_ref.shape, neg_large, f32)
        load.wait()

    scale = jnp.asarray(HEAD ** (-0.5), bf16)
    q_masks = head_masks(wide, heads, 0)
    v_masks = head_masks(wide, heads, (heads * HEAD - start) // HEAD)
    lane = lax.broadcasted_iota(jnp.int32, (1, LIST * BLOCK), 1)
    for u in range(group):
        block = i * group + u
        mine = slice(u * BLOCK, (u + 1) * BLOCK)
        q_all = spread(q_ref[mine] * scale, q_masks)
        listed = listed_rows(addr_ref, kv_ref, block)
        scores = dot32(q_all, listed[:, :wide], ((1,), (1,)))
        limit = jnp.zeros((1, LIST * BLOCK), jnp.int32)
        for e in range(LIST):
            limit = jnp.where(lane // BLOCK == e, valid_ref[block * LIST + e], limit)
        scores = jnp.where(lane % BLOCK < limit, scores, neg_large)
        row_top = jnp.max(scores, axis=1, keepdims=True)
        shifted = jnp.exp(scores - row_top)
        probs = shifted * (1.0 / jnp.sum(shifted, axis=1, keepdims=True))
        probs_low = probs.astype(bf16)
        p_ref[u] = probs_low
        out = dot32(probs_low, listed[:, start:])
        att_ref[mine] = fold(out, v_masks).astype(bf16)
        row = lax.broadcasted_iota(jnp.int32, row_top.shape, 0) % BLOCK
        seen = jnp.where(row < query_ref[block], row_top, neg_large)
        for h in range(heads):
            best = jnp.max(seen[BLOCK * h : BLOCK * (h + 1)], axis=0, keepdims=True)
            top_ref[h : h + 1, :] = jnp.maximum(top_ref[h : h + 1, :], best)


def attention_forward(queries, kv_all, addr, valid, query_valid, heads, group=2):
    tokens, wide = queries.shape
    blocks = tokens // BLOCK
    rows = heads * BLOCK
    cols = LIST * BLOCK
    return pl.pallas_call(
        functools.partial(fwd_kernel, heads=heads, group=group),
        grid_spec=pltpu.PrefetchScalarGridSpec(
            num_scalar_prefetch=3,
            grid=(blocks // group,),
            in_specs=[pl.BlockSpec((group * BLOCK, wide), lambda i, *_: (i, 0)), in_place()],
            out_specs=[
                pl.BlockSpec((group * BLOCK, wide), lambda i, *_: (i, 0)),
                pl.BlockSpec((group, rows, cols), lambda i, *_: (i, 0, 0)),
                whole_block((8, 128)),
            ],
            scratch_shapes=[pltpu.VMEM(kv_all.shape, bf16), pltpu.SemaphoreType.DMA],
        ),
        out_shape=(
            jax.ShapeDtypeStruct((tokens, wide), bf16),
            jax.ShapeDtypeStruct((blocks, rows, cols), bf16),
            jax.ShapeDtypeStruct((8, 128), f32),
        ),
        compiler_params=params_of(11),
        cost_estimate=cost(
            4 * blocks * rows * cols * wide,
            2 * (kv_all.size + 2 * queries.size + blocks * rows * cols),
            blocks * rows * cols,
        ),
        name="attention_forward",
    )(addr, valid, query_valid, queries, kv_all)


def bwd_kernel(addr_ref, q_ref, p_ref, w_ref, kv_src, *refs, heads, group):
    pieces = refs[:4]
    dq_ref, dkv_ref, sums_ref, db_ref, kv_ref, acc_ref, sem, piece_sem = refs[4:]
    i = pl.program_id(0)
    wide = q_ref.shape[1]
    start = kv_ref.shape[1] - wide

    @pl.when(i == 0)
    def _():
        rows = pieces[0].shape[0]
        loads = [
            copy_in(ref, db_ref.at[pl.ds(r * rows, rows)], piece_sem.at[r])
            for r, ref in enumerate(pieces)
        ]
        loads.append(copy_in(kv_src, kv_ref, sem))
        acc_ref[...] = jnp.zeros(acc_ref.shape, f32)
        sums_ref[...] = jnp.zeros(sums_ref.shape, f32)
        for load in loads:
            load.wait()

    scale = jnp.asarray(HEAD ** (-0.5), bf16)
    q_masks = head_masks(wide, heads, 0)
    v_masks = head_masks(wide, heads, (heads * HEAD - start) // HEAD)
    span = group * BLOCK
    d_branch = db_ref[pl.ds(pl.multiple_of(i * span, span), span), :]
    d_out = dot32(d_branch, w_ref[...], ((1,), (1,))).astype(bf16)
    for u in range(group):
        block = i * group + u
        mine = slice(u * BLOCK, (u + 1) * BLOCK)
        q_all = spread(q_ref[mine] * scale, q_masks)
        do_all = spread(d_out[mine], v_masks)
        listed = listed_rows(addr_ref, kv_ref, block)
        probs_low = p_ref[u]
        probs = probs_low.astype(f32)
        d_probs = dot32(do_all, listed[:, start:], ((1,), (1,)))
        delta = jnp.sum(probs * d_probs, axis=1, keepdims=True)
        d_scores = (probs * (d_probs - delta)).astype(bf16)
        d_query = (fold(dot32(d_scores, listed[:, :wide]), q_masks) * HEAD ** (-0.5)).astype(bf16)
        dq_ref[mine] = d_query
        sums_ref[0:1, :] += column_sum(d_query.astype(f32))
        d_key = dot32(d_scores, q_all, ((0,), (0,)))
        d_value = dot32(probs_low, do_all, ((0,), (0,)))
        sums_ref[1:2, :] += column_sum(d_value)
        for e in range(LIST):
            rows = pl.ds(pl.multiple_of(addr_ref[block * LIST + e] * BLOCK, BLOCK), BLOCK)
            part = slice(BLOCK * e, BLOCK * (e + 1))
            acc_ref[rows, :start] += d_key[part, :start]
            acc_ref[rows, start:wide] += d_key[part, start:] + d_value[part, : wide - start]
            acc_ref[rows, wide:] += d_value[part, wide - start :]

    @pl.when(i == pl.num_programs(0) - 1)
    def _():
        dkv_ref[...] = acc_ref[...].astype(bf16)


def attention_backward(queries, pieces, w_out, probs, kv_all, addr, heads, group=2):
    tokens, wide = queries.shape
    blocks = tokens // BLOCK
    rows = heads * BLOCK
    cols = LIST * BLOCK
    return pl.pallas_call(
        functools.partial(bwd_kernel, heads=heads, group=group),
        grid_spec=pltpu.PrefetchScalarGridSpec(
            num_scalar_prefetch=1,
            grid=(blocks // group,),
            in_specs=[
                pl.BlockSpec((group * BLOCK, wide), lambda i, *_: (i, 0)),
                pl.BlockSpec((group, rows, cols), lambda i, *_: (i, 0, 0)),
                whole_block(w_out.shape),
            ]
            + [in_place()] * 5,
            out_specs=[
                pl.BlockSpec((group * BLOCK, wide), lambda i, *_: (i, 0)),
                whole_block(kv_all.shape, single=True),
                whole_block((8, wide)),
                whole_block((tokens, D), single=True),
            ],
            scratch_shapes=[
                pltpu.VMEM(kv_all.shape, bf16),
                pltpu.VMEM(kv_all.shape, f32),
                pltpu.SemaphoreType.DMA,
                pltpu.SemaphoreType.DMA((4,)),
            ],
        ),
        out_shape=(
            jax.ShapeDtypeStruct((tokens, wide), bf16),
            jax.ShapeDtypeStruct(kv_all.shape, bf16),
            jax.ShapeDtypeStruct((8, wide), f32),
            jax.ShapeDtypeStruct((tokens, D), bf16),
        ),
        compiler_params=params_of(24),
        cost_estimate=cost(
            8 * blocks * rows * cols * wide,
            2 * (2 * kv_all.size + 3 * queries.size + blocks * rows * cols),
        ),
        name="attention_backward",
    )(addr, queries, probs, w_out, kv_all, *pieces)


def two_parts(values):
    high = values.astype(bf16)
    return high, (values - high.astype(f32)).astype(bf16)


def shampoo_kernel(turn_ref, *refs, width, groups, heads):
    g_refs = refs[: 3 if groups else 1]
    tail_ref, mb_ref, ls_ref, rs_ref, lr_ref, rr_ref = refs[len(g_refs) : len(g_refs) + 6]
    bg_ref, ln_ref, rn_ref, nb_ref, max_ref, g_ref = refs[len(g_refs) + 6 :]
    i = pl.program_id(0)
    if groups:
        for n in range(3):

            @pl.when(i == n)
            def _():
                g_ref[...] = g_refs[n][...]
    else:
        g_ref[...] = g_refs[0][...]
    slots = tail_ref[0:8, :128]
    lanes = slots.shape[1]
    slots = slots + pltpu.roll(slots, lanes - heads, 1) + pltpu.roll(slots, lanes - 2 * heads, 1)
    lane = lax.broadcasted_iota(jnp.int32, slots.shape, 1)
    row = lax.broadcasted_iota(jnp.int32, slots.shape, 0)
    largest = jnp.zeros(slots.shape, f32)
    scales = []
    for h in range(heads):
        chosen = (row == 7) & (lane % (3 * heads) == h) & (lane < 3 * heads * WIDE)
        best = jnp.max(jnp.where(chosen, slots, neg_large), axis=1, keepdims=True)
        best = jnp.max(best, axis=0, keepdims=True)
        largest = jnp.where(lane == h, best, largest)
        scales.append(jnp.sqrt(tau_clip / jnp.maximum(best, tau_clip)))
    max_ref[...] = largest
    per_row = 3 * heads * HEAD // PB
    column = lax.broadcasted_iota(jnp.int32, (1, PB), 1)
    for j in range(width):
        cut = slice(PB * j, PB * (j + 1))
        grad = g_ref[:, cut]
        bg_ref[j] = grad.astype(f32)
        ln_ref[j] = 0.5 * ls_ref[j] + 0.5 * dot32(grad, grad, ((1,), (1,)))
        rn_ref[j] = 0.5 * rs_ref[j] + 0.5 * dot32(grad, grad, ((0,), (0,)))
        left_hi, left_lo = two_parts(lr_ref[j])
        applied_hi, applied_lo = two_parts(dot32(left_hi, grad) + dot32(left_lo, grad))
        right_hi, right_lo = two_parts(rr_ref[j])
        step_val = (
            dot32(applied_hi, right_hi) + dot32(applied_hi, right_lo) + dot32(applied_lo, right_hi)
        )
        index = (turn_ref[3 * WIDE] * pl.num_programs(0) + i) * width + j
        head_of = (lax.rem(index, per_row) * PB + column) // HEAD
        factor = jnp.ones((1, PB), f32)
        for h in range(heads):
            hit = (head_of == h) | (head_of == heads + h)
            factor = jnp.where(hit & (index < D // PB * per_row), scales[h], factor)
        nb_ref[j] = (mb_ref[j] - rate_matrix * step_val) * factor


def shampoo(turns, grads, groups, tail, master, left_s, right_s, left_r, right_r, heads):
    count = master.shape[0]
    width = WIDE if groups else 1
    block = pl.BlockSpec((width, PB, PB), lambda i, *_: (i, 0, 0))
    shape = jax.ShapeDtypeStruct((count, PB, PB), f32)
    if groups:
        specs = [whole_block(part.shape) for part in grads]
    else:
        specs = [pl.BlockSpec((PB, PB), lambda i, *_: (i, 0))]
    return pl.pallas_call(
        functools.partial(shampoo_kernel, width=width, groups=groups, heads=heads),
        grid_spec=pltpu.PrefetchScalarGridSpec(
            num_scalar_prefetch=1,
            grid=(count // width,),
            in_specs=specs + [whole_block(tail.shape)] + [block] * 5,
            out_specs=[block] * 4 + [whole_block((8, 128))],
            scratch_shapes=[pltpu.VMEM((PB, PB * width), bf16)],
        ),
        out_shape=[shape] * 4 + [jax.ShapeDtypeStruct((8, 128), f32)],
        compiler_params=params_of(16),
        cost_estimate=cost(16 * count * PB**3, 40 * count * PB * PB),
        name="shampoo",
    )(turns, *grads, tail, master, left_s, right_s, left_r, right_r)


def gather_quarters(own):
    side = swap(own, 1)
    across = swap(own, 2)
    return own, side, across, swap(across, 1)


def cross_sum(keep_far, send_far):
    mine = keep_far.astype(f32) + swap(send_far, 1).astype(f32)
    return swap(mine.astype(bf16), 2)


def slot_pairs(slot):
    return [(d, (3 * d + slot) % WIDE) for d in range(WIDE)]


def spread_group(held):
    count = lax.axis_size("ctx")
    near = jnp.stack([held] + [shift_ctx(held, step) for step in range(1, count)], axis=0)
    far = [shift_shard(near, u) for u in range(1, lax.axis_size("shard"))]
    return near, far[0] if len(far) == 1 else jnp.concatenate(far, axis=0)


def reduce_group(near, far):
    count = lax.axis_size("ctx")
    back = [
        shift_shard(far[count * (u - 1) : count * u], u)
        for u in range(1, lax.axis_size("shard"))
    ]
    halves = []
    for step in range(count):
        value = near[step].astype(f32)
        for part in back:
            value = value + part[step].astype(f32)
        halves.append(value)
    return halves[0], [shift_ctx(halves[step].astype(bf16), step) for step in near_first(count)]


def total_of(first, others, *wait):
    if wait:
        others = lax.optimization_barrier(tuple(others) + wait)[: len(others)]
    for other in others:
        first = first + other.astype(f32)
    return first


def per_device(
    inputs,
    lengths,
    global_blocks,
    random_blocks,
    master_blocks,
    outer_vectors,
    inner_biases,
    left_stats,
    right_stats,
    left_roots,
    right_roots,
    cotangent,
):
    tensor_count = lax.axis_size("tp")
    owner_count = lax.axis_size(OWN)
    ctx_count = lax.axis_size("ctx")
    shard_count = lax.axis_size("shard")
    heads_here = HEADS // tensor_count
    cols = heads_here * HEAD
    wide = 256
    pad = wide - cols
    tokens = inputs.shape[1]
    quarter = tokens // 4
    rows_blocks = tokens // BLOCK
    blocks_here = master_blocks.shape[0]
    packed = owner_count == WIDE and blocks_here == 3 * WIDE
    me = lax.axis_index("tp")
    z = lax.axis_index("ctx")
    y = lax.axis_index("shard")
    owner = lax.axis_index(OWN)
    ids = jnp.stack([me, y, z, owner]).astype(jnp.int32)
    addr, valid, query_valid, turns = index_tables(
        ids,
        lengths,
        global_blocks,
        random_blocks.reshape(rows_blocks, 3),
        rows_blocks,
        ctx_count,
        shard_count,
    )
    inner_row = inner_biases[0:1]
    q_bias = jnp.pad(inner_row[:, :cols], ((0, 0), (0, pad)))
    kv_bias = jnp.pad(inner_row[:, cols : 2 * cols], ((0, 0), (cols, 0)))
    up_bias = inner_row[:, 2 * cols :]
    flat_in = inputs.reshape(tokens, D)
    own_in = pick_quarter(ids, flat_in)

    if packed:
        own_packed = after(pack_rows(master_blocks), turns, up_bias, q_bias, kv_bias)
        held = [
            owner_move(own_packed[PB * slot : PB * (slot + 1)], slot_pairs(slot))
            for slot in range(3)
        ]
        held_first, held_rest = sort_held(turns, held)
        first_near, first_far = spread_group(held_first)
        rest_near, rest_far = spread_group(held_rest)
    else:
        weights = pack_rows(lax.all_gather(master_blocks.astype(bf16), OWN, axis=0, tiled=True))
        weights = weights.reshape(3, WIDE, PB, D)
        first_near, first_far = weights[0, : WIDE // 2], weights[0, WIDE // 2 :]
        rest = jnp.concatenate([weights[1], weights[2]], axis=1)
        rest_near, rest_far = rest[: WIDE // 2], rest[WIDE // 2 :]
        order = jnp.arange(WIDE, dtype=jnp.int32)
        turns = jnp.concatenate([order, order, order, turns[3 * WIDE :]])
    w_q, w_kv, w_out = unpack_first(turns, first_near, first_far, cols, wide)

    in_all, kv_all, queries = project_chunk(
        ids, [flat_in], 0, ctx_count, w_kv, kv_bias, w_q, q_bias, None
    )
    moved = []
    for n, step in enumerate(near_first(ctx_count)):
        source = own_in if n < 2 else after(own_in, moved[n - 2])
        moved.append(shift_ctx(source, step))
        pieces = gather_quarters(moved[n])
        in_all, kv_all = project_chunk(
            ids, pieces, step, ctx_count, w_kv, kv_bias, None, None, (in_all, kv_all)
        )

    att, probs, tops = attention_forward(queries, kv_all, addr, valid, query_valid, heads_here)
    keep, send = out_project(att, w_out)
    sent = swap(send, 1)
    got = swap((keep[quarter:].astype(f32) + sent[quarter:].astype(f32)).astype(bf16), 2)
    w_up, w_down = assemble(turns, rest_near, rest_far)
    hidden, x_first, x_own = first_norm(ids, flat_in, keep, sent, got, outer_vectors)
    x_own, x_side, x_across, x_diag = gather_quarters(x_own)
    x_n, gate_n, act_n, keep_n, send_n = feed_forward(x_own, x_side, w_up, w_down, up_bias)
    x_f, gate_f, act_f, keep_f, send_f = feed_forward(
        x_across, x_diag, w_up, w_down, up_bias
    )
    out_own, d_mixed, d_own, sums2 = second_norm(
        turns,
        x_first,
        keep_n,
        swap(send_n, 1),
        cross_sum(keep_f, send_f),
        cotangent.reshape(tokens, D),
        outer_vectors,
    )

    near = ctx_count if packed else WIDE // 2
    d_own, d_side, d_across, d_diag = gather_quarters(d_own)
    d_n, dg_n, keep_n, send_n, up_n = feed_back(d_own, d_side, w_up, w_down, gate_n)
    d_f, dg_f, keep_f, send_f, up_f = feed_back(d_across, d_diag, w_up, w_down, gate_f)
    d_hidden, b_own, sums1 = first_back(
        hidden, d_mixed, keep_n, swap(send_n, 1), cross_sum(keep_f, send_f), outer_vectors
    )
    b_pieces = gather_quarters(b_own)
    g_down = group_grads(turns, (act_n, act_f), (d_n, d_f), near)
    g_up = group_grads(turns, (x_n, x_f), (dg_n, dg_f), near)
    if packed:
        down_own = reduce_group(*g_down)
        up_own = reduce_group(*g_up)
    out_quarters = gather_quarters(after(out_own, b_pieces[3]))
    d_query, d_kv, sums_a, d_branch = attention_backward(
        queries, b_pieces, w_out, probs, kv_all, addr, heads_here
    )

    total = d_hidden
    order = near_first(ctx_count)[::-1] + [0]
    half = len(order) // 2
    d_kv_late = d_kv
    for steps in (order[:half], order[half:]):
        keep, send = dx_part(d_kv, w_kv, steps, tokens, d_query, w_q)
        sent = swap(send, 1)
        keep = keep.reshape(len(steps), 2, quarter, D)
        sent = sent.reshape(len(steps), 2, quarter, D)
        across = (keep[:, 1].astype(f32) + sent[:, 1].astype(f32)).astype(bf16)
        across = swap(across, 2)
        for c, step in enumerate(steps):
            mine = keep[c, 0].astype(f32) + sent[c, 0].astype(f32) + across[c].astype(f32)
            if step:
                mine = shift_ctx(mine.astype(bf16), ctx_count - step).astype(f32)
            total = total + mine
    grad_quarters = gather_quarters(total.astype(bf16))

    near_rows, far_rows = late_grads(
        turns,
        in_all,
        d_kv_late,
        d_query,
        att,
        d_branch,
        sums1,
        sums2,
        sums_a,
        up_n,
        up_f,
        tops,
        cols,
        heads_here,
        near,
    )
    outer_cols = D // owner_count
    inner_cols = inner_biases.shape[1] // owner_count
    if packed:
        down_own = total_of(*down_own, near_rows).astype(bf16)
        up_own = total_of(*up_own, near_rows).astype(bf16)
        late_own = total_of(*reduce_group(near_rows, far_rows))
        dealt = deal_rows(turns, late_own, up_own, down_own)
        tail = late_own[PB:]
        outer_own = tail[:6, :outer_cols]
        inner_own = tail[6:7, :inner_cols]
        grads = [
            owner_move(dealt[slot], [(holder, d) for d, holder in slot_pairs(slot)])
            for slot in range(3)
        ]
        groups = 3
    else:
        rows_of = jnp.concatenate([near_rows, far_rows], axis=0)[:, :PB]
        whole = jnp.concatenate([rows_of, *g_up, *g_down], axis=0).reshape(-1, D)
        blocks = whole.reshape(-1, PB, WIDE, PB).transpose(0, 2, 1, 3).reshape(-1, PB, PB)
        own_grads = lax.psum_scatter(blocks, OWN, scatter_dimension=0, tiled=True)
        grads, groups = [own_grads.reshape(blocks_here * PB, PB)], 0
        outer_part = jnp.stack([sums1[2], sums2[2], sums1[0], sums1[1], sums2[0], sums2[1]], axis=0)
        inner_part = jnp.concatenate([sums_a[0, :cols], sums_a[1, pad:], up_n[0] + up_f[0]])
        outer_own = lax.psum_scatter(outer_part, OWN, scatter_dimension=1, tiled=True)
        inner_own = lax.psum_scatter(inner_part[None, :], OWN, scatter_dimension=1, tiled=True)
        largest = lax.pmax(tops[:heads_here, 0], OWN)
        slots = jnp.tile(jnp.concatenate([largest, jnp.zeros((2 * heads_here,), f32)]), WIDE)
        tail = jnp.zeros((16, D), f32).at[7, : slots.shape[0]].set(slots)
    outer_own = outer_own + swap(outer_own, 1)
    outer_own = outer_own + swap(outer_own, 2)

    block_sum, left_new, right_new, new_blocks, largest = shampoo(
        turns,
        grads,
        groups,
        tail,
        master_blocks,
        left_stats,
        right_stats,
        left_roots,
        right_roots,
        heads_here,
    )
    maxima = largest[0, :heads_here]
    own_outer = lax.dynamic_slice_in_dim(outer_vectors, owner * outer_cols, outer_cols, 1)
    new_outer = own_outer - rate_vector * outer_own
    own_inner = lax.dynamic_slice_in_dim(inner_biases, owner * inner_cols, inner_cols, 1)
    head_of = (owner * inner_cols + jnp.arange(inner_cols, dtype=jnp.int32)) // HEAD
    factor = jnp.ones((inner_cols,), f32)
    for h in range(heads_here):
        scale = jnp.sqrt(tau_clip / jnp.maximum(largest[0, h], tau_clip))
        factor = jnp.where(head_of == h, scale, factor)
    new_inner = (own_inner - rate_vector * inner_own) * factor[None, :]

    return (
        place_quarters(ids, out_quarters).reshape(inputs.shape),
        place_quarters(ids, grad_quarters).reshape(inputs.shape),
        block_sum,
        outer_own,
        inner_own,
        maxima,
        left_new,
        right_new,
        new_blocks,
        new_outer,
        new_inner,
    )


def solution(mesh):
    return jax.shard_map(
        per_device,
        mesh=mesh,
        in_specs=(
            P("shard", "ctx", None),
            P("shard"),
            P("shard", None),
            P("shard", "ctx", None),
            P(("shard", "ctx", "tp"), None, None),
            P(),
            P("tp", None),
            P(("shard", "ctx", "tp"), None, None),
            P(("shard", "ctx", "tp"), None, None),
            P(("shard", "ctx", "tp"), None, None),
            P(("shard", "ctx", "tp"), None, None),
            P("shard", "ctx", None),
        ),
        out_specs=(
            P("shard", "ctx", None),
            P("shard", "ctx", None),
            P(("shard", "ctx", "tp"), None, None),
            P(None, ("shard", "ctx")),
            P("tp", ("shard", "ctx")),
            P("tp"),
            P(("shard", "ctx", "tp"), None, None),
            P(("shard", "ctx", "tp"), None, None),
            P(("shard", "ctx", "tp"), None, None),
            P(None, ("shard", "ctx")),
            P("tp", ("shard", "ctx")),
        ),
        check_vma=False,
    )
```

```python
import functools

import jax
import jax.numpy as jnp
from jax import lax
from jax.experimental import pallas as pl
from jax.experimental.pallas import tpu as pltpu
from jax.sharding import PartitionSpec as P


D = 768
HEADS = 12
HEAD = 64
BLOCK = 64
SEQ = 4096
PB = 96
LIST = 8
WIDE = 8

eps_norm = 1e-06
tau_clip = 9.0
rate_matrix = 0.3
rate_vector = 0.001
neg_large = -1e30
GELU = 0.7978845608028654
ANY = pl.ANY
bf16 = jnp.bfloat16
f32 = jnp.float32
SHARD, CTX, TP = "shard", "ctx", "tp"
OWN = (SHARD, CTX)


def params_of(mib, **more):
    return pltpu.CompilerParams(vmem_limit_bytes=mib << 20, **more)


def in_place():
    return pl.BlockSpec(memory_space=ANY)


def direct():
    return pl.BlockSpec(memory_space=pltpu.VMEM)


def scalars():
    return pl.BlockSpec(memory_space=pltpu.SMEM)


def whole_block(shape, single=False):
    zeros = (0,) * len(shape)
    mode = dict(pipeline_mode=pl.Buffered(1)) if single else {}
    return pl.BlockSpec(shape, lambda *_: zeros, **mode)


def cost(flops, moved, exps=0):
    return pl.CostEstimate(flops=flops, bytes_accessed=moved, transcendentals=exps)


def dot32(left, right, dims=((1,), (0,))):
    return lax.dot_general(left, right, (dims, ((), ())), preferred_element_type=f32)


def normalized(values):
    centred = values - jnp.mean(values, axis=-1, keepdims=True)
    factor = lax.rsqrt(jnp.mean(centred * centred, axis=-1, keepdims=True) + eps_norm)
    return centred * factor, factor


def norm_back(grad, gain, unit, factor):
    scaled = grad * gain
    mean_grad = jnp.mean(scaled, axis=-1, keepdims=True)
    mean_unit = jnp.mean(scaled * unit, axis=-1, keepdims=True)
    return factor * (scaled - mean_grad - unit * mean_unit)


def column_sum(values):
    return jnp.sum(values, axis=0, keepdims=True)


def gelu_parts(gate):
    inner = GELU * (gate + 0.044715 * gate * gate * gate)
    return inner, jnp.tanh(inner)


def copy_in(source, target, sem):
    copy = pltpu.make_async_copy(source, target, sem)
    copy.start()
    return copy


def swap(rows, mask):
    count = lax.axis_size(TP)
    return lax.ppermute(rows, TP, [(i, i ^ mask) for i in range(count)])


def shift_ctx(rows, step):
    count = lax.axis_size(CTX)
    return lax.ppermute(rows, CTX, [(i, (i + step) % count) for i in range(count)])


def forward_two(from_left, from_right):
    right = lax.ppermute(from_left, CTX, [(1, 2), (2, 3)])
    left = lax.ppermute(from_right, CTX, [(1, 0), (2, 1)])
    return right + left


def back_two(rows):
    right = lax.ppermute(rows, CTX, [(0, 1), (1, 2)])
    left = lax.ppermute(rows, CTX, [(2, 1), (3, 2)])
    return right, left


def shift_shard(rows, step):
    count = lax.axis_size(SHARD)
    return lax.ppermute(rows, SHARD, [(i, (i + step) % count) for i in range(count)])


def owner_move(rows, pairs):
    return lax.ppermute(rows, OWN, pairs)


def after(value, *others):
    return lax.optimization_barrier((value,) + others)[0]


def near_first(count):
    return sorted(range(1, count), key=lambda step: min(step, count - step))


def pack_kernel(blocks_ref, out_ref):
    for j in range(WIDE):
        out_ref[:, PB * j : PB * (j + 1)] = blocks_ref[j].astype(bf16)


def pack_rows(blocks):
    rows = blocks.shape[0] // WIDE
    return pl.pallas_call(
        pack_kernel,
        grid=(rows,),
        in_specs=[pl.BlockSpec((WIDE, PB, PB), lambda i: (i, 0, 0))],
        out_specs=pl.BlockSpec((PB, PB * WIDE), lambda i: (i, 0)),
        out_shape=jax.ShapeDtypeStruct((rows * PB, PB * WIDE), bf16),
        compiler_params=params_of(3),
        name="pack",
    )(blocks)


def unpack_kernel(turn_ref, near_ref, far_ref, q_ref, kv_ref, out_ref, all_ref, *, cols):
    half = near_ref.shape[0]
    all_ref[:half] = near_ref[...]
    all_ref[half:] = far_ref[...]
    q_ref[...] = jnp.zeros(q_ref.shape, bf16)
    for i in range(D // PB):
        for c in range(3):
            unit = 3 * i + c
            piece = all_ref[turn_ref[unit // 4], :, cols * (unit % 4) : cols * (unit % 4 + 1)]
            if c == 0:
                q_ref[PB * i : PB * (i + 1), :cols] = piece
            else:
                kv_ref[PB * i : PB * (i + 1), cols * (c - 1) : cols * c] = piece
    pad = out_ref.shape[0] - cols
    out_ref[:pad, :] = jnp.zeros((pad, D), bf16)
    for i in range(cols // PB):
        out_ref[pad + PB * i : pad + PB * (i + 1), :] = all_ref[turn_ref[3 * cols // PB + i]]


def unpack_first(turns, near, far, cols, wide):
    full = pl.BlockSpec(memory_space=pltpu.VMEM)
    return pl.pallas_call(
        functools.partial(unpack_kernel, cols=cols),
        in_specs=[pl.BlockSpec(memory_space=pltpu.SMEM), full, full],
        out_specs=[full, full, full],
        out_shape=(
            jax.ShapeDtypeStruct((D, wide), bf16),
            jax.ShapeDtypeStruct((D, 2 * cols), bf16),
            jax.ShapeDtypeStruct((wide, D), bf16),
        ),
        scratch_shapes=[pltpu.VMEM((near.shape[0] + far.shape[0], PB, D), bf16)],
        compiler_params=params_of(8),
        name="unpack",
    )(turns, near, far)


def tables_kernel(
    ids_ref, len_ref, glob_ref, rand_ref, addr_ref, valid_ref, query_ref, turn_ref, *, rows_blocks, ctx_count, shard_count
):
    me, y, z, owner = ids_ref[0], ids_ref[1], ids_ref[2], ids_ref[3]
    per = rows_blocks // 4
    length = len_ref[0]
    block_count = SEQ // BLOCK

    def body(i, carry):
        place = (lax.div(i, per) ^ me) * per + lax.rem(i, per)
        row = z * rows_blocks + place
        listed = [row - 1, row, row + 1, glob_ref[0, 0], glob_ref[0, 1]]
        listed += [rand_ref[place, n] for n in range(3)]
        for e, block in enumerate(listed):
            held = jnp.clip(block, 0, block_count - 1)
            valid = jnp.clip(length - block * BLOCK, 0, BLOCK)
            valid_ref[i * LIST + e] = jnp.where(held == block, valid, 0)
            chunk = lax.div(held, rows_blocks)
            local = held - chunk * rows_blocks
            step = lax.rem(z - chunk + ctx_count, ctx_count)
            part = lax.div(local, per)
            addr_ref[i * LIST + e] = (
                step * rows_blocks + (part ^ me) * per + (local - part * per)
            )
        query_ref[i] = jnp.clip(length - row * BLOCK, 0, BLOCK)
        return carry

    lax.fori_loop(0, rows_blocks, body, 0)
    for k in range(WIDE):
        ky, kz = k // ctx_count, k % ctx_count
        turn_ref[k] = lax.rem(y - ky + shard_count, shard_count) * ctx_count + lax.rem(
            z - kz + ctx_count, ctx_count
        )
        turn_ref[WIDE + k] = lax.rem(ky - y + shard_count, shard_count) * ctx_count + lax.rem(
            kz - z + ctx_count, ctx_count
        )
        turn_ref[2 * WIDE + k] = lax.rem(y - ky + shard_count, shard_count) * ctx_count + lax.rem(
            z - kz + ctx_count, ctx_count
        )
    turn_ref[3 * WIDE] = owner
    turn_ref[3 * WIDE + 1] = me
    tokens = rows_blocks * BLOCK
    quarter = tokens // 4
    turn_ref[3 * WIDE + 2] = jnp.clip(length - z * tokens - me * quarter, 0, quarter)


def index_tables(ids, lengths, global_blocks, random_blocks, rows_blocks, ctx_count, shard_count):
    smem = pl.BlockSpec(memory_space=pltpu.SMEM)
    shapes = [(rows_blocks * LIST,), (rows_blocks * LIST,), (rows_blocks,), (3 * WIDE + 8,)]
    return pl.pallas_call(
        functools.partial(
            tables_kernel, rows_blocks=rows_blocks, ctx_count=ctx_count, shard_count=shard_count
        ),
        in_specs=[smem] * 4,
        out_specs=[smem] * 4,
        out_shape=[jax.ShapeDtypeStruct(shape, jnp.int32) for shape in shapes],
        compiler_params=params_of(2),
        name="tables",
    )(ids, lengths, global_blocks, random_blocks)


def pick_kernel(ids_ref, x_ref, out_ref):
    out_ref[...] = x_ref[...]


def pick_quarter(ids, values):
    rows = values.shape[0] // 4
    return pl.pallas_call(
        pick_kernel,
        grid_spec=pltpu.PrefetchScalarGridSpec(
            num_scalar_prefetch=1,
            grid=(1,),
            in_specs=[pl.BlockSpec((rows, D), lambda i, ids: (ids[0], 0))],
            out_specs=pl.BlockSpec((rows, D), lambda i, ids: (0, 0)),
        ),
        out_shape=jax.ShapeDtypeStruct((rows, D), bf16),
        compiler_params=params_of(3),
        name="pick",
    )(ids, values)


def place_kernel(ids_ref, *refs):
    pieces, (out_ref, sem) = refs[:4], refs[4:]
    rows = pieces[0].shape[0]
    loads = []
    for r, piece in enumerate(pieces):
        start = pl.multiple_of((ids_ref[0] ^ r) * rows, rows)
        loads.append(copy_in(piece, out_ref.at[pl.ds(start, rows)], sem.at[r]))
    for load in loads:
        load.wait()


def place_quarters(ids, pieces):
    rows = pieces[0].shape[0]
    return pl.pallas_call(
        place_kernel,
        in_specs=[scalars()] + [in_place()] * 4,
        out_specs=in_place(),
        scratch_shapes=[pltpu.SemaphoreType.DMA((4,))],
        out_shape=jax.ShapeDtypeStruct((4 * rows, D), bf16),
        compiler_params=params_of(2),
    )(ids, *pieces)


def sort_kernel(turn_ref, a_ref, b_ref, c_ref, first_ref, rest_ref):
    for group in range(3):
        slot = lax.rem(WIDE * group + turn_ref[3 * WIDE], 3)
        value = jnp.where(slot == 0, a_ref[...], jnp.where(slot == 1, b_ref[...], c_ref[...]))
        if group == 0:
            first_ref[...] = value
        else:
            rest_ref[PB * (group - 1) : PB * group] = value


def sort_held(turns, held):
    return pl.pallas_call(
        sort_kernel,
        grid_spec=pltpu.PrefetchScalarGridSpec(
            num_scalar_prefetch=1,
            grid=(1,),
            in_specs=[whole_block((PB, D))] * 3,
            out_specs=[whole_block((PB, D)), whole_block((2 * PB, D))],
        ),
        out_shape=[
            jax.ShapeDtypeStruct((PB, D), bf16),
            jax.ShapeDtypeStruct((2 * PB, D), bf16),
        ],
        compiler_params=params_of(4),
        name="sort",
    )(turns, *held)


def deal_kernel(turn_ref, first_ref, up_ref, down_ref, a_ref, b_ref, c_ref):
    groups = (first_ref[:PB].astype(bf16), up_ref[...].astype(bf16), down_ref[...].astype(bf16))
    for slot, out_ref in enumerate((a_ref, b_ref, c_ref)):
        target = lax.rem(3 * (turn_ref[3 * WIDE] + WIDE - slot), WIDE)
        group = lax.div(3 * target + slot, WIDE)
        out_ref[...] = jnp.where(group == 0, groups[0], jnp.where(group == 1, groups[1], groups[2]))


def deal_rows(turns, first, up, down):
    one = whole_block((PB, D))
    return pl.pallas_call(
        deal_kernel,
        grid_spec=pltpu.PrefetchScalarGridSpec(
            num_scalar_prefetch=1,
            grid=(1,),
            in_specs=[whole_block(first.shape), one, one],
            out_specs=[one] * 3,
        ),
        out_shape=[jax.ShapeDtypeStruct((PB, D), bf16)] * 3,
        compiler_params=params_of(6),
        name="dealt",
    )(turns, first, up, down)


def project_kernel(ids_ref, *refs, step, with_q, chained):
    pieces = refs[: 1 if with_q else 4]
    rest = list(refs[len(pieces) :])
    wkv_ref, bkv_ref = rest[:2]
    rest = rest[2:]
    if with_q:
        wq_ref, bq_ref = rest[:2]
        rest = rest[2:]
    if chained:
        rest = rest[2:]
    in_all, kv_all = rest[:2]
    tokens = pieces[0].shape[0] * len(pieces)
    rows = tokens // 4
    for r in range(4):
        if with_q:
            x = pieces[0][pl.ds(pl.multiple_of((ids_ref[0] ^ r) * rows, rows), rows), :]
        else:
            x = pieces[r][...]
        mine = slice(step * tokens + r * rows, step * tokens + (r + 1) * rows)
        in_all[mine, :] = x
        kv_all[mine, :] = (dot32(x, wkv_ref[...]) + bkv_ref[...]).astype(bf16)
        if with_q:
            rest[2][r * rows : (r + 1) * rows, :] = (dot32(x, wq_ref[...]) + bq_ref[...]).astype(bf16)


def project_chunk(ids, pieces, step, count, w_kv, b_kv, w_q, b_q, carried):
    width = pieces[0].shape[1]
    tokens = pieces[0].shape[0] * len(pieces)
    kv_cols = w_kv.shape[1]
    with_q = w_q is not None
    chained = carried is not None
    args = list(pieces) + [w_kv, b_kv]
    if with_q:
        args += [w_q, b_q]
    aliases = {}
    if chained:
        aliases = {len(args) + 1: 0, len(args) + 2: 1}
        args += list(carried)
    shapes = [
        jax.ShapeDtypeStruct((count * tokens, width), bf16),
        jax.ShapeDtypeStruct((count * tokens, kv_cols), bf16),
    ]
    if with_q:
        shapes.append(jax.ShapeDtypeStruct((tokens, w_q.shape[1]), bf16))
    return pl.pallas_call(
        functools.partial(project_kernel, step=step, with_q=with_q, chained=chained),
        in_specs=[scalars()] + [direct()] * len(args),
        out_specs=[direct()] * len(shapes),
        out_shape=shapes,
        input_output_aliases=aliases,
        compiler_params=params_of(8),
        cost_estimate=cost(2 * tokens * width * kv_cols, 4 * tokens * (width + kv_cols)),
    )(ids, *args)


def split_store(r, value, keep_ref, send_ref):
    @pl.when(r % 2 == 0)
    def _():
        keep_ref[...] = value

    @pl.when(r % 2 == 1)
    def _():
        send_ref[...] = value


def out_kernel(att_ref, w_ref, keep_ref, send_ref):
    split_store(
        pl.program_id(0), dot32(att_ref[...], w_ref[...]).astype(bf16), keep_ref, send_ref
    )


def out_project(att, w_out):
    tokens, wide = att.shape
    rows = tokens // 4
    half = pl.BlockSpec((rows, D), lambda r: (r // 2, 0))
    shape = jax.ShapeDtypeStruct((tokens // 2, D), bf16)
    return pl.pallas_call(
        out_kernel,
        grid=(4,),
        in_specs=[pl.BlockSpec((rows, wide), lambda r: (r, 0)), whole_block(w_out.shape)],
        out_specs=[half, half],
        out_shape=[shape, shape],
        compiler_params=params_of(4),
        cost_estimate=cost(2 * tokens * wide * D, 2 * tokens * (wide + D)),
        name="oproj",
    )(att, w_out)


def summed(keep_ref, sent_ref, got_ref):
    return keep_ref[...].astype(f32) + sent_ref[...].astype(f32) + got_ref[...].astype(f32)


def first_norm_kernel(ids_ref, x_ref, keep_ref, sent_ref, got_ref, vec_ref, hid_ref, x1_ref, low_ref):
    hidden = x_ref[...].astype(f32) + (summed(keep_ref, sent_ref, got_ref) + vec_ref[0:1, :])
    hid_ref[...] = hidden
    unit, _ = normalized(hidden)
    x1 = unit * vec_ref[2:3, :] + vec_ref[3:4, :]
    x1_ref[...] = x1
    low_ref[...] = x1.astype(bf16)


def norm_tiles(rows):
    return 4 if rows % 64 == 0 else 1


def first_norm(ids, values, keep, sent, got, vectors):
    rows = got.shape[0]
    tiles = norm_tiles(rows)
    block = pl.BlockSpec((rows // tiles, D), lambda i, ids: (i, 0))
    mine = pl.BlockSpec((rows // tiles, D), lambda i, ids: (ids[0] * tiles + i, 0))
    return pl.pallas_call(
        first_norm_kernel,
        grid_spec=pltpu.PrefetchScalarGridSpec(
            num_scalar_prefetch=1,
            grid=(tiles,),
            in_specs=[mine] + [block] * 3 + [whole_block(vectors.shape)],
            out_specs=[block] * 3,
        ),
        out_shape=[
            jax.ShapeDtypeStruct((rows, D), f32),
            jax.ShapeDtypeStruct((rows, D), f32),
            jax.ShapeDtypeStruct((rows, D), bf16),
        ],
        compiler_params=params_of(5),
        cost_estimate=cost(20 * rows * D, 20 * rows * D),
        name="norm1",
    )(ids, values, keep, sent, got, vectors)


def second_norm_kernel(
    turn_ref, x1_ref, keep_ref, sent_ref, got_ref, cot_ref, vec_ref, out_ref, dmix_ref, low_ref, sums_ref
):
    i = pl.program_id(0)

    @pl.when(i == 0)
    def _():
        sums_ref[...] = jnp.zeros(sums_ref.shape, f32)

    mixed = x1_ref[...] + (summed(keep_ref, sent_ref, got_ref) + vec_ref[1:2, :])
    unit, factor = normalized(mixed)
    out_ref[...] = (unit * vec_ref[4:5, :] + vec_ref[5:6, :]).astype(bf16)
    row = lax.broadcasted_iota(jnp.int32, mixed.shape, 0) + i * mixed.shape[0]
    grad = jnp.where(row < turn_ref[3 * WIDE + 2], cot_ref[...].astype(f32), 0.0)
    d_mixed = norm_back(grad, vec_ref[4:5, :], unit, factor)
    dmix_ref[...] = d_mixed
    low = d_mixed.astype(bf16)
    low_ref[...] = low
    sums_ref[0:1, :] += column_sum(grad * unit)
    sums_ref[1:2, :] += column_sum(grad)
    sums_ref[2:3, :] += column_sum(low.astype(f32))


def second_norm(turns, x1, keep, sent, got, cot, vectors):
    rows = x1.shape[0]
    tiles = norm_tiles(rows)
    block = pl.BlockSpec((rows // tiles, D), lambda i, *_: (i, 0))
    mine = pl.BlockSpec((rows // tiles, D), lambda i, turns: (turns[3 * WIDE + 1] * tiles + i, 0))
    return pl.pallas_call(
        second_norm_kernel,
        grid_spec=pltpu.PrefetchScalarGridSpec(
            num_scalar_prefetch=1,
            grid=(tiles,),
            in_specs=[block] * 4 + [mine, whole_block(vectors.shape)],
            out_specs=[block] * 3 + [whole_block((8, D))],
        ),
        out_shape=[
            jax.ShapeDtypeStruct((rows, D), bf16),
            jax.ShapeDtypeStruct((rows, D), f32),
            jax.ShapeDtypeStruct((rows, D), bf16),
            jax.ShapeDtypeStruct((8, D), f32),
        ],
        compiler_params=params_of(6),
        cost_estimate=cost(40 * rows * D, 20 * rows * D),
        name="norm2",
    )(turns, x1, keep, sent, got, cot, vectors)


def first_back_kernel(
    hid_ref, dmix_ref, keep_ref, sent_ref, got_ref, vec_ref, dhid_ref, low_ref, sums_ref
):
    @pl.when(pl.program_id(0) == 0)
    def _():
        sums_ref[...] = jnp.zeros(sums_ref.shape, f32)

    grad = dmix_ref[...] + summed(keep_ref, sent_ref, got_ref)
    unit, factor = normalized(hid_ref[...])
    d_hidden = norm_back(grad, vec_ref[2:3, :], unit, factor)
    dhid_ref[...] = d_hidden
    low = d_hidden.astype(bf16)
    low_ref[...] = low
    sums_ref[0:1, :] += column_sum(grad * unit)
    sums_ref[1:2, :] += column_sum(grad)
    sums_ref[2:3, :] += column_sum(low.astype(f32))


def first_back(hidden, d_mixed, keep, sent, got, vectors):
    rows = hidden.shape[0]
    tiles = norm_tiles(rows)
    block = pl.BlockSpec((rows // tiles, D), lambda i: (i, 0))
    return pl.pallas_call(
        first_back_kernel,
        grid=(tiles,),
        in_specs=[block] * 5 + [whole_block(vectors.shape)],
        out_specs=[block] * 2 + [whole_block((8, D))],
        out_shape=[
            jax.ShapeDtypeStruct((rows, D), f32),
            jax.ShapeDtypeStruct((rows, D), bf16),
            jax.ShapeDtypeStruct((8, D), f32),
        ],
        compiler_params=params_of(6),
        cost_estimate=cost(40 * rows * D, 20 * rows * D),
        name="back1",
    )(hidden, d_mixed, keep, sent, got, vectors)


def assemble_kernel(turn_ref, near_ref, far_ref, up_ref, down_ref):
    near = near_ref.shape[0]
    for p in range(WIDE):
        start = pl.multiple_of(turn_ref[2 * WIDE + p] * PB, PB)
        for n, target in enumerate((up_ref, down_ref)):
            cut = slice(PB * n, PB * (n + 1))
            target[pl.ds(start, PB), :] = near_ref[p, cut] if p < near else far_ref[p - near, cut]


def assemble(turns, near, far):
    return pl.pallas_call(
        assemble_kernel,
        in_specs=[scalars(), direct(), direct()],
        out_specs=[direct()] * 2,
        out_shape=[jax.ShapeDtypeStruct((D, D), bf16)] * 2,
        compiler_params=params_of(6),
        cost_estimate=cost(0, 8 * D * D),
        name="assemble",
    )(turns, near, far)


def feed_kernel(
    xa_ref, xb_ref, wu_ref, wd_ref, b_ref, x_ref, gate_ref, act_ref, keep_ref, send_ref, sem
):
    i = pl.program_id(0)
    rows = xa_ref.shape[0]

    first = pltpu.make_async_copy(xa_ref, x_ref.at[pl.ds(0, rows)], sem.at[0])
    second = pltpu.make_async_copy(xb_ref, x_ref.at[pl.ds(rows, rows)], sem.at[1])

    @pl.when(i == 0)
    def _():
        first.start()
        second.start()
        first.wait()

    @pl.when(i == 1)
    def _():
        second.wait()

    mine = pl.ds(pl.multiple_of(i * rows, rows), rows)
    gate = dot32(x_ref[mine, :], wu_ref[...]) + b_ref[...]
    gate_ref[...] = gate
    _, tanh = gelu_parts(gate)
    act = (0.5 * gate * (1.0 + tanh)).astype(bf16)
    act_ref[...] = act

    split_store(i, dot32(act, wd_ref[...]).astype(bf16), keep_ref, send_ref)


def feed_forward(piece_a, piece_b, w_up, w_down, up_bias):
    rows = piece_a.shape[0]
    step = pl.BlockSpec((rows, D), lambda i, *_: (i, 0))
    one = whole_block((rows, D))
    return pl.pallas_call(
        feed_kernel,
        grid_spec=pltpu.PrefetchScalarGridSpec(num_scalar_prefetch=0, grid=(2,),
        in_specs=[in_place()] * 2 + [whole_block((D, D))] * 2 + [whole_block(up_bias.shape)],
        out_specs=[whole_block((2 * rows, D)), step, step, one, one],
        scratch_shapes=[pltpu.SemaphoreType.DMA((2,))],
        ),
        out_shape=[
            jax.ShapeDtypeStruct((2 * rows, D), bf16),
            jax.ShapeDtypeStruct((2 * rows, D), f32),
            jax.ShapeDtypeStruct((2 * rows, D), bf16),
            jax.ShapeDtypeStruct((rows, D), bf16),
            jax.ShapeDtypeStruct((rows, D), bf16),
        ],
        compiler_params=params_of(13),
        cost_estimate=cost(8 * rows * D * D, 24 * rows * D),
        name="feed",
    )(piece_a, piece_b, w_up, w_down, up_bias)


def feed_back_kernel(
    da_ref, db_ref, wu_ref, wd_ref, gate_ref, d_ref, dgate_ref, keep_ref, send_ref, sums_ref, sem
):
    i = pl.program_id(0)
    rows = da_ref.shape[0]

    first = pltpu.make_async_copy(da_ref, d_ref.at[pl.ds(0, rows)], sem.at[0])
    second = pltpu.make_async_copy(db_ref, d_ref.at[pl.ds(rows, rows)], sem.at[1])

    @pl.when(i == 0)
    def _():
        first.start()
        second.start()
        sums_ref[...] = jnp.zeros(sums_ref.shape, f32)
        first.wait()

    @pl.when(i == 1)
    def _():
        second.wait()

    mine = pl.ds(pl.multiple_of(i * rows, rows), rows)
    d_act = dot32(d_ref[mine, :], wd_ref[...], ((1,), (1,)))
    gate = gate_ref[...]
    _, tanh = gelu_parts(gate)
    slope = GELU * (1.0 + 3.0 * 0.044715 * gate * gate)
    d_gate = (d_act * (0.5 * (1.0 + tanh) + 0.5 * gate * (1.0 - tanh * tanh) * slope)).astype(bf16)
    dgate_ref[...] = d_gate
    sums_ref[0:1, :] += column_sum(d_gate.astype(f32))

    split_store(i, dot32(d_gate, wu_ref[...], ((1,), (1,))).astype(bf16), keep_ref, send_ref)


def feed_back(piece_a, piece_b, w_up, w_down, gate):
    rows = piece_a.shape[0]
    step = pl.BlockSpec((rows, D), lambda i, *_: (i, 0))
    one = whole_block((rows, D))
    return pl.pallas_call(
        feed_back_kernel,
        grid_spec=pltpu.PrefetchScalarGridSpec(num_scalar_prefetch=0, grid=(2,),
        in_specs=[in_place()] * 2 + [whole_block((D, D))] * 2 + [step],
        out_specs=[whole_block((2 * rows, D)), step, one, one, whole_block((8, D))],
        scratch_shapes=[pltpu.SemaphoreType.DMA((2,))],
        ),
        out_shape=[
            jax.ShapeDtypeStruct((2 * rows, D), bf16),
            jax.ShapeDtypeStruct((2 * rows, D), bf16),
            jax.ShapeDtypeStruct((rows, D), bf16),
            jax.ShapeDtypeStruct((rows, D), bf16),
            jax.ShapeDtypeStruct((8, D), f32),
        ],
        compiler_params=params_of(13),
        cost_estimate=cost(8 * rows * D * D, 24 * rows * D),
        name="fback",
    )(piece_a, piece_b, w_up, w_down, gate)


def group_kernel(turn_ref, left_n, left_f, right_n, right_f, keep_ref, send_ref, all_ref):
    i = pl.program_id(0)
    value = dot32(left_n[...], right_n[...], ((0,), (0,)))
    value = (value + dot32(left_f[...], right_f[...], ((0,), (0,)))).astype(bf16)
    per = value.shape[0] // PB
    for k in range(per):
        all_ref[turn_ref[WIDE + i * per + k]] = value[PB * k : PB * (k + 1)]

    @pl.when(i == pl.num_programs(0) - 1)
    def _():
        near = keep_ref.shape[0]
        keep_ref[...] = all_ref[:near]
        send_ref[...] = all_ref[near:]


def group_grads(turns, left, right, near):
    rows = left[0].shape[0]
    wide = D // 2
    tile = pl.BlockSpec((rows, wide), lambda i, *_: (0, i))
    full = whole_block((rows, D))
    shapes = [(near, PB, D), (WIDE - near, PB, D)]
    return pl.pallas_call(
        group_kernel,
        grid_spec=pltpu.PrefetchScalarGridSpec(
            num_scalar_prefetch=1,
            grid=(2,),
            in_specs=[tile] * 2 + [full] * 2,
            out_specs=[whole_block(shape) for shape in shapes],
            scratch_shapes=[pltpu.VMEM((WIDE, PB, D), bf16)],
        ),
        out_shape=[jax.ShapeDtypeStruct(shape, bf16) for shape in shapes],
        compiler_params=params_of(12),
        cost_estimate=cost(4 * rows * D * D, 12 * rows * D),
    )(turns, *left, *right)


def dx_kernel(dkv_ref, w_ref, *refs, with_q):
    keep_ref, send_ref = refs[-2:]
    i = pl.program_id(0)
    part = dot32(dkv_ref[...], w_ref[...], ((1,), (1,)))
    if with_q:

        part = part + dot32(refs[0][...], refs[1][...], ((1,), (1,)))
    split_store(i, part.astype(bf16), keep_ref, send_ref)


def dx_part(d_kv, w_kv, steps, tokens, d_query, w_q):
    rows = tokens // 4
    count = len(steps)
    with_q = steps[-1] == 0
    half = pl.BlockSpec((rows, D), lambda i: (i // 2, 0))
    shape = jax.ShapeDtypeStruct((count * tokens // 2, D), bf16)
    cols = w_kv.shape[1]

    def chunk_row(i):
        step = steps[-1]
        for n in range(count - 1):
            step = jnp.where(i // 4 == n, steps[n], step)
        return 4 * step + i % 4, 0

    args = [d_kv, w_kv]
    specs = [pl.BlockSpec((rows, cols), chunk_row), whole_block(w_kv.shape)]
    if with_q:
        args += [d_query, w_q]
        specs += [
            pl.BlockSpec((rows, w_q.shape[1]), lambda i: (i % 4, 0)),
            whole_block(w_q.shape),
        ]
    return pl.pallas_call(
        functools.partial(dx_kernel, with_q=with_q),
        grid=(4 * count,),
        in_specs=specs,
        out_specs=[half, half],
        out_shape=[shape, shape],
        compiler_params=params_of(7),
        cost_estimate=cost(2 * count * tokens * cols * D, 2 * count * tokens * (cols + D)),
    )(*args)


def late_kernel(
    turn_ref, x_ref, dkv_ref, dq_ref, att_ref, db_ref, s1_ref, s2_ref, sa_ref, bn_ref, bf_ref, top_ref,
    keep_ref, send_ref, acc_kv, acc_q, acc_o, turn_kv, turn_q, inner_ref, vec_ref, all_ref,
    *, cols, tile, heads, owners
):

    acc_kv[...] = jnp.zeros(acc_kv.shape, f32)

    def step(i, carry):
        mine = pl.ds(pl.multiple_of(i * tile, tile), tile)
        acc_kv[...] += dot32(dkv_ref[mine, :], x_ref[mine, :], ((0,), (0,)))
        return carry

    lax.fori_loop(0, x_ref.shape[0] // tile, step, 0)
    own = slice(0, dq_ref.shape[0])
    acc_q[...] = dot32(dq_ref[...], x_ref[own, :], ((0,), (0,)))
    acc_o[...] = dot32(att_ref[...], db_ref[...], ((0,), (0,)))
    turn_kv[...] = acc_kv[...].T.astype(bf16)
    turn_q[...] = acc_q[...].T.astype(bf16)
    pad = acc_o.shape[0] - cols
    for k in range(D // PB):
        for c in range(3):
            unit = 3 * k + c
            rows = slice(PB * k, PB * (k + 1))
            piece = turn_q[rows, :cols] if c == 0 else turn_kv[rows, cols * (c - 1) : cols * c]
            all_ref[
                turn_ref[WIDE + unit // 4], :PB, cols * (unit % 4) : cols * (unit % 4 + 1)
            ] = piece
    for k in range(cols // PB):
        all_ref[turn_ref[WIDE + 3 * cols // PB + k], :PB, :] = acc_o[
            pad + PB * k : pad + PB * (k + 1), :
        ].astype(bf16)
    inner_ref[0:1, :cols] = sa_ref[0:1, :cols]
    inner_ref[0:1, cols : 2 * cols] = sa_ref[1:2, pad : pad + cols]
    inner_ref[0:1, 2 * cols :] = bn_ref[0:1, :] + bf_ref[0:1, :]
    outer_cols = D // owners
    inner_cols = inner_ref.shape[1] // owners
    lane = lax.broadcasted_iota(jnp.int32, (1, D), 1)
    slots = jnp.zeros((1, D), f32)
    base = turn_ref[3 * WIDE] * 3 * heads
    for h in range(heads):
        left = top_ref[h : h + 1, :1]
        for part in range(3):
            piece = left.astype(bf16).astype(f32)
            slots = jnp.where(lane == base + part * heads + h, piece, slots)
            left = left - piece
    vec_ref[...] = jnp.zeros(vec_ref.shape, f32)
    vec_ref[7:8, :] = slots
    outer_rows = [(s1_ref, 2), (s2_ref, 2), (s1_ref, 0), (s1_ref, 1), (s2_ref, 0), (s2_ref, 1)]
    for k in range(owners):
        for n, (ref, row) in enumerate(outer_rows):
            vec_ref[n : n + 1, :outer_cols] = ref[
                row : row + 1, outer_cols * k : outer_cols * (k + 1)
            ]
        vec_ref[6:7, :inner_cols] = inner_ref[0:1, inner_cols * k : inner_cols * (k + 1)]
        all_ref[turn_ref[WIDE + k], PB:, :] = vec_ref[...].astype(bf16)
    near = keep_ref.shape[0]
    keep_ref[...] = all_ref[:near]
    send_ref[...] = all_ref[near:]


def late_grads(turns, in_all, d_kv, d_query, att, d_branch, s1, s2, sa, bn, bf, tops, cols, heads, near):
    _, wide = d_query.shape
    tile = 1024
    owners = WIDE
    under = 16

    small = [s1, s2, sa, bn, bf, tops]
    return pl.pallas_call(
        functools.partial(late_kernel, cols=cols, tile=tile, heads=heads, owners=owners),
        in_specs=[scalars()] + [direct()] * (5 + len(small)),
        out_specs=[direct()] * 2,
        scratch_shapes=[
            pltpu.VMEM((2 * cols, D), f32),
            pltpu.VMEM((wide, D), f32),
            pltpu.VMEM((wide, D), f32),
            pltpu.VMEM((D, 2 * cols), bf16),
            pltpu.VMEM((D, wide), bf16),
            pltpu.VMEM((1, 2 * cols + D), f32),
            pltpu.VMEM((under, D), f32),
            pltpu.VMEM((owners, PB + under, D), bf16),
        ],
        out_shape=[
            jax.ShapeDtypeStruct((near, PB + under, D), bf16),
            jax.ShapeDtypeStruct((owners - near, PB + under, D), bf16),
        ],
        compiler_params=params_of(20),
        cost_estimate=cost(2 * in_all.shape[0] * D * 2 * cols, 2 * in_all.shape[0] * (D + 2 * cols)),
        name="late",
    )(turns, in_all, d_kv, d_query, att, d_branch, *small)


def head_masks(wide, heads, first):
    lane = lax.broadcasted_iota(jnp.int32, (BLOCK, wide), 1) // HEAD
    return [lane == h + first for h in range(heads)]


def spread(block, masks):
    zero = jnp.zeros_like(block)
    return jnp.concatenate([jnp.where(mask, block, zero) for mask in masks], axis=0)


def fold(stacked, masks):
    total = None
    for h, mask in enumerate(masks):
        part = jnp.where(mask, stacked[BLOCK * h : BLOCK * (h + 1)], 0.0)
        total = part if total is None else total + part
    return total


def listed_rows(addr_ref, kv_ref, i):
    return jnp.concatenate(
        [
            kv_ref[pl.ds(pl.multiple_of(addr_ref[i * LIST + e] * BLOCK, BLOCK), BLOCK), :]
            for e in range(LIST)
        ],
        axis=0,
    )


def fwd_kernel(
    addr_ref, valid_ref, query_ref, q_ref, kv_ref, att_ref, p_ref, top_ref, *, heads, group
):
    wide = q_ref.shape[1]
    start = kv_ref.shape[1] - wide
    top_ref[...] = jnp.full(top_ref.shape, neg_large, f32)
    scale = jnp.asarray(HEAD ** (-0.5), bf16)
    q_masks = head_masks(wide, heads, 0)
    v_masks = head_masks(wide, heads, (heads * HEAD - start) // HEAD)
    lane = lax.broadcasted_iota(jnp.int32, (1, LIST * BLOCK), 1)

    def step(i, carry):
        for u in range(group):
            block = i * group + u
            mine = pl.ds(pl.multiple_of(block * BLOCK, BLOCK), BLOCK)
            q_all = spread(q_ref[mine, :] * scale, q_masks)
            listed = listed_rows(addr_ref, kv_ref, block)
            scores = dot32(q_all, listed[:, :wide], ((1,), (1,)))
            limit = jnp.zeros((1, LIST * BLOCK), jnp.int32)
            for e in range(LIST):
                limit = jnp.where(lane // BLOCK == e, valid_ref[block * LIST + e], limit)
            scores = jnp.where(lane % BLOCK < limit, scores, neg_large)
            row_top = jnp.max(scores, axis=1, keepdims=True)
            shifted = jnp.exp(scores - row_top)
            probs = shifted * (1.0 / jnp.sum(shifted, axis=1, keepdims=True))
            probs_low = probs.astype(bf16)
            p_ref[block] = probs_low
            out = dot32(probs_low, listed[:, start:])
            att_ref[mine, :] = fold(out, v_masks).astype(bf16)
            row = lax.broadcasted_iota(jnp.int32, row_top.shape, 0) % BLOCK
            seen = jnp.where(row < query_ref[block], row_top, neg_large)
            for h in range(heads):
                best = jnp.max(seen[BLOCK * h : BLOCK * (h + 1)], axis=0, keepdims=True)
                top_ref[h : h + 1, :] = jnp.maximum(top_ref[h : h + 1, :], best)
        return carry

    lax.fori_loop(0, q_ref.shape[0] // (group * BLOCK), step, 0)


def attention_forward(queries, kv_all, addr, valid, query_valid, heads, group=2):
    tokens, wide = queries.shape
    blocks = tokens // BLOCK
    rows = heads * BLOCK
    cols = LIST * BLOCK
    return pl.pallas_call(
        functools.partial(fwd_kernel, heads=heads, group=group),
        in_specs=[scalars()] * 3 + [direct()] * 2,
        out_specs=[direct()] * 3,
        out_shape=(
            jax.ShapeDtypeStruct((tokens, wide), bf16),
            jax.ShapeDtypeStruct((blocks, rows, cols), bf16),
            jax.ShapeDtypeStruct((8, 128), f32),
        ),
        compiler_params=params_of(11),
        cost_estimate=cost(
            4 * blocks * rows * cols * wide,
            2 * (kv_all.size + 2 * queries.size + blocks * rows * cols),
            blocks * rows * cols,
        ),
        name="afwd",
    )(addr, valid, query_valid, queries, kv_all)


def bwd_kernel(addr_ref, q_ref, p_ref, w_ref, kv_ref, *refs, heads, group):
    pieces = refs[:4]
    dq_ref, dkv_ref, sums_ref, db_ref, acc_ref = refs[4:]
    wide = q_ref.shape[1]
    start = kv_ref.shape[1] - wide
    rows = pieces[0].shape[0]
    for r, piece in enumerate(pieces):
        db_ref[r * rows : (r + 1) * rows, :] = piece[...]
    acc_ref[...] = jnp.zeros(acc_ref.shape, f32)
    sums_ref[...] = jnp.zeros(sums_ref.shape, f32)
    scale = jnp.asarray(HEAD ** (-0.5), bf16)
    q_masks = head_masks(wide, heads, 0)
    v_masks = head_masks(wide, heads, (heads * HEAD - start) // HEAD)

    def step(i, carry):
        span = group * BLOCK
        d_branch = db_ref[pl.ds(pl.multiple_of(i * span, span), span), :]
        d_out = dot32(d_branch, w_ref[...], ((1,), (1,))).astype(bf16)
        for u in range(group):
            block = i * group + u
            here = slice(u * BLOCK, (u + 1) * BLOCK)
            mine = pl.ds(pl.multiple_of(block * BLOCK, BLOCK), BLOCK)
            q_all = spread(q_ref[mine, :] * scale, q_masks)
            do_all = spread(d_out[here], v_masks)
            listed = listed_rows(addr_ref, kv_ref, block)
            probs_low = p_ref[block]
            probs = probs_low.astype(f32)
            d_probs = dot32(do_all, listed[:, start:], ((1,), (1,)))
            delta = jnp.sum(probs * d_probs, axis=1, keepdims=True)
            d_scores = (probs * (d_probs - delta)).astype(bf16)
            d_query = (fold(dot32(d_scores, listed[:, :wide]), q_masks) * HEAD ** (-0.5)).astype(bf16)
            dq_ref[mine, :] = d_query
            sums_ref[0:1, :] += column_sum(d_query.astype(f32))
            d_key = dot32(d_scores, q_all, ((0,), (0,)))
            d_value = dot32(probs_low, do_all, ((0,), (0,)))
            sums_ref[1:2, :] += column_sum(d_value)
            for e in range(LIST):
                rows = pl.ds(pl.multiple_of(addr_ref[block * LIST + e] * BLOCK, BLOCK), BLOCK)
                part = slice(BLOCK * e, BLOCK * (e + 1))
                acc_ref[rows, :start] += d_key[part, :start]
                acc_ref[rows, start:wide] += d_key[part, start:] + d_value[part, : wide - start]
                acc_ref[rows, wide:] += d_value[part, wide - start :]
        return carry

    lax.fori_loop(0, q_ref.shape[0] // (group * BLOCK), step, 0)
    dkv_ref[...] = acc_ref[...].astype(bf16)


def attention_backward(queries, pieces, w_out, probs, kv_all, addr, heads, group=2):
    tokens, wide = queries.shape
    blocks = tokens // BLOCK
    rows = heads * BLOCK
    cols = LIST * BLOCK
    return pl.pallas_call(
        functools.partial(bwd_kernel, heads=heads, group=group),
        in_specs=[scalars()] + [direct()] * 8,
        out_specs=[direct()] * 4,
        scratch_shapes=[pltpu.VMEM(kv_all.shape, f32)],
        out_shape=(
            jax.ShapeDtypeStruct((tokens, wide), bf16),
            jax.ShapeDtypeStruct(kv_all.shape, bf16),
            jax.ShapeDtypeStruct((8, wide), f32),
            jax.ShapeDtypeStruct((tokens, D), bf16),
        ),
        compiler_params=params_of(24),
        cost_estimate=cost(
            8 * blocks * rows * cols * wide,
            2 * (2 * kv_all.size + 3 * queries.size + blocks * rows * cols),
        ),
        name="abwd",
    )(addr, queries, probs, w_out, kv_all, *pieces)


def two_parts(values):
    high = values.astype(bf16)
    return high, (values - high.astype(f32)).astype(bf16)


def shampoo_kernel(turn_ref, *refs, width, groups, heads):
    g_refs = refs[: 3 if groups else 1]
    tail_ref, mb_ref, ls_ref, rs_ref, lr_ref, rr_ref = refs[len(g_refs) : len(g_refs) + 6]
    bg_ref, ln_ref, rn_ref, nb_ref, max_ref, g_ref = refs[len(g_refs) + 6 :]
    i = pl.program_id(0)
    if groups:
        for n in range(3):

            @pl.when(i == n)
            def _():
                g_ref[...] = g_refs[n][...]
    else:
        g_ref[...] = g_refs[0][...]
    slots = tail_ref[0:8, :128]
    lanes = slots.shape[1]
    slots = slots + pltpu.roll(slots, lanes - heads, 1) + pltpu.roll(slots, lanes - 2 * heads, 1)
    lane = lax.broadcasted_iota(jnp.int32, slots.shape, 1)
    row = lax.broadcasted_iota(jnp.int32, slots.shape, 0)
    largest = jnp.zeros(slots.shape, f32)
    scales = []
    for h in range(heads):
        chosen = (row == 7) & (lane % (3 * heads) == h) & (lane < 3 * heads * WIDE)
        best = jnp.max(jnp.where(chosen, slots, neg_large), axis=1, keepdims=True)
        best = jnp.max(best, axis=0, keepdims=True)
        largest = jnp.where(lane == h, best, largest)
        scales.append(jnp.sqrt(tau_clip / jnp.maximum(best, tau_clip)))
    max_ref[...] = largest
    per_row = 3 * heads * HEAD // PB
    column = lax.broadcasted_iota(jnp.int32, (1, PB), 1)
    for j in range(width):
        cut = slice(PB * j, PB * (j + 1))
        grad = g_ref[:, cut]
        bg_ref[j] = grad.astype(f32)
        ln_ref[j] = 0.5 * ls_ref[j] + 0.5 * dot32(grad, grad, ((1,), (1,)))
        rn_ref[j] = 0.5 * rs_ref[j] + 0.5 * dot32(grad, grad, ((0,), (0,)))
        left_hi, left_lo = two_parts(lr_ref[j])
        applied_hi, applied_lo = two_parts(dot32(left_hi, grad) + dot32(left_lo, grad))
        right_hi, right_lo = two_parts(rr_ref[j])
        step_val = (
            dot32(applied_hi, right_hi) + dot32(applied_hi, right_lo) + dot32(applied_lo, right_hi)
        )
        index = (turn_ref[3 * WIDE] * pl.num_programs(0) + i) * width + j
        head_of = (lax.rem(index, per_row) * PB + column) // HEAD
        factor = jnp.ones((1, PB), f32)
        for h in range(heads):
            hit = (head_of == h) | (head_of == heads + h)
            factor = jnp.where(hit & (index < D // PB * per_row), scales[h], factor)
        nb_ref[j] = (mb_ref[j] - rate_matrix * step_val) * factor


def shampoo(turns, grads, groups, tail, master, left_s, right_s, left_r, right_r, heads):
    count = master.shape[0]
    width = WIDE if groups else 1
    block = pl.BlockSpec((width, PB, PB), lambda i, *_: (i, 0, 0))
    shape = jax.ShapeDtypeStruct((count, PB, PB), f32)
    if groups:
        specs = [whole_block(part.shape) for part in grads]
    else:
        specs = [pl.BlockSpec((PB, PB), lambda i, *_: (i, 0))]
    return pl.pallas_call(
        functools.partial(shampoo_kernel, width=width, groups=groups, heads=heads),
        grid_spec=pltpu.PrefetchScalarGridSpec(
            num_scalar_prefetch=1,
            grid=(count // width,),
            in_specs=specs + [whole_block(tail.shape)] + [block] * 5,
            out_specs=[block] * 4 + [whole_block((8, 128))],
            scratch_shapes=[pltpu.VMEM((PB, PB * width), bf16)],
        ),
        out_shape=[shape] * 4 + [jax.ShapeDtypeStruct((8, 128), f32)],
        compiler_params=params_of(16),
        cost_estimate=cost(16 * count * PB**3, 40 * count * PB * PB),
        name="shampoo",
    )(turns, *grads, tail, master, left_s, right_s, left_r, right_r)


def gather_quarters(own):
    side = swap(own, 1)
    across = swap(own, 2)
    return own, side, across, swap(across, 1)


def cross_sum(keep_far, send_far):
    mine = keep_far.astype(f32) + swap(send_far, 1).astype(f32)
    return swap(mine.astype(bf16), 2)


def slot_pairs(slot):
    return [(d, (3 * d + slot) % WIDE) for d in range(WIDE)]


def spread_group(held, group):
    count = lax.axis_size(CTX)
    pieces = [held] + [None] * (count - 1)
    for step in near_first(count):
        if count == 4 and step == 2 and group:
            pieces[2] = forward_two(pieces[1], pieces[3])
        else:
            pieces[step] = shift_ctx(held, step)
    near = jnp.stack(pieces, axis=0)
    far = [shift_shard(near, u) for u in range(1, lax.axis_size(SHARD))]
    return near, far[0] if len(far) == 1 else jnp.concatenate(far, axis=0)


def reduce_group(near, far):
    count = lax.axis_size(CTX)
    back = [
        shift_shard(far[count * (u - 1) : count * u], u)
        for u in range(1, lax.axis_size(SHARD))
    ]
    halves = []
    for step in range(count):
        value = near[step].astype(f32)
        for part in back:
            value = value + part[step].astype(f32)
        halves.append(value)
    return halves[0], [shift_ctx(halves[step].astype(bf16), step) for step in near_first(count)]


def total_of(first, others, *wait):
    if wait:
        others = lax.optimization_barrier(tuple(others) + wait)[: len(others)]
    for other in others:
        first = first + other.astype(f32)
    return first


def per_device(
    inputs,
    lengths,
    global_blocks,
    random_blocks,
    master_blocks,
    outer_vectors,
    inner_biases,
    left_stats,
    right_stats,
    left_roots,
    right_roots,
    cotangent,
):
    tensor_count = lax.axis_size(TP)
    owner_count = lax.axis_size(OWN)
    ctx_count = lax.axis_size(CTX)
    shard_count = lax.axis_size(SHARD)
    heads_here = HEADS // tensor_count
    cols = heads_here * HEAD
    wide = 256
    pad = wide - cols
    tokens = inputs.shape[1]
    quarter = tokens // 4
    rows_blocks = tokens // BLOCK
    blocks_here = master_blocks.shape[0]
    packed = owner_count == WIDE and blocks_here == 3 * WIDE
    me = lax.axis_index(TP)
    z = lax.axis_index(CTX)
    y = lax.axis_index(SHARD)
    owner = lax.axis_index(OWN)
    ids = jnp.stack([me, y, z, owner]).astype(jnp.int32)
    addr, valid, query_valid, turns = index_tables(
        ids,
        lengths,
        global_blocks,
        random_blocks.reshape(rows_blocks, 3),
        rows_blocks,
        ctx_count,
        shard_count,
    )
    inner_row = inner_biases[0:1]
    q_bias = jnp.pad(inner_row[:, :cols], ((0, 0), (0, pad)))
    kv_bias = jnp.pad(inner_row[:, cols : 2 * cols], ((0, 0), (cols, 0)))
    up_bias = inner_row[:, 2 * cols :]
    flat_in = inputs.reshape(tokens, D)
    own_in = pick_quarter(ids, flat_in)

    if packed:
        own_packed = after(pack_rows(master_blocks), turns, up_bias, q_bias, kv_bias)
        held = [
            owner_move(own_packed[PB * slot : PB * (slot + 1)], slot_pairs(slot))
            for slot in range(3)
        ]
        held_first, held_rest = sort_held(turns, held)
        first_near, first_far = spread_group(held_first, 0)
        rest_near, rest_far = spread_group(held_rest, 1)
    else:
        weights = pack_rows(lax.all_gather(master_blocks.astype(bf16), OWN, axis=0, tiled=True))
        weights = weights.reshape(3, WIDE, PB, D)
        first_near, first_far = weights[0, : WIDE // 2], weights[0, WIDE // 2 :]
        rest = jnp.concatenate([weights[1], weights[2]], axis=1)
        rest_near, rest_far = rest[: WIDE // 2], rest[WIDE // 2 :]
        order = jnp.arange(WIDE, dtype=jnp.int32)
        turns = jnp.concatenate([order, order, order, turns[3 * WIDE :]])
    w_q, w_kv, w_out = unpack_first(turns, first_near, first_far, cols, wide)

    in_all, kv_all, queries = project_chunk(
        ids, [flat_in], 0, ctx_count, w_kv, kv_bias, w_q, q_bias, None
    )
    moved = []
    for n, step in enumerate(near_first(ctx_count)):
        if ctx_count == 4 and n == 2:
            moved.append(forward_two(moved[0], moved[1]))
        else:
            source = own_in if n < 2 else after(own_in, moved[n - 2])
            moved.append(shift_ctx(source, step))
        pieces = gather_quarters(moved[n])
        in_all, kv_all = project_chunk(
            ids, pieces, step, ctx_count, w_kv, kv_bias, None, None, (in_all, kv_all)
        )

    att, probs, tops = attention_forward(queries, kv_all, addr, valid, query_valid, heads_here)
    keep, send = out_project(att, w_out)
    sent = swap(send, 1)
    got = swap((keep[quarter:].astype(f32) + sent[quarter:].astype(f32)).astype(bf16), 2)
    w_up, w_down = assemble(turns, rest_near, rest_far)
    hidden, x_first, x_own = first_norm(ids, flat_in, keep, sent, got, outer_vectors)
    x_own, x_side, x_across, x_diag = gather_quarters(x_own)
    x_n, gate_n, act_n, keep_n, send_n = feed_forward(x_own, x_side, w_up, w_down, up_bias)
    x_f, gate_f, act_f, keep_f, send_f = feed_forward(
        x_across, x_diag, w_up, w_down, up_bias
    )
    out_own, d_mixed, d_own, sums2 = second_norm(
        turns,
        x_first,
        keep_n,
        swap(send_n, 1),
        cross_sum(keep_f, send_f),
        cotangent.reshape(tokens, D),
        outer_vectors,
    )

    near = ctx_count if packed else WIDE // 2
    d_own, d_side, d_across, d_diag = gather_quarters(d_own)
    d_n, dg_n, keep_n, send_n, up_n = feed_back(d_own, d_side, w_up, w_down, gate_n)
    d_f, dg_f, keep_f, send_f, up_f = feed_back(d_across, d_diag, w_up, w_down, gate_f)
    d_hidden, b_own, sums1 = first_back(
        hidden, d_mixed, keep_n, swap(send_n, 1), cross_sum(keep_f, send_f), outer_vectors
    )
    b_pieces = gather_quarters(b_own)
    g_down = group_grads(turns, (act_n, act_f), (d_n, d_f), near)
    g_up = group_grads(turns, (x_n, x_f), (dg_n, dg_f), near)
    if packed:
        down_own = reduce_group(*g_down)
        up_own = reduce_group(*g_up)
    out_quarters = gather_quarters(after(out_own, b_pieces[3]))
    d_query, d_kv, sums_a, d_branch = attention_backward(
        queries, b_pieces, w_out, probs, kv_all, addr, heads_here
    )

    total = d_hidden
    d_kv_late = d_kv
    extra = {}
    for step in near_first(ctx_count)[::-1] + [0]:
        keep, send = dx_part(d_kv, w_kv, [step], tokens, d_query, w_q)
        sent = swap(send, 1)
        across = (keep[quarter:].astype(f32) + sent[quarter:].astype(f32)).astype(bf16)
        across = swap(across, 2)
        mine = keep[:quarter].astype(f32) + sent[:quarter].astype(f32) + across.astype(f32)
        if step in extra:
            mine = mine + extra[step].astype(f32)
        if step == 2 and ctx_count == 4:
            extra[3], extra[1] = back_two(mine.astype(bf16))
            continue
        if step:
            mine = shift_ctx(mine.astype(bf16), ctx_count - step).astype(f32)
        total = total + mine
    grad_quarters = gather_quarters(total.astype(bf16))

    near_rows, far_rows = late_grads(
        turns,
        in_all,
        d_kv_late,
        d_query,
        att,
        d_branch,
        sums1,
        sums2,
        sums_a,
        up_n,
        up_f,
        tops,
        cols,
        heads_here,
        near,
    )
    outer_cols = D // owner_count
    inner_cols = inner_biases.shape[1] // owner_count
    if packed:
        down_own = total_of(*down_own, near_rows).astype(bf16)
        up_own = total_of(*up_own, near_rows).astype(bf16)
        late_own = total_of(*reduce_group(near_rows, far_rows))
        dealt = deal_rows(turns, late_own, up_own, down_own)
        tail = late_own[PB:]
        outer_own = tail[:6, :outer_cols]
        inner_own = tail[6:7, :inner_cols]
        grads = [
            owner_move(dealt[slot], [(holder, d) for d, holder in slot_pairs(slot)])
            for slot in range(3)
        ]
        groups = 3
    else:
        rows_of = jnp.concatenate([near_rows, far_rows], axis=0)[:, :PB]
        whole = jnp.concatenate([rows_of, *g_up, *g_down], axis=0).reshape(-1, D)
        blocks = whole.reshape(-1, PB, WIDE, PB).transpose(0, 2, 1, 3).reshape(-1, PB, PB)
        own_grads = lax.psum_scatter(blocks, OWN, scatter_dimension=0, tiled=True)
        grads, groups = [own_grads.reshape(blocks_here * PB, PB)], 0
        outer_part = jnp.stack([sums1[2], sums2[2], sums1[0], sums1[1], sums2[0], sums2[1]], axis=0)
        inner_part = jnp.concatenate([sums_a[0, :cols], sums_a[1, pad:], up_n[0] + up_f[0]])
        outer_own = lax.psum_scatter(outer_part, OWN, scatter_dimension=1, tiled=True)
        inner_own = lax.psum_scatter(inner_part[None, :], OWN, scatter_dimension=1, tiled=True)
        largest = lax.pmax(tops[:heads_here, 0], OWN)
        slots = jnp.tile(jnp.concatenate([largest, jnp.zeros((2 * heads_here,), f32)]), WIDE)
        tail = jnp.zeros((16, D), f32).at[7, : slots.shape[0]].set(slots)
    outer_own = outer_own + swap(outer_own, 1)
    outer_own = outer_own + swap(outer_own, 2)

    block_sum, left_new, right_new, new_blocks, largest = shampoo(
        turns,
        grads,
        groups,
        tail,
        master_blocks,
        left_stats,
        right_stats,
        left_roots,
        right_roots,
        heads_here,
    )
    maxima = largest[0, :heads_here]
    own_outer = lax.dynamic_slice_in_dim(outer_vectors, owner * outer_cols, outer_cols, 1)
    new_outer = own_outer - rate_vector * outer_own
    own_inner = lax.dynamic_slice_in_dim(inner_biases, owner * inner_cols, inner_cols, 1)
    head_of = (owner * inner_cols + jnp.arange(inner_cols, dtype=jnp.int32)) // HEAD
    factor = jnp.ones((inner_cols,), f32)
    for h in range(heads_here):
        scale = jnp.sqrt(tau_clip / jnp.maximum(largest[0, h], tau_clip))
        factor = jnp.where(head_of == h, scale, factor)
    new_inner = (own_inner - rate_vector * inner_own) * factor[None, :]

    return (
        place_quarters(ids, out_quarters).reshape(inputs.shape),
        place_quarters(ids, grad_quarters).reshape(inputs.shape),
        block_sum,
        outer_own,
        inner_own,
        maxima,
        left_new,
        right_new,
        new_blocks,
        new_outer,
        new_inner,
    )


def solution(mesh):
    return jax.shard_map(
        per_device,
        mesh=mesh,
        in_specs=(
            P(SHARD, CTX, None),
            P(SHARD),
            P(SHARD, None),
            P(SHARD, CTX, None),
            P((SHARD, CTX, TP), None, None),
            P(),
            P(TP, None),
            P((SHARD, CTX, TP), None, None),
            P((SHARD, CTX, TP), None, None),
            P((SHARD, CTX, TP), None, None),
            P((SHARD, CTX, TP), None, None),
            P(SHARD, CTX, None),
        ),
        out_specs=(
            P(SHARD, CTX, None),
            P(SHARD, CTX, None),
            P((SHARD, CTX, TP), None, None),
            P(None, (SHARD, CTX)),
            P(TP, (SHARD, CTX)),
            P(TP),
            P((SHARD, CTX, TP), None, None),
            P((SHARD, CTX, TP), None, None),
            P((SHARD, CTX, TP), None, None),
            P(None, (SHARD, CTX)),
            P(TP, (SHARD, CTX)),
        ),
        check_vma=False,
    )
```

```python
import functools

import jax
import jax.numpy as jnp
from jax import lax
from jax.experimental import pallas as pl
from jax.experimental.pallas import tpu as pltpu
from jax.sharding import PartitionSpec as P


D = 768
HEADS = 12
HEAD = 64
BLOCK = 64
SEQ = 4096
PB = 96
LIST = 8
WIDE = 8

eps_norm = 1e-06
tau_clip = 9.0
rate_matrix = 0.3
rate_vector = 0.001
neg_large = -1e30
GELU = 0.7978845608028654
ANY = pl.ANY
bf16 = jnp.bfloat16
f32 = jnp.float32
SHARD, CTX, TP = "shard", "ctx", "tp"
OWN = (SHARD, CTX)


def params_of(mib, **more):
    return pltpu.CompilerParams(vmem_limit_bytes=mib << 20, **more)


def in_place():
    return pl.BlockSpec(memory_space=ANY)


def direct():
    return pl.BlockSpec(memory_space=pltpu.VMEM)


def scalars():
    return pl.BlockSpec(memory_space=pltpu.SMEM)


def whole_block(shape, single=False):
    zeros = (0,) * len(shape)
    mode = dict(pipeline_mode=pl.Buffered(1)) if single else {}
    return pl.BlockSpec(shape, lambda *_: zeros, **mode)


def cost(flops, moved, exps=0):
    return pl.CostEstimate(flops=flops, bytes_accessed=moved, transcendentals=exps)


def dot32(left, right, dims=((1,), (0,))):
    return lax.dot_general(left, right, (dims, ((), ())), preferred_element_type=f32)


def normalized(values):
    centred = values - jnp.mean(values, axis=-1, keepdims=True)
    factor = lax.rsqrt(jnp.mean(centred * centred, axis=-1, keepdims=True) + eps_norm)
    return centred * factor, factor


def norm_back(grad, gain, unit, factor):
    scaled = grad * gain
    mean_grad = jnp.mean(scaled, axis=-1, keepdims=True)
    mean_unit = jnp.mean(scaled * unit, axis=-1, keepdims=True)
    return factor * (scaled - mean_grad - unit * mean_unit)


def column_sum(values):
    return jnp.sum(values, axis=0, keepdims=True)


def gelu_parts(gate):
    inner = GELU * (gate + 0.044715 * gate * gate * gate)
    return inner, jnp.tanh(inner)


def copy_in(source, target, sem):
    copy = pltpu.make_async_copy(source, target, sem)
    copy.start()
    return copy


def swap(rows, mask):
    count = lax.axis_size(TP)
    return lax.ppermute(rows, TP, [(i, i ^ mask) for i in range(count)])


def shift_ctx(rows, step):
    count = lax.axis_size(CTX)
    return lax.ppermute(rows, CTX, [(i, (i + step) % count) for i in range(count)])


def forward_two(from_left, from_right):
    right = lax.ppermute(from_left, CTX, [(1, 2), (2, 3)])
    left = lax.ppermute(from_right, CTX, [(1, 0), (2, 1)])
    return right + left


def back_two(rows):
    right = lax.ppermute(rows, CTX, [(0, 1), (1, 2)])
    left = lax.ppermute(rows, CTX, [(2, 1), (3, 2)])
    return right, left


def shift_shard(rows, step):
    count = lax.axis_size(SHARD)
    return lax.ppermute(rows, SHARD, [(i, (i + step) % count) for i in range(count)])


def owner_move(rows, pairs):
    return lax.ppermute(rows, OWN, pairs)


def after(value, *others):
    return lax.optimization_barrier((value,) + others)[0]


def near_first(count):
    return sorted(range(1, count), key=lambda step: min(step, count - step))


def pack_kernel(blocks_ref, out_ref):
    for j in range(WIDE):
        out_ref[:, PB * j : PB * (j + 1)] = blocks_ref[j].astype(bf16)


def pack_rows(blocks):
    rows = blocks.shape[0] // WIDE
    return pl.pallas_call(
        pack_kernel,
        grid=(rows,),
        in_specs=[pl.BlockSpec((WIDE, PB, PB), lambda i: (i, 0, 0))],
        out_specs=pl.BlockSpec((PB, PB * WIDE), lambda i: (i, 0)),
        out_shape=jax.ShapeDtypeStruct((rows * PB, PB * WIDE), bf16),
        compiler_params=params_of(3),
        name="pack",
    )(blocks)


def unpack_kernel(turn_ref, near_ref, far_ref, q_ref, kv_ref, out_ref, all_ref, *, cols):
    half = near_ref.shape[0]
    all_ref[:half] = near_ref[...]
    all_ref[half:] = far_ref[...]
    q_ref[...] = jnp.zeros(q_ref.shape, bf16)
    for i in range(D // PB):
        for c in range(3):
            unit = 3 * i + c
            piece = all_ref[turn_ref[unit // 4], :, cols * (unit % 4) : cols * (unit % 4 + 1)]
            if c == 0:
                q_ref[PB * i : PB * (i + 1), :cols] = piece
            else:
                kv_ref[PB * i : PB * (i + 1), cols * (c - 1) : cols * c] = piece
    pad = out_ref.shape[0] - cols
    out_ref[:pad, :] = jnp.zeros((pad, D), bf16)
    for i in range(cols // PB):
        out_ref[pad + PB * i : pad + PB * (i + 1), :] = all_ref[turn_ref[3 * cols // PB + i]]


def unpack_first(turns, near, far, cols, wide):
    full = pl.BlockSpec(memory_space=pltpu.VMEM)
    return pl.pallas_call(
        functools.partial(unpack_kernel, cols=cols),
        in_specs=[pl.BlockSpec(memory_space=pltpu.SMEM), full, full],
        out_specs=[full, full, full],
        out_shape=(
            jax.ShapeDtypeStruct((D, wide), bf16),
            jax.ShapeDtypeStruct((D, 2 * cols), bf16),
            jax.ShapeDtypeStruct((wide, D), bf16),
        ),
        scratch_shapes=[pltpu.VMEM((near.shape[0] + far.shape[0], PB, D), bf16)],
        compiler_params=params_of(8),
        name="unpack",
    )(turns, near, far)


def tables_kernel(
    ids_ref, len_ref, glob_ref, rand_ref, addr_ref, valid_ref, query_ref, turn_ref, *, rows_blocks, ctx_count, shard_count
):
    me, y, z, owner = ids_ref[0], ids_ref[1], ids_ref[2], ids_ref[3]
    per = rows_blocks // 4
    length = len_ref[0]
    block_count = SEQ // BLOCK

    def body(i, carry):
        place = (lax.div(i, per) ^ me) * per + lax.rem(i, per)
        row = z * rows_blocks + place
        listed = [row - 1, row, row + 1, glob_ref[0, 0], glob_ref[0, 1]]
        listed += [rand_ref[place, n] for n in range(3)]
        for e, block in enumerate(listed):
            held = jnp.clip(block, 0, block_count - 1)
            valid = jnp.clip(length - block * BLOCK, 0, BLOCK)
            valid_ref[i * LIST + e] = jnp.where(held == block, valid, 0)
            chunk = lax.div(held, rows_blocks)
            local = held - chunk * rows_blocks
            step = lax.rem(z - chunk + ctx_count, ctx_count)
            part = lax.div(local, per)
            addr_ref[i * LIST + e] = (
                step * rows_blocks + (part ^ me) * per + (local - part * per)
            )
        query_ref[i] = jnp.clip(length - row * BLOCK, 0, BLOCK)
        return carry

    lax.fori_loop(0, rows_blocks, body, 0)
    for k in range(WIDE):
        ky, kz = k // ctx_count, k % ctx_count
        turn_ref[k] = lax.rem(y - ky + shard_count, shard_count) * ctx_count + lax.rem(
            z - kz + ctx_count, ctx_count
        )
        turn_ref[WIDE + k] = lax.rem(ky - y + shard_count, shard_count) * ctx_count + lax.rem(
            kz - z + ctx_count, ctx_count
        )
        turn_ref[2 * WIDE + k] = lax.rem(y - ky + shard_count, shard_count) * ctx_count + lax.rem(
            z - kz + ctx_count, ctx_count
        )
    turn_ref[3 * WIDE] = owner
    turn_ref[3 * WIDE + 1] = me
    tokens = rows_blocks * BLOCK
    quarter = tokens // 4
    turn_ref[3 * WIDE + 2] = jnp.clip(length - z * tokens - me * quarter, 0, quarter)


def index_tables(ids, lengths, global_blocks, random_blocks, rows_blocks, ctx_count, shard_count):
    smem = pl.BlockSpec(memory_space=pltpu.SMEM)
    shapes = [(rows_blocks * LIST,), (rows_blocks * LIST,), (rows_blocks,), (3 * WIDE + 8,)]
    return pl.pallas_call(
        functools.partial(
            tables_kernel, rows_blocks=rows_blocks, ctx_count=ctx_count, shard_count=shard_count
        ),
        in_specs=[smem] * 4,
        out_specs=[smem] * 4,
        out_shape=[jax.ShapeDtypeStruct(shape, jnp.int32) for shape in shapes],
        compiler_params=params_of(2),
        name="tables",
    )(ids, lengths, global_blocks, random_blocks)


def pick_kernel(ids_ref, x_ref, out_ref):
    out_ref[...] = x_ref[...]


def pick_quarter(ids, values):
    rows = values.shape[0] // 4
    return pl.pallas_call(
        pick_kernel,
        grid_spec=pltpu.PrefetchScalarGridSpec(
            num_scalar_prefetch=1,
            grid=(1,),
            in_specs=[pl.BlockSpec((rows, D), lambda i, ids: (ids[0], 0))],
            out_specs=pl.BlockSpec((rows, D), lambda i, ids: (0, 0)),
        ),
        out_shape=jax.ShapeDtypeStruct((rows, D), bf16),
        compiler_params=params_of(3),
        name="pick",
    )(ids, values)


def place_kernel(ids_ref, *refs):
    pieces, (out_ref, sem) = refs[:4], refs[4:]
    rows = pieces[0].shape[0]
    loads = []
    for r, piece in enumerate(pieces):
        start = pl.multiple_of((ids_ref[0] ^ r) * rows, rows)
        loads.append(copy_in(piece, out_ref.at[pl.ds(start, rows)], sem.at[r]))
    for load in loads:
        load.wait()


def place_quarters(ids, pieces):
    rows = pieces[0].shape[0]
    return pl.pallas_call(
        place_kernel,
        in_specs=[scalars()] + [in_place()] * 4,
        out_specs=in_place(),
        scratch_shapes=[pltpu.SemaphoreType.DMA((4,))],
        out_shape=jax.ShapeDtypeStruct((4 * rows, D), bf16),
        compiler_params=params_of(2),
    )(ids, *pieces)


def sort_kernel(turn_ref, a_ref, b_ref, c_ref, first_ref, rest_ref):
    for group in range(3):
        slot = lax.rem(WIDE * group + turn_ref[3 * WIDE], 3)
        value = jnp.where(slot == 0, a_ref[...], jnp.where(slot == 1, b_ref[...], c_ref[...]))
        if group == 0:
            first_ref[...] = value
        else:
            rest_ref[PB * (group - 1) : PB * group] = value


def sort_held(turns, held):
    return pl.pallas_call(
        sort_kernel,
        grid_spec=pltpu.PrefetchScalarGridSpec(
            num_scalar_prefetch=1,
            grid=(1,),
            in_specs=[whole_block((PB, D))] * 3,
            out_specs=[whole_block((PB, D)), whole_block((2 * PB, D))],
        ),
        out_shape=[
            jax.ShapeDtypeStruct((PB, D), bf16),
            jax.ShapeDtypeStruct((2 * PB, D), bf16),
        ],
        compiler_params=params_of(4),
        name="sort",
    )(turns, *held)


def deal_kernel(turn_ref, *refs, parts, heads):
    outs = refs[sum(parts) :]
    groups = []
    for group in range(3):
        base = sum(parts[:group])
        total = refs[base][...]
        for part in refs[base + 1 : base + parts[group]]:
            total = total + part[...].astype(f32)
        groups.append(total)
    rows = [total[:PB].astype(bf16) for total in groups]
    for slot in range(3):
        target = lax.rem(3 * (turn_ref[3 * WIDE] + WIDE - slot), WIDE)
        group = lax.div(3 * target + slot, WIDE)
        outs[slot][...] = jnp.where(group == 0, rows[0], jnp.where(group == 1, rows[1], rows[2]))
    outs[3][...] = groups[0][PB:]
    slots = groups[0][PB : PB + 8, :128]
    lanes = slots.shape[1]
    slots = slots + pltpu.roll(slots, lanes - heads, 1) + pltpu.roll(slots, lanes - 2 * heads, 1)
    lane = lax.broadcasted_iota(jnp.int32, slots.shape, 1)
    row = lax.broadcasted_iota(jnp.int32, slots.shape, 0)
    largest = jnp.zeros(slots.shape, f32)
    for h in range(heads):
        chosen = (row == 7) & (lane % (3 * heads) == h) & (lane < 3 * heads * WIDE)
        best = jnp.max(jnp.where(chosen, slots, neg_large), axis=1, keepdims=True)
        largest = jnp.where(lane == h, jnp.max(best, axis=0, keepdims=True), largest)
    outs[4][...] = largest


def deal_rows(turns, first, up, down, heads):
    args = [*first, *up, *down]
    one = jax.ShapeDtypeStruct((PB, D), bf16)
    under = first[0].shape[0] - PB
    shapes = [one] * 3 + [
        jax.ShapeDtypeStruct((under, D), f32),
        jax.ShapeDtypeStruct((8, 128), f32),
    ]
    return pl.pallas_call(
        functools.partial(deal_kernel, parts=(len(first), len(up), len(down)), heads=heads),
        in_specs=[scalars()] + [direct()] * len(args),
        out_specs=[direct()] * 5,
        out_shape=shapes,
        compiler_params=params_of(8),
        name="dealt",
    )(turns, *args)


def project_kernel(ids_ref, *refs, step, with_q, chained):
    pieces = refs[: 1 if with_q else 4]
    rest = list(refs[len(pieces) :])
    wkv_ref, bkv_ref = rest[:2]
    rest = rest[2:]
    if with_q:
        wq_ref, bq_ref = rest[:2]
        rest = rest[2:]
    if chained:
        rest = rest[2:]
    in_all, kv_all = rest[:2]
    tokens = pieces[0].shape[0] * len(pieces)
    rows = tokens // 4
    for r in range(4):
        if with_q:
            x = pieces[0][pl.ds(pl.multiple_of((ids_ref[0] ^ r) * rows, rows), rows), :]
        else:
            x = pieces[r][...]
        mine = slice(step * tokens + r * rows, step * tokens + (r + 1) * rows)
        in_all[mine, :] = x
        kv_all[mine, :] = (dot32(x, wkv_ref[...]) + bkv_ref[...]).astype(bf16)
        if with_q:
            rest[2][r * rows : (r + 1) * rows, :] = (dot32(x, wq_ref[...]) + bq_ref[...]).astype(bf16)


def project_chunk(ids, pieces, step, count, w_kv, b_kv, w_q, b_q, carried):
    width = pieces[0].shape[1]
    tokens = pieces[0].shape[0] * len(pieces)
    kv_cols = w_kv.shape[1]
    with_q = w_q is not None
    chained = carried is not None
    args = list(pieces) + [w_kv, b_kv]
    if with_q:
        args += [w_q, b_q]
    aliases = {}
    if chained:
        aliases = {len(args) + 1: 0, len(args) + 2: 1}
        args += list(carried)
    shapes = [
        jax.ShapeDtypeStruct((count * tokens, width), bf16),
        jax.ShapeDtypeStruct((count * tokens, kv_cols), bf16),
    ]
    if with_q:
        shapes.append(jax.ShapeDtypeStruct((tokens, w_q.shape[1]), bf16))
    return pl.pallas_call(
        functools.partial(project_kernel, step=step, with_q=with_q, chained=chained),
        in_specs=[scalars()] + [direct()] * len(args),
        out_specs=[direct()] * len(shapes),
        out_shape=shapes,
        input_output_aliases=aliases,
        compiler_params=params_of(8),
        cost_estimate=cost(2 * tokens * width * kv_cols, 4 * tokens * (width + kv_cols)),
    )(ids, *args)


def split_store(r, value, keep_ref, send_ref):
    @pl.when(r % 2 == 0)
    def _():
        keep_ref[...] = value

    @pl.when(r % 2 == 1)
    def _():
        send_ref[...] = value


def out_kernel(att_ref, w_ref, keep_ref, send_ref):
    split_store(
        pl.program_id(0), dot32(att_ref[...], w_ref[...]).astype(bf16), keep_ref, send_ref
    )


def out_project(att, w_out):
    tokens, wide = att.shape
    rows = tokens // 4
    half = pl.BlockSpec((rows, D), lambda r: (r // 2, 0))
    shape = jax.ShapeDtypeStruct((tokens // 2, D), bf16)
    return pl.pallas_call(
        out_kernel,
        grid=(4,),
        in_specs=[pl.BlockSpec((rows, wide), lambda r: (r, 0)), whole_block(w_out.shape)],
        out_specs=[half, half],
        out_shape=[shape, shape],
        compiler_params=params_of(4),
        cost_estimate=cost(2 * tokens * wide * D, 2 * tokens * (wide + D)),
        name="oproj",
    )(att, w_out)


def summed(keep_ref, sent_ref, got_ref):
    return keep_ref[...].astype(f32) + sent_ref[...].astype(f32) + got_ref[...].astype(f32)


def first_norm_kernel(ids_ref, x_ref, keep_ref, sent_ref, got_ref, vec_ref, hid_ref, x1_ref, low_ref):
    hidden = x_ref[...].astype(f32) + (summed(keep_ref, sent_ref, got_ref) + vec_ref[0:1, :])
    hid_ref[...] = hidden
    unit, _ = normalized(hidden)
    x1 = unit * vec_ref[2:3, :] + vec_ref[3:4, :]
    x1_ref[...] = x1
    low_ref[...] = x1.astype(bf16)


def norm_tiles(rows):
    return 4 if rows % 64 == 0 else 1


def first_norm(ids, values, keep, sent, got, vectors):
    rows = got.shape[0]
    tiles = norm_tiles(rows)
    block = pl.BlockSpec((rows // tiles, D), lambda i, ids: (i, 0))
    mine = pl.BlockSpec((rows // tiles, D), lambda i, ids: (ids[0] * tiles + i, 0))
    return pl.pallas_call(
        first_norm_kernel,
        grid_spec=pltpu.PrefetchScalarGridSpec(
            num_scalar_prefetch=1,
            grid=(tiles,),
            in_specs=[mine] + [block] * 3 + [whole_block(vectors.shape)],
            out_specs=[block] * 3,
        ),
        out_shape=[
            jax.ShapeDtypeStruct((rows, D), f32),
            jax.ShapeDtypeStruct((rows, D), f32),
            jax.ShapeDtypeStruct((rows, D), bf16),
        ],
        compiler_params=params_of(5),
        cost_estimate=cost(20 * rows * D, 20 * rows * D),
        name="norm1",
    )(ids, values, keep, sent, got, vectors)


def second_norm_kernel(
    turn_ref, x1_ref, keep_ref, sent_ref, got_ref, cot_ref, vec_ref, out_ref, dmix_ref, low_ref, sums_ref
):
    i = pl.program_id(0)

    @pl.when(i == 0)
    def _():
        sums_ref[...] = jnp.zeros(sums_ref.shape, f32)

    mixed = x1_ref[...] + (summed(keep_ref, sent_ref, got_ref) + vec_ref[1:2, :])
    unit, factor = normalized(mixed)
    out_ref[...] = (unit * vec_ref[4:5, :] + vec_ref[5:6, :]).astype(bf16)
    row = lax.broadcasted_iota(jnp.int32, mixed.shape, 0) + i * mixed.shape[0]
    grad = jnp.where(row < turn_ref[3 * WIDE + 2], cot_ref[...].astype(f32), 0.0)
    d_mixed = norm_back(grad, vec_ref[4:5, :], unit, factor)
    dmix_ref[...] = d_mixed
    low = d_mixed.astype(bf16)
    low_ref[...] = low
    sums_ref[0:1, :] += column_sum(grad * unit)
    sums_ref[1:2, :] += column_sum(grad)
    sums_ref[2:3, :] += column_sum(low.astype(f32))


def second_norm(turns, x1, keep, sent, got, cot, vectors):
    rows = x1.shape[0]
    tiles = norm_tiles(rows)
    block = pl.BlockSpec((rows // tiles, D), lambda i, *_: (i, 0))
    mine = pl.BlockSpec((rows // tiles, D), lambda i, turns: (turns[3 * WIDE + 1] * tiles + i, 0))
    return pl.pallas_call(
        second_norm_kernel,
        grid_spec=pltpu.PrefetchScalarGridSpec(
            num_scalar_prefetch=1,
            grid=(tiles,),
            in_specs=[block] * 4 + [mine, whole_block(vectors.shape)],
            out_specs=[block] * 3 + [whole_block((8, D))],
        ),
        out_shape=[
            jax.ShapeDtypeStruct((rows, D), bf16),
            jax.ShapeDtypeStruct((rows, D), f32),
            jax.ShapeDtypeStruct((rows, D), bf16),
            jax.ShapeDtypeStruct((8, D), f32),
        ],
        compiler_params=params_of(6),
        cost_estimate=cost(40 * rows * D, 20 * rows * D),
        name="norm2",
    )(turns, x1, keep, sent, got, cot, vectors)


def first_back_kernel(
    hid_ref, dmix_ref, keep_ref, sent_ref, got_ref, vec_ref, dhid_ref, low_ref, sums_ref
):
    @pl.when(pl.program_id(0) == 0)
    def _():
        sums_ref[...] = jnp.zeros(sums_ref.shape, f32)

    grad = dmix_ref[...] + summed(keep_ref, sent_ref, got_ref)
    unit, factor = normalized(hid_ref[...])
    d_hidden = norm_back(grad, vec_ref[2:3, :], unit, factor)
    dhid_ref[...] = d_hidden
    low = d_hidden.astype(bf16)
    low_ref[...] = low
    sums_ref[0:1, :] += column_sum(grad * unit)
    sums_ref[1:2, :] += column_sum(grad)
    sums_ref[2:3, :] += column_sum(low.astype(f32))


def first_back(hidden, d_mixed, keep, sent, got, vectors):
    rows = hidden.shape[0]
    tiles = norm_tiles(rows)
    block = pl.BlockSpec((rows // tiles, D), lambda i: (i, 0))
    return pl.pallas_call(
        first_back_kernel,
        grid=(tiles,),
        in_specs=[block] * 5 + [whole_block(vectors.shape)],
        out_specs=[block] * 2 + [whole_block((8, D))],
        out_shape=[
            jax.ShapeDtypeStruct((rows, D), f32),
            jax.ShapeDtypeStruct((rows, D), bf16),
            jax.ShapeDtypeStruct((8, D), f32),
        ],
        compiler_params=params_of(6),
        cost_estimate=cost(40 * rows * D, 20 * rows * D),
        name="back1",
    )(hidden, d_mixed, keep, sent, got, vectors)


def assemble_kernel(turn_ref, near_ref, far_ref, up_ref, down_ref):
    near = near_ref.shape[0]
    for p in range(WIDE):
        start = pl.multiple_of(turn_ref[2 * WIDE + p] * PB, PB)
        for n, target in enumerate((up_ref, down_ref)):
            cut = slice(PB * n, PB * (n + 1))
            target[pl.ds(start, PB), :] = near_ref[p, cut] if p < near else far_ref[p - near, cut]


def assemble(turns, near, far):
    return pl.pallas_call(
        assemble_kernel,
        in_specs=[scalars(), direct(), direct()],
        out_specs=[direct()] * 2,
        out_shape=[jax.ShapeDtypeStruct((D, D), bf16)] * 2,
        compiler_params=params_of(6),
        cost_estimate=cost(0, 8 * D * D),
        name="assemble",
    )(turns, near, far)


def feed_kernel(
    xa_ref, xb_ref, wu_ref, wd_ref, b_ref, x_ref, gate_ref, act_ref, keep_ref, send_ref, sem
):
    i = pl.program_id(0)
    rows = xa_ref.shape[0]

    first = pltpu.make_async_copy(xa_ref, x_ref.at[pl.ds(0, rows)], sem.at[0])
    second = pltpu.make_async_copy(xb_ref, x_ref.at[pl.ds(rows, rows)], sem.at[1])

    @pl.when(i == 0)
    def _():
        first.start()
        second.start()
        first.wait()

    @pl.when(i == 1)
    def _():
        second.wait()

    mine = pl.ds(pl.multiple_of(i * rows, rows), rows)
    gate = dot32(x_ref[mine, :], wu_ref[...]) + b_ref[...]
    gate_ref[...] = gate
    _, tanh = gelu_parts(gate)
    act = (0.5 * gate * (1.0 + tanh)).astype(bf16)
    act_ref[...] = act

    split_store(i, dot32(act, wd_ref[...]).astype(bf16), keep_ref, send_ref)


def feed_forward(piece_a, piece_b, w_up, w_down, up_bias):
    rows = piece_a.shape[0]
    step = pl.BlockSpec((rows, D), lambda i, *_: (i, 0))
    one = whole_block((rows, D))
    return pl.pallas_call(
        feed_kernel,
        grid_spec=pltpu.PrefetchScalarGridSpec(num_scalar_prefetch=0, grid=(2,),
        in_specs=[in_place()] * 2 + [whole_block((D, D))] * 2 + [whole_block(up_bias.shape)],
        out_specs=[whole_block((2 * rows, D)), step, step, one, one],
        scratch_shapes=[pltpu.SemaphoreType.DMA((2,))],
        ),
        out_shape=[
            jax.ShapeDtypeStruct((2 * rows, D), bf16),
            jax.ShapeDtypeStruct((2 * rows, D), f32),
            jax.ShapeDtypeStruct((2 * rows, D), bf16),
            jax.ShapeDtypeStruct((rows, D), bf16),
            jax.ShapeDtypeStruct((rows, D), bf16),
        ],
        compiler_params=params_of(13),
        cost_estimate=cost(8 * rows * D * D, 24 * rows * D),
        name="feed",
    )(piece_a, piece_b, w_up, w_down, up_bias)


def feed_back_kernel(
    da_ref, db_ref, wu_ref, wd_ref, gate_ref, d_ref, dgate_ref, keep_ref, send_ref, sums_ref, sem
):
    i = pl.program_id(0)
    rows = da_ref.shape[0]

    first = pltpu.make_async_copy(da_ref, d_ref.at[pl.ds(0, rows)], sem.at[0])
    second = pltpu.make_async_copy(db_ref, d_ref.at[pl.ds(rows, rows)], sem.at[1])

    @pl.when(i == 0)
    def _():
        first.start()
        second.start()
        sums_ref[...] = jnp.zeros(sums_ref.shape, f32)
        first.wait()

    @pl.when(i == 1)
    def _():
        second.wait()

    mine = pl.ds(pl.multiple_of(i * rows, rows), rows)
    d_act = dot32(d_ref[mine, :], wd_ref[...], ((1,), (1,)))
    gate = gate_ref[...]
    _, tanh = gelu_parts(gate)
    slope = GELU * (1.0 + 3.0 * 0.044715 * gate * gate)
    d_gate = (d_act * (0.5 * (1.0 + tanh) + 0.5 * gate * (1.0 - tanh * tanh) * slope)).astype(bf16)
    dgate_ref[...] = d_gate
    sums_ref[0:1, :] += column_sum(d_gate.astype(f32))

    split_store(i, dot32(d_gate, wu_ref[...], ((1,), (1,))).astype(bf16), keep_ref, send_ref)


def feed_back(piece_a, piece_b, w_up, w_down, gate):
    rows = piece_a.shape[0]
    step = pl.BlockSpec((rows, D), lambda i, *_: (i, 0))
    one = whole_block((rows, D))
    return pl.pallas_call(
        feed_back_kernel,
        grid_spec=pltpu.PrefetchScalarGridSpec(num_scalar_prefetch=0, grid=(2,),
        in_specs=[in_place()] * 2 + [whole_block((D, D))] * 2 + [step],
        out_specs=[whole_block((2 * rows, D)), step, one, one, whole_block((8, D))],
        scratch_shapes=[pltpu.SemaphoreType.DMA((2,))],
        ),
        out_shape=[
            jax.ShapeDtypeStruct((2 * rows, D), bf16),
            jax.ShapeDtypeStruct((2 * rows, D), bf16),
            jax.ShapeDtypeStruct((rows, D), bf16),
            jax.ShapeDtypeStruct((rows, D), bf16),
            jax.ShapeDtypeStruct((8, D), f32),
        ],
        compiler_params=params_of(13),
        cost_estimate=cost(8 * rows * D * D, 24 * rows * D),
        name="fback",
    )(piece_a, piece_b, w_up, w_down, gate)


def group_kernel(turn_ref, left_n, left_f, right_n, right_f, keep_ref, send_ref, all_ref):
    i = pl.program_id(0)
    value = dot32(left_n[...], right_n[...], ((0,), (0,)))
    value = (value + dot32(left_f[...], right_f[...], ((0,), (0,)))).astype(bf16)
    per = value.shape[0] // PB
    for k in range(per):
        all_ref[turn_ref[WIDE + i * per + k]] = value[PB * k : PB * (k + 1)]

    @pl.when(i == pl.num_programs(0) - 1)
    def _():
        near = keep_ref.shape[0]
        keep_ref[...] = all_ref[:near]
        send_ref[...] = all_ref[near:]


def group_grads(turns, left, right, near):
    rows = left[0].shape[0]
    wide = D // 2
    tile = pl.BlockSpec((rows, wide), lambda i, *_: (0, i))
    full = whole_block((rows, D))
    shapes = [(near, PB, D), (WIDE - near, PB, D)]
    return pl.pallas_call(
        group_kernel,
        grid_spec=pltpu.PrefetchScalarGridSpec(
            num_scalar_prefetch=1,
            grid=(2,),
            in_specs=[tile] * 2 + [full] * 2,
            out_specs=[whole_block(shape) for shape in shapes],
            scratch_shapes=[pltpu.VMEM((WIDE, PB, D), bf16)],
        ),
        out_shape=[jax.ShapeDtypeStruct(shape, bf16) for shape in shapes],
        compiler_params=params_of(12),
        cost_estimate=cost(4 * rows * D * D, 12 * rows * D),
    )(turns, *left, *right)


def dx_kernel(dkv_ref, w_ref, *refs, with_q):
    keep_ref, send_ref = refs[-2:]
    i = pl.program_id(0)
    part = dot32(dkv_ref[...], w_ref[...], ((1,), (1,)))
    if with_q:

        part = part + dot32(refs[0][...], refs[1][...], ((1,), (1,)))
    split_store(i, part.astype(bf16), keep_ref, send_ref)


def dx_part(d_kv, w_kv, steps, tokens, d_query, w_q):
    rows = tokens // 4
    count = len(steps)
    with_q = steps[-1] == 0
    half = pl.BlockSpec((rows, D), lambda i: (i // 2, 0))
    shape = jax.ShapeDtypeStruct((count * tokens // 2, D), bf16)
    cols = w_kv.shape[1]

    def chunk_row(i):
        step = steps[-1]
        for n in range(count - 1):
            step = jnp.where(i // 4 == n, steps[n], step)
        return 4 * step + i % 4, 0

    args = [d_kv, w_kv]
    specs = [pl.BlockSpec((rows, cols), chunk_row), whole_block(w_kv.shape)]
    if with_q:
        args += [d_query, w_q]
        specs += [
            pl.BlockSpec((rows, w_q.shape[1]), lambda i: (i % 4, 0)),
            whole_block(w_q.shape),
        ]
    return pl.pallas_call(
        functools.partial(dx_kernel, with_q=with_q),
        grid=(4 * count,),
        in_specs=specs,
        out_specs=[half, half],
        out_shape=[shape, shape],
        compiler_params=params_of(7),
        cost_estimate=cost(2 * count * tokens * cols * D, 2 * count * tokens * (cols + D)),
    )(*args)


def late_kernel(
    turn_ref, x_ref, dkv_ref, dq_ref, att_ref, db_ref, s1_ref, s2_ref, sa_ref, bn_ref, bf_ref, top_ref,
    keep_ref, send_ref, acc_kv, acc_q, acc_o, turn_kv, turn_q, inner_ref, vec_ref, all_ref,
    *, cols, tile, heads, owners
):

    acc_kv[...] = jnp.zeros(acc_kv.shape, f32)

    def step(i, carry):
        mine = pl.ds(pl.multiple_of(i * tile, tile), tile)
        acc_kv[...] += dot32(dkv_ref[mine, :], x_ref[mine, :], ((0,), (0,)))
        return carry

    lax.fori_loop(0, x_ref.shape[0] // tile, step, 0)
    own = slice(0, dq_ref.shape[0])
    acc_q[...] = dot32(dq_ref[...], x_ref[own, :], ((0,), (0,)))
    acc_o[...] = dot32(att_ref[...], db_ref[...], ((0,), (0,)))
    turn_kv[...] = acc_kv[...].T.astype(bf16)
    turn_q[...] = acc_q[...].T.astype(bf16)
    pad = acc_o.shape[0] - cols
    for k in range(D // PB):
        for c in range(3):
            unit = 3 * k + c
            rows = slice(PB * k, PB * (k + 1))
            piece = turn_q[rows, :cols] if c == 0 else turn_kv[rows, cols * (c - 1) : cols * c]
            all_ref[
                turn_ref[WIDE + unit // 4], :PB, cols * (unit % 4) : cols * (unit % 4 + 1)
            ] = piece
    for k in range(cols // PB):
        all_ref[turn_ref[WIDE + 3 * cols // PB + k], :PB, :] = acc_o[
            pad + PB * k : pad + PB * (k + 1), :
        ].astype(bf16)
    inner_ref[0:1, :cols] = sa_ref[0:1, :cols]
    inner_ref[0:1, cols : 2 * cols] = sa_ref[1:2, pad : pad + cols]
    inner_ref[0:1, 2 * cols :] = bn_ref[0:1, :] + bf_ref[0:1, :]
    outer_cols = D // owners
    inner_cols = inner_ref.shape[1] // owners
    lane = lax.broadcasted_iota(jnp.int32, (1, D), 1)
    slots = jnp.zeros((1, D), f32)
    base = turn_ref[3 * WIDE] * 3 * heads
    for h in range(heads):
        left = top_ref[h : h + 1, :1]
        for part in range(3):
            piece = left.astype(bf16).astype(f32)
            slots = jnp.where(lane == base + part * heads + h, piece, slots)
            left = left - piece
    vec_ref[...] = jnp.zeros(vec_ref.shape, f32)
    vec_ref[7:8, :] = slots
    outer_rows = [(s1_ref, 2), (s2_ref, 2), (s1_ref, 0), (s1_ref, 1), (s2_ref, 0), (s2_ref, 1)]
    for k in range(owners):
        for n, (ref, row) in enumerate(outer_rows):
            vec_ref[n : n + 1, :outer_cols] = ref[
                row : row + 1, outer_cols * k : outer_cols * (k + 1)
            ]
        vec_ref[6:7, :inner_cols] = inner_ref[0:1, inner_cols * k : inner_cols * (k + 1)]
        all_ref[turn_ref[WIDE + k], PB:, :] = vec_ref[...].astype(bf16)
    near = keep_ref.shape[0]
    keep_ref[...] = all_ref[:near]
    send_ref[...] = all_ref[near:]


def late_grads(turns, in_all, d_kv, d_query, att, d_branch, s1, s2, sa, bn, bf, tops, cols, heads, near):
    _, wide = d_query.shape
    tile = 1024
    owners = WIDE
    under = 16

    small = [s1, s2, sa, bn, bf, tops]
    return pl.pallas_call(
        functools.partial(late_kernel, cols=cols, tile=tile, heads=heads, owners=owners),
        in_specs=[scalars()] + [direct()] * (5 + len(small)),
        out_specs=[direct()] * 2,
        scratch_shapes=[
            pltpu.VMEM((2 * cols, D), f32),
            pltpu.VMEM((wide, D), f32),
            pltpu.VMEM((wide, D), f32),
            pltpu.VMEM((D, 2 * cols), bf16),
            pltpu.VMEM((D, wide), bf16),
            pltpu.VMEM((1, 2 * cols + D), f32),
            pltpu.VMEM((under, D), f32),
            pltpu.VMEM((owners, PB + under, D), bf16),
        ],
        out_shape=[
            jax.ShapeDtypeStruct((near, PB + under, D), bf16),
            jax.ShapeDtypeStruct((owners - near, PB + under, D), bf16),
        ],
        compiler_params=params_of(20),
        cost_estimate=cost(2 * in_all.shape[0] * D * 2 * cols, 2 * in_all.shape[0] * (D + 2 * cols)),
        name="late",
    )(turns, in_all, d_kv, d_query, att, d_branch, *small)


def head_masks(wide, heads, first):
    lane = lax.broadcasted_iota(jnp.int32, (BLOCK, wide), 1) // HEAD
    return [lane == h + first for h in range(heads)]


def spread(block, masks):
    zero = jnp.zeros_like(block)
    return jnp.concatenate([jnp.where(mask, block, zero) for mask in masks], axis=0)


def fold(stacked, masks):
    total = None
    for h, mask in enumerate(masks):
        part = jnp.where(mask, stacked[BLOCK * h : BLOCK * (h + 1)], 0.0)
        total = part if total is None else total + part
    return total


def listed_rows(addr_ref, kv_ref, i):
    return jnp.concatenate(
        [
            kv_ref[pl.ds(pl.multiple_of(addr_ref[i * LIST + e] * BLOCK, BLOCK), BLOCK), :]
            for e in range(LIST)
        ],
        axis=0,
    )


def fwd_kernel(
    addr_ref, valid_ref, query_ref, q_ref, kv_ref, att_ref, p_ref, top_ref, *, heads, group
):
    wide = q_ref.shape[1]
    start = kv_ref.shape[1] - wide
    top_ref[...] = jnp.full(top_ref.shape, neg_large, f32)
    scale = jnp.asarray(HEAD ** (-0.5), bf16)
    q_masks = head_masks(wide, heads, 0)
    v_masks = head_masks(wide, heads, (heads * HEAD - start) // HEAD)
    lane = lax.broadcasted_iota(jnp.int32, (1, LIST * BLOCK), 1)

    def step(i, carry):
        for u in range(group):
            block = i * group + u
            mine = pl.ds(pl.multiple_of(block * BLOCK, BLOCK), BLOCK)
            q_all = spread(q_ref[mine, :] * scale, q_masks)
            listed = listed_rows(addr_ref, kv_ref, block)
            scores = dot32(q_all, listed[:, :wide], ((1,), (1,)))
            limit = jnp.zeros((1, LIST * BLOCK), jnp.int32)
            for e in range(LIST):
                limit = jnp.where(lane // BLOCK == e, valid_ref[block * LIST + e], limit)
            scores = jnp.where(lane % BLOCK < limit, scores, neg_large)
            row_top = jnp.max(scores, axis=1, keepdims=True)
            shifted = jnp.exp(scores - row_top)
            probs = shifted * (1.0 / jnp.sum(shifted, axis=1, keepdims=True))
            probs_low = probs.astype(bf16)
            p_ref[block] = probs_low
            out = dot32(probs_low, listed[:, start:])
            att_ref[mine, :] = fold(out, v_masks).astype(bf16)
            row = lax.broadcasted_iota(jnp.int32, row_top.shape, 0) % BLOCK
            seen = jnp.where(row < query_ref[block], row_top, neg_large)
            for h in range(heads):
                best = jnp.max(seen[BLOCK * h : BLOCK * (h + 1)], axis=0, keepdims=True)
                top_ref[h : h + 1, :] = jnp.maximum(top_ref[h : h + 1, :], best)
        return carry

    lax.fori_loop(0, q_ref.shape[0] // (group * BLOCK), step, 0)


def attention_forward(queries, kv_all, addr, valid, query_valid, heads, group=2):
    tokens, wide = queries.shape
    blocks = tokens // BLOCK
    rows = heads * BLOCK
    cols = LIST * BLOCK
    return pl.pallas_call(
        functools.partial(fwd_kernel, heads=heads, group=group),
        in_specs=[scalars()] * 3 + [direct()] * 2,
        out_specs=[direct()] * 3,
        out_shape=(
            jax.ShapeDtypeStruct((tokens, wide), bf16),
            jax.ShapeDtypeStruct((blocks, rows, cols), bf16),
            jax.ShapeDtypeStruct((8, 128), f32),
        ),
        compiler_params=params_of(11),
        cost_estimate=cost(
            4 * blocks * rows * cols * wide,
            2 * (kv_all.size + 2 * queries.size + blocks * rows * cols),
            blocks * rows * cols,
        ),
        name="afwd",
    )(addr, valid, query_valid, queries, kv_all)


def bwd_kernel(addr_ref, q_ref, p_ref, w_ref, kv_ref, *refs, heads, group):
    pieces = refs[:4]
    dq_ref, dkv_ref, sums_ref, db_ref, acc_ref = refs[4:]
    wide = q_ref.shape[1]
    start = kv_ref.shape[1] - wide
    rows = pieces[0].shape[0]
    for r, piece in enumerate(pieces):
        db_ref[r * rows : (r + 1) * rows, :] = piece[...]
    acc_ref[...] = jnp.zeros(acc_ref.shape, f32)
    sums_ref[...] = jnp.zeros(sums_ref.shape, f32)
    scale = jnp.asarray(HEAD ** (-0.5), bf16)
    q_masks = head_masks(wide, heads, 0)
    v_masks = head_masks(wide, heads, (heads * HEAD - start) // HEAD)

    def step(i, carry):
        span = group * BLOCK
        d_branch = db_ref[pl.ds(pl.multiple_of(i * span, span), span), :]
        d_out = dot32(d_branch, w_ref[...], ((1,), (1,))).astype(bf16)
        for u in range(group):
            block = i * group + u
            here = slice(u * BLOCK, (u + 1) * BLOCK)
            mine = pl.ds(pl.multiple_of(block * BLOCK, BLOCK), BLOCK)
            q_all = spread(q_ref[mine, :] * scale, q_masks)
            do_all = spread(d_out[here], v_masks)
            listed = listed_rows(addr_ref, kv_ref, block)
            probs_low = p_ref[block]
            probs = probs_low.astype(f32)
            d_probs = dot32(do_all, listed[:, start:], ((1,), (1,)))
            delta = jnp.sum(probs * d_probs, axis=1, keepdims=True)
            d_scores = (probs * (d_probs - delta)).astype(bf16)
            d_query = (fold(dot32(d_scores, listed[:, :wide]), q_masks) * HEAD ** (-0.5)).astype(bf16)
            dq_ref[mine, :] = d_query
            sums_ref[0:1, :] += column_sum(d_query.astype(f32))
            d_key = dot32(d_scores, q_all, ((0,), (0,)))
            d_value = dot32(probs_low, do_all, ((0,), (0,)))
            sums_ref[1:2, :] += column_sum(d_value)
            for e in range(LIST):
                rows = pl.ds(pl.multiple_of(addr_ref[block * LIST + e] * BLOCK, BLOCK), BLOCK)
                part = slice(BLOCK * e, BLOCK * (e + 1))
                acc_ref[rows, :start] += d_key[part, :start]
                acc_ref[rows, start:wide] += d_key[part, start:] + d_value[part, : wide - start]
                acc_ref[rows, wide:] += d_value[part, wide - start :]
        return carry

    lax.fori_loop(0, q_ref.shape[0] // (group * BLOCK), step, 0)
    dkv_ref[...] = acc_ref[...].astype(bf16)


def attention_backward(queries, pieces, w_out, probs, kv_all, addr, heads, group=2):
    tokens, wide = queries.shape
    blocks = tokens // BLOCK
    rows = heads * BLOCK
    cols = LIST * BLOCK
    return pl.pallas_call(
        functools.partial(bwd_kernel, heads=heads, group=group),
        in_specs=[scalars()] + [direct()] * 8,
        out_specs=[direct()] * 4,
        scratch_shapes=[pltpu.VMEM(kv_all.shape, f32)],
        out_shape=(
            jax.ShapeDtypeStruct((tokens, wide), bf16),
            jax.ShapeDtypeStruct(kv_all.shape, bf16),
            jax.ShapeDtypeStruct((8, wide), f32),
            jax.ShapeDtypeStruct((tokens, D), bf16),
        ),
        compiler_params=params_of(24),
        cost_estimate=cost(
            8 * blocks * rows * cols * wide,
            2 * (2 * kv_all.size + 3 * queries.size + blocks * rows * cols),
        ),
        name="abwd",
    )(addr, queries, probs, w_out, kv_all, *pieces)


def two_parts(values):
    high = values.astype(bf16)
    return high, (values - high.astype(f32)).astype(bf16)


def shampoo_kernel(turn_ref, *refs, width, groups, heads):
    g_refs = refs[: 3 if groups else 1]
    max_ref, mb_ref, ls_ref, rs_ref, lr_ref, rr_ref = refs[len(g_refs) : len(g_refs) + 6]
    bg_ref, ln_ref, rn_ref, nb_ref, g_ref = refs[len(g_refs) + 6 :]
    i = pl.program_id(0)
    if groups:
        for n in range(3):

            @pl.when(i == n)
            def _():
                g_ref[...] = g_refs[n][...]
    else:
        g_ref[...] = g_refs[0][...]
    scales = [
        jnp.sqrt(tau_clip / jnp.maximum(max_ref[0:1, h : h + 1], tau_clip)) for h in range(heads)
    ]
    per_row = 3 * heads * HEAD // PB
    column = lax.broadcasted_iota(jnp.int32, (1, PB), 1)
    for j in range(width):
        cut = slice(PB * j, PB * (j + 1))
        grad = g_ref[:, cut]
        bg_ref[j] = grad.astype(f32)
        ln_ref[j] = 0.5 * ls_ref[j] + 0.5 * dot32(grad, grad, ((1,), (1,)))
        rn_ref[j] = 0.5 * rs_ref[j] + 0.5 * dot32(grad, grad, ((0,), (0,)))
        left_hi, left_lo = two_parts(lr_ref[j])
        applied_hi, applied_lo = two_parts(dot32(left_hi, grad) + dot32(left_lo, grad))
        right_hi, right_lo = two_parts(rr_ref[j])
        step_val = (
            dot32(applied_hi, right_hi) + dot32(applied_hi, right_lo) + dot32(applied_lo, right_hi)
        )
        index = (turn_ref[3 * WIDE] * pl.num_programs(0) + i) * width + j
        head_of = (lax.rem(index, per_row) * PB + column) // HEAD
        factor = jnp.ones((1, PB), f32)
        for h in range(heads):
            hit = (head_of == h) | (head_of == heads + h)
            factor = jnp.where(hit & (index < D // PB * per_row), scales[h], factor)
        nb_ref[j] = (mb_ref[j] - rate_matrix * step_val) * factor


def shampoo(turns, grads, groups, largest, master, left_s, right_s, left_r, right_r, heads):
    count = master.shape[0]
    width = WIDE if groups else 1
    block = pl.BlockSpec((width, PB, PB), lambda i, *_: (i, 0, 0))
    shape = jax.ShapeDtypeStruct((count, PB, PB), f32)
    if groups:
        specs = [whole_block(part.shape) for part in grads]
    else:
        specs = [pl.BlockSpec((PB, PB), lambda i, *_: (i, 0))]
    return pl.pallas_call(
        functools.partial(shampoo_kernel, width=width, groups=groups, heads=heads),
        grid_spec=pltpu.PrefetchScalarGridSpec(
            num_scalar_prefetch=1,
            grid=(count // width,),
            in_specs=specs + [whole_block(largest.shape)] + [block] * 5,
            out_specs=[block] * 4,
            scratch_shapes=[pltpu.VMEM((PB, PB * width), bf16)],
        ),
        out_shape=[shape] * 4,
        compiler_params=params_of(16),
        cost_estimate=cost(16 * count * PB**3, 40 * count * PB * PB),
        name="shampoo",
    )(turns, *grads, largest, master, left_s, right_s, left_r, right_r)


def gather_quarters(own):
    side = swap(own, 1)
    across = swap(own, 2)
    return own, side, across, swap(across, 1)


def cross_sum(keep_far, send_far):
    mine = keep_far.astype(f32) + swap(send_far, 1).astype(f32)
    return swap(mine.astype(bf16), 2)


def slot_pairs(slot):
    return [(d, (3 * d + slot) % WIDE) for d in range(WIDE)]


def spread_group(held, group):
    count = lax.axis_size(CTX)
    pieces = [held] + [None] * (count - 1)
    for step in near_first(count):
        if count == 4 and step == 2 and group:
            pieces[2] = forward_two(pieces[1], pieces[3])
        else:
            pieces[step] = shift_ctx(held, step)
    near = jnp.stack(pieces, axis=0)
    far = [shift_shard(near, u) for u in range(1, lax.axis_size(SHARD))]
    return near, far[0] if len(far) == 1 else jnp.concatenate(far, axis=0)


def reduce_group(near, far, label):
    count = lax.axis_size(CTX)
    back = [
        shift_shard(far[count * (u - 1) : count * u], u)
        for u in range(1, lax.axis_size(SHARD))
    ]
    halves = []
    for step in range(count):
        value = near[step].astype(f32)
        for part in back:
            value = value + part[step].astype(f32)
        halves.append(value)
    steps = near_first(count)
    if count == 4 and label == "0":
        right, left = back_two(halves[2].astype(bf16))
        halves[1] = halves[1] + right.astype(f32)
        halves[3] = halves[3] + left.astype(f32)
        steps = [1, 3]
    return [halves[0]] + [shift_ctx(halves[step].astype(bf16), step) for step in steps]


def per_device(
    inputs,
    lengths,
    global_blocks,
    random_blocks,
    master_blocks,
    outer_vectors,
    inner_biases,
    left_stats,
    right_stats,
    left_roots,
    right_roots,
    cotangent,
):
    tensor_count = lax.axis_size(TP)
    owner_count = lax.axis_size(OWN)
    ctx_count = lax.axis_size(CTX)
    shard_count = lax.axis_size(SHARD)
    heads_here = HEADS // tensor_count
    cols = heads_here * HEAD
    wide = 256
    pad = wide - cols
    tokens = inputs.shape[1]
    quarter = tokens // 4
    rows_blocks = tokens // BLOCK
    blocks_here = master_blocks.shape[0]
    packed = owner_count == WIDE and blocks_here == 3 * WIDE
    me = lax.axis_index(TP)
    z = lax.axis_index(CTX)
    y = lax.axis_index(SHARD)
    owner = lax.axis_index(OWN)
    ids = jnp.stack([me, y, z, owner]).astype(jnp.int32)
    addr, valid, query_valid, turns = index_tables(
        ids,
        lengths,
        global_blocks,
        random_blocks.reshape(rows_blocks, 3),
        rows_blocks,
        ctx_count,
        shard_count,
    )
    inner_row = inner_biases[0:1]
    q_bias = jnp.pad(inner_row[:, :cols], ((0, 0), (0, pad)))
    kv_bias = jnp.pad(inner_row[:, cols : 2 * cols], ((0, 0), (cols, 0)))
    up_bias = inner_row[:, 2 * cols :]
    flat_in = inputs.reshape(tokens, D)
    own_in = pick_quarter(ids, flat_in)

    if packed:
        own_packed = pack_rows(master_blocks)
        held = [
            owner_move(own_packed[PB * slot : PB * (slot + 1)], slot_pairs(slot))
            for slot in range(3)
        ]
        held_first, held_rest = sort_held(turns, held)
        first_near, first_far = spread_group(held_first, 0)
        rest_near, rest_far = spread_group(held_rest, 1)
    else:
        weights = pack_rows(lax.all_gather(master_blocks.astype(bf16), OWN, axis=0, tiled=True))
        weights = weights.reshape(3, WIDE, PB, D)
        first_near, first_far = weights[0, : WIDE // 2], weights[0, WIDE // 2 :]
        rest = jnp.concatenate([weights[1], weights[2]], axis=1)
        rest_near, rest_far = rest[: WIDE // 2], rest[WIDE // 2 :]
        order = jnp.arange(WIDE, dtype=jnp.int32)
        turns = jnp.concatenate([order, order, order, turns[3 * WIDE :]])
    w_q, w_kv, w_out = unpack_first(turns, first_near, first_far, cols, wide)

    in_all, kv_all, queries = project_chunk(
        ids, [flat_in], 0, ctx_count, w_kv, kv_bias, w_q, q_bias, None
    )
    moved = []
    for n, step in enumerate(near_first(ctx_count)):
        if ctx_count == 4 and n == 2:
            moved.append(forward_two(moved[0], moved[1]))
        else:
            source = own_in if n < 2 else after(own_in, moved[n - 2])
            moved.append(shift_ctx(source, step))
        pieces = gather_quarters(moved[n])
        in_all, kv_all = project_chunk(
            ids, pieces, step, ctx_count, w_kv, kv_bias, None, None, (in_all, kv_all)
        )

    att, probs, tops = attention_forward(queries, kv_all, addr, valid, query_valid, heads_here)
    keep, send = out_project(att, w_out)
    sent = swap(send, 1)
    got = swap((keep[quarter:].astype(f32) + sent[quarter:].astype(f32)).astype(bf16), 2)
    w_up, w_down = assemble(turns, rest_near, rest_far)
    hidden, x_first, x_own = first_norm(ids, flat_in, keep, sent, got, outer_vectors)
    x_own, x_side, x_across, x_diag = gather_quarters(x_own)
    x_n, gate_n, act_n, keep_n, send_n = feed_forward(x_own, x_side, w_up, w_down, up_bias)
    x_f, gate_f, act_f, keep_f, send_f = feed_forward(
        x_across, x_diag, w_up, w_down, up_bias
    )
    out_own, d_mixed, d_own, sums2 = second_norm(
        turns,
        x_first,
        keep_n,
        swap(send_n, 1),
        cross_sum(keep_f, send_f),
        cotangent.reshape(tokens, D),
        outer_vectors,
    )

    near = ctx_count if packed else WIDE // 2
    d_own, d_side, d_across, d_diag = gather_quarters(d_own)
    d_n, dg_n, keep_n, send_n, up_n = feed_back(d_own, d_side, w_up, w_down, gate_n)
    d_f, dg_f, keep_f, send_f, up_f = feed_back(d_across, d_diag, w_up, w_down, gate_f)
    d_hidden, b_own, sums1 = first_back(
        hidden, d_mixed, keep_n, swap(send_n, 1), cross_sum(keep_f, send_f), outer_vectors
    )
    b_pieces = gather_quarters(b_own)
    g_down = group_grads(turns, (act_n, act_f), (d_n, d_f), near)
    g_up = group_grads(turns, (x_n, x_f), (dg_n, dg_f), near)
    if packed:
        down_own = reduce_group(*g_down, "2")
        up_own = reduce_group(*g_up, "1")
    out_quarters = gather_quarters(after(out_own, b_pieces[3]))
    d_query, d_kv, sums_a, d_branch = attention_backward(
        queries, b_pieces, w_out, probs, kv_all, addr, heads_here
    )

    total = d_hidden
    d_kv_late = d_kv
    extra = {}
    for step in near_first(ctx_count)[::-1] + [0]:
        keep, send = dx_part(d_kv, w_kv, [step], tokens, d_query, w_q)
        sent = swap(send, 1)
        across = (keep[quarter:].astype(f32) + sent[quarter:].astype(f32)).astype(bf16)
        across = swap(across, 2)
        mine = keep[:quarter].astype(f32) + sent[:quarter].astype(f32) + across.astype(f32)
        if step in extra:
            mine = mine + extra[step].astype(f32)
        if step == 2 and ctx_count == 4:
            extra[3], extra[1] = back_two(mine.astype(bf16))
            continue
        if step:
            mine = shift_ctx(mine.astype(bf16), ctx_count - step).astype(f32)
        total = total + mine
    grad_quarters = gather_quarters(total.astype(bf16))

    near_rows, far_rows = late_grads(
        turns,
        in_all,
        d_kv_late,
        d_query,
        att,
        d_branch,
        sums1,
        sums2,
        sums_a,
        up_n,
        up_f,
        tops,
        cols,
        heads_here,
        near,
    )
    outer_cols = D // owner_count
    inner_cols = inner_biases.shape[1] // owner_count
    if packed:
        *dealt, tail, largest = deal_rows(
            turns, reduce_group(near_rows, far_rows, "0"), up_own, down_own, heads_here
        )
        outer_own = tail[:6, :outer_cols]
        inner_own = tail[6:7, :inner_cols]
        grads = [
            owner_move(dealt[slot], [(holder, d) for d, holder in slot_pairs(slot)])
            for slot in range(3)
        ]
        groups = 3
    else:
        rows_of = jnp.concatenate([near_rows, far_rows], axis=0)[:, :PB]
        whole = jnp.concatenate([rows_of, *g_up, *g_down], axis=0).reshape(-1, D)
        blocks = whole.reshape(-1, PB, WIDE, PB).transpose(0, 2, 1, 3).reshape(-1, PB, PB)
        own_grads = lax.psum_scatter(blocks, OWN, scatter_dimension=0, tiled=True)
        grads, groups = [own_grads.reshape(blocks_here * PB, PB)], 0
        outer_part = jnp.stack([sums1[2], sums2[2], sums1[0], sums1[1], sums2[0], sums2[1]], axis=0)
        inner_part = jnp.concatenate([sums_a[0, :cols], sums_a[1, pad:], up_n[0] + up_f[0]])
        outer_own = lax.psum_scatter(outer_part, OWN, scatter_dimension=1, tiled=True)
        inner_own = lax.psum_scatter(inner_part[None, :], OWN, scatter_dimension=1, tiled=True)
        largest = lax.pmax(tops[:heads_here, 0], OWN)
        largest = jnp.zeros((8, 128), f32).at[0, :heads_here].set(largest)
    outer_own = outer_own + swap(outer_own, 1)
    outer_own = outer_own + swap(outer_own, 2)

    block_sum, left_new, right_new, new_blocks = shampoo(
        turns,
        grads,
        groups,
        largest,
        master_blocks,
        left_stats,
        right_stats,
        left_roots,
        right_roots,
        heads_here,
    )
    maxima = largest[0, :heads_here]
    own_outer = lax.dynamic_slice_in_dim(outer_vectors, owner * outer_cols, outer_cols, 1)
    new_outer = own_outer - rate_vector * outer_own
    own_inner = lax.dynamic_slice_in_dim(inner_biases, owner * inner_cols, inner_cols, 1)
    head_of = (owner * inner_cols + jnp.arange(inner_cols, dtype=jnp.int32)) // HEAD
    factor = jnp.ones((inner_cols,), f32)
    for h in range(heads_here):
        scale = jnp.sqrt(tau_clip / jnp.maximum(largest[0, h], tau_clip))
        factor = jnp.where(head_of == h, scale, factor)
    new_inner = (own_inner - rate_vector * inner_own) * factor[None, :]

    return (
        place_quarters(ids, out_quarters).reshape(inputs.shape),
        place_quarters(ids, grad_quarters).reshape(inputs.shape),
        block_sum,
        outer_own,
        inner_own,
        maxima,
        left_new,
        right_new,
        new_blocks,
        new_outer,
        new_inner,
    )


def solution(mesh):
    return jax.shard_map(
        per_device,
        mesh=mesh,
        in_specs=(
            P(SHARD, CTX, None),
            P(SHARD),
            P(SHARD, None),
            P(SHARD, CTX, None),
            P((SHARD, CTX, TP), None, None),
            P(),
            P(TP, None),
            P((SHARD, CTX, TP), None, None),
            P((SHARD, CTX, TP), None, None),
            P((SHARD, CTX, TP), None, None),
            P((SHARD, CTX, TP), None, None),
            P(SHARD, CTX, None),
        ),
        out_specs=(
            P(SHARD, CTX, None),
            P(SHARD, CTX, None),
            P((SHARD, CTX, TP), None, None),
            P(None, (SHARD, CTX)),
            P(TP, (SHARD, CTX)),
            P(TP),
            P((SHARD, CTX, TP), None, None),
            P((SHARD, CTX, TP), None, None),
            P((SHARD, CTX, TP), None, None),
            P(None, (SHARD, CTX)),
            P(TP, (SHARD, CTX)),
        ),
        check_vma=False,
    )
```
